32 devices in a mesh: expert: 8 (over z, x), dp: 4 (over y, core).
Axes of the slice: x: 2, y: 2, z: 4, core: 2. Of those that a mesh axis runs over, the one named last changes fastest.
Arguments:
- enc_state: bfloat16 [4, 8, 256, 1024], P('dp', 'expert'), may hold values from -6 to 6
- baseline: bfloat16 [4, 8, 256, 1024], P('dp', 'expert'), may hold values from -6 to 6
- enc_keys: bfloat16 [4, 8, 256, 1024], P('dp', 'expert'), may hold values from -4 to 4
- dec_queries: bfloat16 [4, 8, 128, 1024], P('dp', 'expert'), may hold values from -200 to 200
- out_mult: bfloat16 [4, 8, 128, 1024], P('dp', 'expert'), may hold values from -6 to 6
- doc_lengths: int32 [4, 8], P('dp', 'expert'), may hold values from 128 to 256, as said below
- expert_ids: int32 [4, 8, 256], P('dp', 'expert'), may hold values from 0 to 15
- slot_ids: int32 [4, 8, 256], P('dp', 'expert'), may hold values from 0 to 31, as said below
- gate_prob: float32 [4, 8, 256], P('dp', 'expert'), may hold values from 0.2 to 1
- norm_gain: float32 [1024], replicated, may hold values from 0.5 to 2
- w_in: bfloat16 [16, 1024, 2816], P('expert', None, 'dp'), may hold values from -0.1875 to 0.1875
- w_out_t: bfloat16 [16, 1024, 2816], P('expert', None, 'dp'), may hold values from -0.109375 to 0.109375
- w_value: bfloat16 [1024, 1024], replicated, may hold values from -0.1875 to 0.1875
Outputs:
- enc_mult: bfloat16 [4, 8, 256, 1024], P('dp', 'expert')
The draws below stay inside these ranges and needn't reach their ends.
Inputs may be any that keep to these rules, and one draw needn't show every extreme that they name: `slot_ids`: within one document no two tokens share an expert and a slot, and every token has a slot; one expert has all 32 slots used in every document. `doc_lengths`: some document has all 256 tokens.
All inputs are finite; a program needn't handle non-finite values.
Results may differ from the reference program's by a relative error of at most 0.0069.
Values may be sent and summed in bfloat16 or wider, within the bound.
A program may use at most 128 MiB of HBM per device.

```python
import math
import jax
import jax.numpy as jnp
from jax import lax

D = 1024
FF = 2816
HEADS = 16
HEAD_DIM = 64
ENC_LEN = 256
DEC_LEN = 128
EXPERTS = 16
CAP = 32
GROUPS = 4
DOC_GRP = 8


def routing_draw(key):
    levels = jax.random.randint(jax.random.fold_in(key, 101), (EXPERTS,), 0, 4)
    busiest = jax.random.randint(jax.random.fold_in(key, 102), (), 0, EXPERTS)
    levels = jnp.where(jnp.arange(EXPERTS) == busiest, 9, levels)
    jitter = jax.random.randint(jax.random.fold_in(key, 103), (GROUPS, DOC_GRP, EXPERTS, CAP), 0, 3072)
    scores = (levels[:, None] * 1024 + jitter).reshape(GROUPS, DOC_GRP, EXPERTS * CAP)
    ranked = jnp.argsort(-scores, axis=-1, stable=True)[:, :, :ENC_LEN]
    shuffle_keys = jax.random.randint(jax.random.fold_in(key, 104), (GROUPS, DOC_GRP, ENC_LEN), 0, 2 ** 30)
    shuffle = jnp.argsort(shuffle_keys, axis=-1, stable=True)
    chosen = jnp.take_along_axis(ranked, shuffle, axis=-1)
    return ((chosen // CAP).astype(jnp.int32), (chosen % CAP).astype(jnp.int32))


def attention_draw(key):
    keys = jnp.clip(jax.random.normal(jax.random.fold_in(key, 201), (GROUPS, DOC_GRP, ENC_LEN, D), jnp.float32), -4.0, 4.0)
    queries = 0.5 * jnp.clip(jax.random.normal(jax.random.fold_in(key, 202), (GROUPS, DOC_GRP, DEC_LEN, D), jnp.float32), -6.0, 6.0)
    return (keys, queries)


def draw_enc_keys(key, part):
    return attention_draw(key)[0].astype(jnp.bfloat16)


def draw_dec_queries(key, part):
    return attention_draw(key)[1].astype(jnp.bfloat16)


def draw_doc_lengths(key, part):
    doc_len = jax.random.randint(jax.random.fold_in(key, 301), (GROUPS, DOC_GRP), ENC_LEN // 2, ENC_LEN + 1)
    full_doc = jax.random.randint(jax.random.fold_in(key, 302), (), 0, GROUPS * DOC_GRP)
    doc_index = jnp.arange(GROUPS * DOC_GRP).reshape(GROUPS, DOC_GRP)
    return jnp.where(doc_index == full_doc, ENC_LEN, doc_len).astype(jnp.int32)


def draw_expert_ids(key, part):
    return routing_draw(key)[0]


def draw_slot_ids(key, part):
    return routing_draw(key)[1]


def block_scale(stream_key, dims, shards, least, top_value):
    loudness, own = 1.0, jax.random.fold_in(stream_key, 6)
    for axis_at, shards_of in shards:
        heights = jnp.exp(jax.random.uniform(jax.random.fold_in(own, axis_at), (shards_of,), jnp.float32, least / len(shards), top_value / len(shards)))
        loudness = loudness * jnp.repeat(heights, dims[axis_at] // shards_of).reshape([-1 if axis == axis_at else 1 for axis in range(len(dims))])
    return loudness


def normal_values(own_key, shape, deviation, reach, cuts=(), held_as=jnp.bfloat16):
    factor_of = block_scale(own_key, shape, cuts, -0.22, 0.18) if cuts else 1.0
    values = jax.random.normal(own_key, shape, jnp.float32) * deviation * factor_of
    return jnp.minimum(jnp.maximum(values, -reach), reach).astype(held_as)


def setup_inputs(seed: int = 0) -> dict:
    streams_of = jax.random.split(jax.random.key(seed), 14)
    return {
        "enc_state": normal_values(streams_of[0], (GROUPS, DOC_GRP, ENC_LEN, D), 1.0, 6.0, ((0, 4), (1, 8))),
        "baseline": normal_values(streams_of[1], (GROUPS, DOC_GRP, ENC_LEN, D), 1.0, 6.0, ((0, 4), (1, 8))),
        "enc_keys": draw_enc_keys(jax.random.fold_in(streams_of[13], 71), 0),
        "dec_queries": draw_dec_queries(jax.random.fold_in(streams_of[13], 71), 0),
        "out_mult": normal_values(streams_of[4], (GROUPS, DOC_GRP, DEC_LEN, D), 1.0, 6.0, ((0, 4), (1, 8))),
        "doc_lengths": draw_doc_lengths(jax.random.fold_in(streams_of[13], 71), 0),
        "expert_ids": draw_expert_ids(jax.random.fold_in(streams_of[13], 71), 0),
        "slot_ids": draw_slot_ids(jax.random.fold_in(streams_of[13], 71), 0),
        "gate_prob": jnp.clip(jnp.exp(math.log(1.0) - 1.609438 * jax.random.uniform(streams_of[8], (GROUPS, DOC_GRP, ENC_LEN), jnp.float32) ** block_scale(streams_of[8], (GROUPS, DOC_GRP, ENC_LEN), ((0, 4), (1, 8)), -0.2, 0.2)), 0.2, 1.0),
        "norm_gain": jnp.clip(jnp.exp(jax.random.uniform(streams_of[9], (D,), jnp.float32, math.log(0.5), math.log(2.0))), 0.5, 2.0),
        "w_in": normal_values(streams_of[10], (EXPERTS, D, FF), D ** -0.5, 0.1875, ((0, 8), (2, 4))),
        "w_out_t": normal_values(streams_of[11], (EXPERTS, D, FF), FF ** -0.5, 0.109375, ((0, 8), (2, 4))),
        "w_value": normal_values(streams_of[12], (D, D), D ** -0.5, 0.1875),
    }


def rescale(pre_act, base_act):
    upper_part = jnp.maximum(jnp.maximum(pre_act, base_act), 0.0)
    lower_part = jnp.maximum(-jnp.minimum(pre_act, base_act), 0.0)
    return upper_part / (upper_part + lower_part + jnp.where(upper_part > 0.0, 0.0, 1.0))

def attend(query_rows, key_rows, mult_rows, length, w_value):
    enc_len = key_rows.shape[0]
    dec_len = query_rows.shape[0]
    queries = query_rows.astype(jnp.float32).reshape(dec_len, HEADS, HEAD_DIM)
    keys = key_rows.astype(jnp.float32).reshape(enc_len, HEADS, HEAD_DIM)
    mults = mult_rows.astype(jnp.float32).reshape(dec_len, HEADS, HEAD_DIM)
    scores = jnp.einsum('qhd,khd->hqk', queries, keys) * (1.0 / math.sqrt(HEAD_DIM))
    valid = jnp.arange(enc_len, dtype=jnp.int32) < length
    scores = jnp.where(valid[None, None, :], scores, -jnp.inf)
    top_score = lax.optimization_barrier(jnp.max(scores, axis=-1, keepdims=True))
    expo = jnp.exp(scores - top_score)
    attn = (expo / lax.optimization_barrier(jnp.sum(expo, axis=-1, keepdims=True))).astype(jnp.bfloat16)
    value_mult = jnp.einsum('hqk,qhd->khd', attn.astype(jnp.float32), mults).astype(jnp.bfloat16)
    return jnp.dot(value_mult.reshape(enc_len, HEADS * HEAD_DIM), w_value.T, preferred_element_type=jnp.float32)

def reference(enc_state, baseline, enc_keys, dec_queries, out_mult, doc_lengths, expert_ids, slot_ids, gate_prob, norm_gain, w_in, w_out_t, w_value):
    n_docs = GROUPS * DOC_GRP
    flat_queries = dec_queries.reshape(n_docs, DEC_LEN, D)
    flat_keys = enc_keys.reshape(n_docs, ENC_LEN, D)
    flat_mults = out_mult.reshape(n_docs, DEC_LEN, D)
    flat_len = doc_lengths.reshape(n_docs)
    layer_mult = lax.map(lambda item: attend(item[0], item[1], item[2], item[3], w_value), (flat_queries, flat_keys, flat_mults, flat_len))
    tokens = enc_state.reshape(n_docs, ENC_LEN, D).astype(jnp.float32)
    row_scale = norm_gain.astype(jnp.float32) * lax.rsqrt(lax.optimization_barrier(jnp.mean(tokens * tokens, axis=-1, keepdims=True)) + 1e-06)
    inputs = (tokens * row_scale).astype(jnp.bfloat16)
    base_inputs = (baseline.reshape(n_docs, ENC_LEN, D).astype(jnp.float32) * row_scale).astype(jnp.bfloat16)
    scaled_mult = (gate_prob.reshape(n_docs, ENC_LEN, 1).astype(jnp.float32) * layer_mult).astype(jnp.bfloat16)
    doc_index = jnp.broadcast_to(jnp.arange(n_docs, dtype=jnp.int32)[:, None], (n_docs, ENC_LEN))
    flat_ids = expert_ids.reshape(n_docs, ENC_LEN).astype(jnp.int32)
    flat_slots = slot_ids.reshape(n_docs, ENC_LEN).astype(jnp.int32)

    def place_rows(values):
        filled = jnp.zeros((n_docs, EXPERTS, CAP, D), jnp.bfloat16).at[doc_index, flat_ids, flat_slots].set(values)
        return jnp.swapaxes(filled, 0, 1)
    buf_in = place_rows(inputs)
    buf_base = place_rows(base_inputs)
    buf_mult = place_rows(scaled_mult)

    def one_expert(item):
        weight_in, weight_out, rows_in, rows_base, rows_mult = item
        rows_in = rows_in.reshape(n_docs * CAP, D)
        rows_base = rows_base.reshape(n_docs * CAP, D)
        rows_mult = rows_mult.reshape(n_docs * CAP, D)
        pre_act = jnp.dot(rows_in, weight_in, preferred_element_type=jnp.float32)
        base_act = jnp.dot(rows_base, weight_in, preferred_element_type=jnp.float32)
        hidden_mult = jnp.dot(rows_mult, weight_out, preferred_element_type=jnp.float32)
        act_mult = (rescale(pre_act, base_act) * hidden_mult).astype(jnp.bfloat16)
        slot_mult = jnp.dot(act_mult, weight_in.T, preferred_element_type=jnp.float32).astype(jnp.bfloat16)
        return slot_mult.reshape(n_docs, CAP, D)
    expert_out = lax.map(one_expert, (w_in, w_out_t, buf_in, buf_base, buf_mult))
    per_token = expert_out[flat_ids, doc_index, flat_slots].astype(jnp.float32)
    result = (layer_mult + row_scale * per_token).astype(jnp.bfloat16)
    return result.reshape(GROUPS, DOC_GRP, ENC_LEN, D)
```

```python
import functools
import math

import jax
import jax.numpy as jnp
from jax import lax
from jax.experimental import pallas as pl
from jax.experimental.pallas import tpu as pltpu
from jax.sharding import PartitionSpec as P

HEADS = 16
HEAD_DIM = 64


def rescale(pre_act, base_act):
    upper_part = jnp.maximum(jnp.maximum(pre_act, base_act), 0.0)
    lower_part = jnp.maximum(-jnp.minimum(pre_act, base_act), 0.0)
    return upper_part / (upper_part + lower_part + jnp.where(upper_part > 0.0, 0.0, 1.0))


def attend(query_rows, key_rows, mult_rows, length, w_value):
    enc_len = key_rows.shape[0]
    dec_len = query_rows.shape[0]
    queries = query_rows.reshape(dec_len, HEADS, HEAD_DIM)
    keys = key_rows.reshape(enc_len, HEADS, HEAD_DIM)
    mults = mult_rows.reshape(dec_len, HEADS, HEAD_DIM)
    scores = jnp.einsum("qhd,khd->hqk", queries, keys, preferred_element_type=jnp.float32) * (
        1.0 / math.sqrt(HEAD_DIM)
    )
    valid = jnp.arange(enc_len, dtype=jnp.int32) < length
    scores = jnp.where(valid[None, None, :], scores, -jnp.inf)
    top_score = jnp.max(scores, axis=-1, keepdims=True)
    expo = jnp.exp(scores - top_score)
    attn = (expo / jnp.sum(expo, axis=-1, keepdims=True)).astype(jnp.bfloat16)
    value_mult = jnp.einsum("hqk,qhd->khd", attn, mults, preferred_element_type=jnp.float32).astype(
        jnp.bfloat16
    )
    return lax.dot_general(
        value_mult.reshape(enc_len, HEADS * HEAD_DIM),
        w_value,
        (((1,), (1,)), ((), ())),
        preferred_element_type=jnp.float32,
    )


def expert_terms(rows_in, rows_base, rows_mult, part_in, part_out):
    pre_act = jnp.einsum("erd,edf->erf", rows_in, part_in, preferred_element_type=jnp.float32)
    base_act = jnp.einsum("erd,edf->erf", rows_base, part_in, preferred_element_type=jnp.float32)
    hidden_mult = jnp.einsum(
        "erd,edf->erf", rows_mult, part_out, preferred_element_type=jnp.float32
    )
    act_mult = (rescale(pre_act, base_act) * hidden_mult).astype(jnp.bfloat16)
    return jnp.einsum("erf,edf->erd", act_mult, part_in, preferred_element_type=jnp.float32)


def times_t(left, right):
    return lax.dot_general(left, right, (((1,), (1,)), ((), ())), preferred_element_type=jnp.float32)


def whole_kernel(
    n_peers,
    n_dp,
    cap,
    chunk,
    state_at,
    base_at,
    expert_at,
    place_at,
    gate_at,
    gain_at,
    length_at,
    keys_at,
    queries_at,
    mults_at,
    value_at,
    w_in,
    w_out,
    out,
    state,
    base_state,
    expert_row,
    place_row,
    gate,
    gain,
    length,
    keys,
    queries,
    mults,
    value,
    value_mult,
    layer,
    scale,
    sends,
    all_in,
    all_out,
    held,
    ratio,
    act,
    near_sum,
    far_sum,
    far_got,
    slot_sum,
    back,
    load_sem,
    weight_sem,
    swap_send,
    swap_recv,
    row_send,
    row_recv,
    hop_send,
    hop_recv,
    part_send,
    part_recv,
    back_send,
    back_recv,
):
    n_local = w_in.shape[0]
    tokens, width = state.shape
    rows = n_peers * cap
    half = n_peers // 2
    half_rows = half * cap
    n_chunks = width // chunk
    bf16, f32 = jnp.bfloat16, jnp.float32
    me = lax.axis_index("expert")
    dp = lax.axis_index("dp")
    pair = dp + 1 - 2 * lax.rem(dp, 2)
    across = lax.rem(dp + 2, n_dp)
    mesh_id = pl.DeviceIdType.MESH
    my_half = me // half
    inner = lax.rem(my_half + lax.rem(me // (half // 2), 2), 2)

    def peer_at(step):
        peer, bit = 0, 1
        while bit < n_peers:
            digit = lax.rem(me // bit, 2)
            flip = (step // bit) % 2
            peer = peer + bit * (digit + flip - 2 * digit * flip)
            bit *= 2
        return peer

    barrier = pltpu.get_barrier_semaphore()
    for step in range(1, n_peers):
        pl.semaphore_signal(barrier, inc=1, device_id={"expert": peer_at(step)}, device_id_type=mesh_id)
    for other in (pair, across):
        pl.semaphore_signal(barrier, inc=1, device_id={"dp": other}, device_id_type=mesh_id)

    def load(pairs, first_sem):
        copies = []
        for at, (ref, held_at) in enumerate(pairs):
            copy = pltpu.make_async_copy(ref, held_at, load_sem.at[first_sem + at])
            copy.start()
            copies.append(copy)
        return copies

    small = load(
        (
            (state_at, state),
            (gain_at, gain),
            (expert_at, expert_row),
            (place_at, place_row),
            (base_at, base_state),
            (gate_at, gate),
            (length_at, length),
        ),
        0,
    )
    loads = load(((queries_at, queries), (keys_at, keys), (mults_at, mults), (value_at, value)), len(small))
    own_weights = []
    for at, (ref, held_at) in enumerate(((w_in, all_in), (w_out, all_out))):
        copy = pltpu.make_async_copy(ref, held_at.at[0], weight_sem.at[at])
        copy.start()
        own_weights.append(copy)
    for copy in small[:4]:
        copy.wait()

    expert = expert_row[...]
    owner = lax.div(expert, n_local)
    slot_row = lax.rem(expert, n_local) * rows + owner * cap + place_row[...]

    def column(row):
        return jnp.transpose(jnp.broadcast_to(row, (128, tokens)))[:, :1]

    def place_rows(a, l, values):
        at = lax.broadcasted_iota(jnp.int32, (rows, tokens), 0) + l * rows
        onehot = jnp.where(at == slot_row, 1.0, 0.0).astype(bf16)
        sends[a, l] = jnp.dot(onehot, values, preferred_element_type=f32).astype(bf16)

    def block_of(src):
        return pl.ds(pl.multiple_of(src * cap, cap), cap)

    def near_block(src):
        return block_of(lax.rem(src, half))

    def far_block(src):
        return pl.ds(pl.multiple_of(half_rows + lax.rem(src, half) * cap, cap), cap)

    same, cross = 0, 1

    def row_copy(a, l, step):
        peer = peer_at(step)
        kind = step // half
        return pltpu.make_async_remote_copy(
            src_ref=sends.at[a, l, block_of(peer), :],
            dst_ref=held.at[a, l, kind, near_block(me), :],
            send_sem=row_send.at[0],
            recv_sem=row_recv.at[a, l, kind * (step - half + 1)],
            device_id={"expert": peer},
            device_id_type=mesh_id,
        )

    def keep_own(a, l):
        held[a, l, same, near_block(me), :] = sends[a, l, block_of(me), :]

    def hop_copy(a, l, kind, step):
        src = peer_at(step)
        return pltpu.make_async_remote_copy(
            src_ref=held.at[a, l, kind, near_block(src), :],
            dst_ref=held.at[a, l, kind, far_block(src), :],
            send_sem=hop_send.at[0],
            recv_sem=hop_recv.at[a, l, kind],
            device_id={"dp": across},
            device_id_type=mesh_id,
        )

    def own_hop(a, l):
        return pltpu.make_async_remote_copy(
            src_ref=sends.at[a, l, block_of(me), :],
            dst_ref=held.at[a, l, same, far_block(me), :],
            send_sem=hop_send.at[0],
            recv_sem=hop_recv.at[a, l, same],
            device_id={"dp": across},
            device_id_type=mesh_id,
        )

    def await_bytes(ref, sem):
        pltpu.make_async_copy(ref, ref, sem).wait()

    def cross_step(k):
        return n_peers - 1 - lax.rem(k + (half // 2) * inner, half)

    def send_same(a, l):
        for step in range(1, half):
            row_copy(a, l, step).start()

    def send_cross(a, l):
        for step in range(n_peers - 1, half - 1, -1):
            row_copy(a, l, step).start()

    def relay_same(a, l):
        await_bytes(held.at[a, l, same, pl.ds(0, (half - 1) * cap), :], row_recv.at[a, l, 0])
        for step in range(1, half):
            hop_copy(a, l, same, step).start()

    def relay_cross(a, l, ks):
        for k in ks:
            step = cross_step(k)
            await_bytes(held.at[a, l, cross, pl.ds(0, cap), :], row_recv.at[a, l, step - half + 1])
            hop_copy(a, l, cross, step).start()

    first, later = range(0, half // 2), range(half // 2, half)

    def wait_unit(a, l, kind):
        await_bytes(held.at[a, l, kind, pl.ds(half_rows, half_rows), :], hop_recv.at[a, l, kind])

    token_rows = state[...].astype(f32)
    scale[...] = gain[...] * lax.rsqrt(
        jnp.mean(token_rows * token_rows, axis=-1, keepdims=True) + 1e-06
    )
    inputs = (token_rows * scale[...]).astype(bf16)
    for l in range(n_local):
        place_rows(0, l, inputs)
    small[4].wait()
    base_inputs = (base_state[...].astype(f32) * scale[...]).astype(bf16)
    for l in range(n_local):
        place_rows(1, l, base_inputs)
        for a in range(2):
            keep_own(a, l)
    for copy in small[5:]:
        copy.wait()
    with jax.named_scope("barr"):
        pl.semaphore_wait(barrier, n_peers + 1)
    for l in range(n_local):
        for a in range(2):
            own_hop(a, l).start()
    for l in range(n_local):
        for a in range(2):
            send_same(a, l)
        send_cross(l, 0)

    swaps = []
    for at, (ref, held_at) in enumerate(((w_in, all_in), (w_out, all_out))):
        swap = pltpu.make_async_remote_copy(
            src_ref=ref,
            dst_ref=held_at.at[1],
            send_sem=swap_send.at[at],
            recv_sem=swap_recv.at[at],
            device_id={"dp": pair},
            device_id_type=mesh_id,
        )
        swap.start()
        swaps.append(swap)

    for copy in loads:
        copy.wait()

    def two_heads(both):
        cols = pl.ds(pl.multiple_of(both * 2 * HEAD_DIM, 2 * HEAD_DIM), 2 * HEAD_DIM)
        query, key, mult = queries[:, cols], keys[:, cols], mults[:, cols]
        first_head = lax.broadcasted_iota(jnp.int32, query.shape, 1) < HEAD_DIM
        zero = jnp.zeros_like(query)
        found = []
        for head in range(2):
            mine = jnp.where(first_head, query, zero) if head == 0 else jnp.where(first_head, zero, query)
            scores = times_t(key, mine) * (1.0 / math.sqrt(HEAD_DIM))
            at = lax.broadcasted_iota(jnp.int32, scores.shape, 0)
            scores = jnp.where(at < length[...], scores, -jnp.inf)
            expo = jnp.exp(scores - jnp.max(scores, axis=0, keepdims=True))
            attn = (expo / jnp.sum(expo, axis=0, keepdims=True)).astype(bf16)
            found.append(jnp.dot(attn, mult, preferred_element_type=f32))
        left = lax.broadcasted_iota(jnp.int32, found[0].shape, 1) < HEAD_DIM
        value_mult[:, cols] = jnp.where(left, found[0], found[1]).astype(bf16)

    pieces = width // (2 * HEAD_DIM)
    bounds = [pieces * at // 4 for at in range(5)]
    for at in range(4):
        with jax.named_scope(f"attn{at}"):
            pl.loop(bounds[at], bounds[at + 1])(two_heads)
        if at == 2:
            with jax.named_scope("r_s00"):
                relay_same(0, 0)

    def chunk_of(c):
        return pl.ds(pl.multiple_of(c * chunk, chunk), chunk)

    with jax.named_scope("layer"):

        @pl.loop(0, n_chunks)
        def _(c):
            layer[:, chunk_of(c)] = times_t(value_mult[...], value[chunk_of(c), :])

    with jax.named_scope("r_s10"):
        relay_same(1, 0)
    scaled = (column(gate[...]) * layer[...]).astype(bf16)
    for l in range(n_local):
        place_rows(2, l, scaled)
        keep_own(2, l)
        own_hop(2, l).start()
        send_same(2, l)

    def ratio_of(l, kind):
        @pl.loop(0, 2)
        def _(shard):
            weight = all_in[shard, l]
            pre = times_t(held[0, l, kind], weight)
            base = times_t(held[1, l, kind], weight)
            ratio[l, kind, shard] = rescale(pre, base)

    def part_copy(l, kind, c):
        return pltpu.make_async_remote_copy(
            src_ref=far_sum.at[l, kind, :, chunk_of(c)],
            dst_ref=far_got.at[l, kind, :, chunk_of(c)],
            send_sem=part_send.at[0],
            recv_sem=part_recv.at[l, kind, c],
            device_id={"dp": across},
            device_id_type=mesh_id,
        )

    def sums_of(l, kind):
        @pl.loop(0, 2)
        def _(shard):
            hidden = times_t(held[2, l, kind], all_out[shard, l])
            act[shard] = (ratio[l, kind, shard] * hidden).astype(bf16)

        @pl.loop(0, n_chunks)
        def _(c):
            cols = chunk_of(c)
            total = jnp.dot(act[0], all_in[0, l, :, cols], preferred_element_type=f32) + jnp.dot(
                act[1], all_in[1, l, :, cols], preferred_element_type=f32
            )
            near_sum[l, kind, :, cols] = total[:half_rows]
            far_sum[l, kind, :, cols] = total[half_rows:].astype(bf16)
            part_copy(l, kind, c).start()

    def steps_of(kind):
        return range(1, half) if kind == same else range(half, n_peers)

    def back_copy(l, kind, c, step):
        peer = peer_at(step)
        return pltpu.make_async_remote_copy(
            src_ref=slot_sum.at[l, kind, near_block(peer), chunk_of(c)],
            dst_ref=back.at[kind, l, near_block(me), chunk_of(c)],
            send_sem=back_send.at[0],
            recv_sem=back_recv.at[kind, c],
            device_id={"expert": peer},
            device_id_type=mesh_id,
        )

    def send_back(l, kind):
        @pl.loop(0, n_chunks)
        def _(c):
            part_copy(l, kind, c).wait_recv()
            cols = chunk_of(c)
            slot_sum[l, kind, :, cols] = (
                near_sum[l, kind, :, cols] + far_got[l, kind, :, cols].astype(f32)
            ).astype(bf16)
            for step in steps_of(kind)[::-1]:
                back_copy(l, kind, c, step).start()
            if kind == same:
                mine = near_block(me)
                back[same, l, mine, cols] = (
                    near_sum[l, same, mine, cols] + far_got[l, same, mine, cols].astype(f32)
                ).astype(bf16)

    def scoped(name, call, *args):
        with jax.named_scope(name):
            call(*args)

    scoped("r_c00a", relay_cross, 0, 0, first)
    scoped("r_c00b", relay_cross, 0, 0, later)
    send_cross(2, 0)
    scoped("r_s01", relay_same, 0, 1)
    scoped("r_c10a", relay_cross, 1, 0, first)
    scoped("r_c10b", relay_cross, 1, 0, later)
    send_cross(0, 1)
    scoped("r_s11", relay_same, 1, 1)
    with jax.named_scope("weights"):
        for copy in own_weights:
            copy.wait()
        for swap in swaps:
            swap.wait_recv()
    scoped("w_s00", wait_unit, 0, 0, same)
    scoped("w_s10", wait_unit, 1, 0, same)
    scoped("ratio0s", ratio_of, 0, same)
    scoped("r_s20", relay_same, 2, 0)
    scoped("r_c20a", relay_cross, 2, 0, first)
    scoped("r_c20b", relay_cross, 2, 0, later)
    send_cross(1, 1)
    scoped("w_s20", wait_unit, 2, 0, same)
    scoped("sums0s", sums_of, 0, same)
    scoped("r_c01a", relay_cross, 0, 1, first)
    scoped("w_c00", wait_unit, 0, 0, cross)
    scoped("w_c10", wait_unit, 1, 0, cross)
    scoped("ratio0c", ratio_of, 0, cross)
    scoped("r_c01b", relay_cross, 0, 1, later)
    send_cross(2, 1)
    scoped("w_c20", wait_unit, 2, 0, cross)
    scoped("sums0c", sums_of, 0, cross)
    scoped("back0s", send_back, 0, same)
    scoped("r_c11a", relay_cross, 1, 1, first)
    scoped("w_s01", wait_unit, 0, 1, same)
    scoped("w_s11", wait_unit, 1, 1, same)
    scoped("ratio1s", ratio_of, 1, same)
    scoped("r_c11b", relay_cross, 1, 1, later)
    scoped("back0c", send_back, 0, cross)
    scoped("r_c21a", relay_cross, 2, 1, first)
    scoped("w_c01", wait_unit, 0, 1, cross)
    scoped("w_c11", wait_unit, 1, 1, cross)
    scoped("ratio1c", ratio_of, 1, cross)
    scoped("r_c21b", relay_cross, 2, 1, later)
    scoped("r_s21", relay_same, 2, 1)
    scoped("w_c21", wait_unit, 2, 1, cross)
    scoped("sums1c", sums_of, 1, cross)
    scoped("w_s21", wait_unit, 2, 1, same)
    scoped("sums1s", sums_of, 1, same)
    scoped("back1c", send_back, 1, cross)
    scoped("back1s", send_back, 1, same)

    group = owner // half
    other = group + my_half - 2 * group * my_half
    in_half = lax.rem(expert, n_local) * half_rows + lax.rem(owner, half) * cap + place_row[...]
    got_row = other * (n_local * half_rows) + in_half
    got_col = column(got_row.astype(f32))

    def pick_of(kind):
        shape = (tokens, n_local * half_rows)
        at = lax.broadcasted_iota(jnp.int32, shape, 1) + kind * n_local * half_rows
        return jnp.where(at.astype(f32) == got_col, 1.0, 0.0).astype(bf16)

    def wait_back(kind, c):
        remote = len(steps_of(kind)) * cap
        await_bytes(back.at[kind, :, pl.ds(0, remote), chunk_of(c)], back_recv.at[kind, c])

    def got_of(kind, cols):
        return back[kind, :, :, cols].reshape(n_local * half_rows, chunk)

    with jax.named_scope("pick_c"):
        pick = pick_of(cross)
        for c in range(n_chunks):
            wait_back(cross, c)
            cols = chunk_of(c)
            layer[:, cols] += scale[:, cols] * jnp.dot(pick, got_of(cross, cols), preferred_element_type=f32)
    with jax.named_scope("pick_s"):
        pick = pick_of(same)
        for c in range(n_chunks):
            cols = chunk_of(c)
            with jax.named_scope(f"w_{c}"):
                wait_back(same, c)
            out[:, cols] = (
                layer[:, cols] + scale[:, cols] * jnp.dot(pick, got_of(same, cols), preferred_element_type=f32)
            ).astype(bf16)

    with jax.named_scope("drain"):
        for swap in swaps:
            swap.wait_send()
        remote = (n_peers - 1) * cap
        await_bytes(sends.at[:, :, pl.ds(0, remote), :], row_send.at[0])
        await_bytes(sends, hop_send.at[0])
        await_bytes(far_sum, part_send.at[0])
        await_bytes(sends.at[0, :, pl.ds(0, remote), :], back_send.at[0])


def whole_pass(
    state, base_state, keys, queries, mults, length, expert, place, gate, gain, w_in, w_out_t, value, n_peers, n_dp, cap
):
    tokens, width = state.shape
    n_local, _, part = w_in.shape
    w_in, w_out_t = jnp.swapaxes(w_in, 1, 2), jnp.swapaxes(w_out_t, 1, 2)
    rows = n_peers * cap
    half_rows = rows // 2
    chunk = width // 4
    n_chunks = width // chunk
    bf16, f32 = jnp.bfloat16, jnp.float32
    dma = pltpu.SemaphoreType.DMA
    vmem = pl.BlockSpec(memory_space=pltpu.VMEM)
    anyw = pl.BlockSpec(memory_space=pl.ANY)
    halves = (n_local, 2, half_rows, width)
    return pl.pallas_call(
        functools.partial(whole_kernel, n_peers, n_dp, cap, chunk),
        out_shape=jax.ShapeDtypeStruct((tokens, width), bf16),
        in_specs=[anyw] * 13,
        out_specs=vmem,
        scratch_shapes=[
            pltpu.VMEM(state.shape, bf16),
            pltpu.VMEM(base_state.shape, bf16),
            pltpu.VMEM(expert.shape, expert.dtype),
            pltpu.VMEM(place.shape, place.dtype),
            pltpu.VMEM(gate.shape, f32),
            pltpu.VMEM((1, width), f32),
            pltpu.VMEM(length.shape, length.dtype),
            pltpu.VMEM(keys.shape, bf16),
            pltpu.VMEM(queries.shape, bf16),
            pltpu.VMEM(mults.shape, bf16),
            pltpu.VMEM(value.shape, bf16),
            pltpu.VMEM((tokens, width), bf16),
            pltpu.VMEM((tokens, width), f32),
            pltpu.VMEM((tokens, width), f32),
            pltpu.VMEM((3, n_local, rows, width), bf16),
            pltpu.VMEM((2, n_local, part, width), bf16),
            pltpu.VMEM((2, n_local, part, width), bf16),
            pltpu.VMEM((3, n_local, 2, 2 * half_rows, width), bf16),
            pltpu.VMEM((n_local, 2, 2, 2 * half_rows, part), f32),
            pltpu.VMEM((2, 2 * half_rows, part), bf16),
            pltpu.VMEM(halves, f32),
            pltpu.VMEM(halves, bf16),
            pltpu.VMEM(halves, bf16),
            pltpu.VMEM(halves, bf16),
            pltpu.VMEM((2, n_local, half_rows, width), bf16),
            dma((11,)),
            dma((2,)),
            dma((2,)),
            dma((2,)),
            dma((1,)),
            dma((3, n_local, 1 + n_peers // 2)),
            dma((1,)),
            dma((3, n_local, 2)),
            dma((1,)),
            dma((n_local, 2, n_chunks)),
            dma((1,)),
            dma((2, n_chunks)),
        ],
        compiler_params=pltpu.CompilerParams(
            collective_id=0, has_side_effects=True, vmem_limit_bytes=60 * 1024 * 1024
        ),
        name="whole_pass",
    )(
        state,
        base_state,
        expert,
        place,
        gate,
        gain[None, :],
        length,
        keys,
        queries,
        mults,
        value,
        w_in,
        w_out_t,
    )


def plain_pass(sent, w_in, w_out_t, n_peers, n_dp):
    near = 2 if n_dp % 2 == 0 else 1
    shards = [(w_in, w_out_t)]
    if near == 2:
        swap = [(i, i ^ 1) for i in range(n_dp)]
        shards.append((lax.ppermute(w_in, "dp", swap), lax.ppermute(w_out_t, "dp", swap)))
    own_rows = tuple(
        lax.all_to_all(a, "expert", split_axis=0, concat_axis=1, tiled=True) for a in sent
    )

    def partial_sum(rows):
        total = expert_terms(*rows, *shards[0])
        for part in shards[1:]:
            total = total + expert_terms(*rows, *part)
        return total

    far = n_dp // near
    far_rows = []
    for hop in range(1, far):
        ahead = [(i, (i + hop * near) % n_dp) for i in range(n_dp)]
        far_rows.append(tuple(lax.ppermute(a, "dp", ahead) for a in own_rows))
    slot_mult = partial_sum(own_rows)
    for hop in range(1, far):
        back = [((i + hop * near) % n_dp, i) for i in range(n_dp)]
        far_part = partial_sum(far_rows[hop - 1]).astype(jnp.bfloat16)
        slot_mult = slot_mult + lax.ppermute(far_part, "dp", back).astype(jnp.float32)

    return lax.all_to_all(
        slot_mult.astype(jnp.bfloat16), "expert", split_axis=1, concat_axis=0, tiled=True
    )


def body(
    enc_state,
    baseline,
    enc_keys,
    dec_queries,
    out_mult,
    doc_lengths,
    expert_ids,
    slot_ids,
    gate_prob,
    norm_gain,
    w_in,
    w_out_t,
    w_value,
):
    enc_len = enc_state.shape[2]
    feature_width = enc_state.shape[3]
    local_experts = w_in.shape[0]
    n_experts = local_experts * lax.axis_size("expert")
    n_dp = lax.axis_size("dp")
    capacity = max(2, 2 * enc_len // n_experts)

    n_peers = lax.axis_size("expert")
    if n_dp == 4 and local_experts == 2 and capacity % 16 == 0 and n_peers >= 4 and n_peers & (n_peers - 1) == 0 and feature_width % 512 == 0:
        return whole_pass(
            enc_state[0, 0],
            baseline[0, 0],
            enc_keys[0, 0],
            dec_queries[0, 0],
            out_mult[0, 0],
            doc_lengths,
            expert_ids[0],
            slot_ids[0],
            gate_prob[0],
            norm_gain,
            w_in,
            w_out_t,
            w_value,
            n_peers,
            n_dp,
            capacity,
        )[None, None]

    tokens = enc_state[0, 0].astype(jnp.float32)
    row_scale = norm_gain * lax.rsqrt(jnp.mean(tokens * tokens, axis=-1, keepdims=True) + 1e-06)
    inputs = (tokens * row_scale).astype(jnp.bfloat16)
    base_inputs = (baseline[0, 0].astype(jnp.float32) * row_scale).astype(jnp.bfloat16)
    flat_slot = expert_ids[0, 0] * capacity + slot_ids[0, 0]
    onehot = (
        flat_slot[None, :] == jnp.arange(n_experts * capacity, dtype=jnp.int32)[:, None]
    ).astype(jnp.bfloat16)

    def dispatch(values):
        placed = jnp.dot(onehot, values, preferred_element_type=jnp.float32).astype(jnp.bfloat16)
        return placed.reshape(n_experts, capacity, feature_width)

    layer_mult = attend(
        dec_queries[0, 0], enc_keys[0, 0], out_mult[0, 0], doc_lengths[0, 0], w_value
    )
    scaled_mult = (gate_prob[0, 0][:, None] * layer_mult).astype(jnp.bfloat16)
    sent = (dispatch(inputs), dispatch(base_inputs), dispatch(scaled_mult))
    returned = plain_pass(sent, w_in, w_out_t, n_peers, n_dp)
    per_token = lax.dot_general(
        onehot,
        returned.reshape(n_experts * capacity, feature_width),
        (((0,), (0,)), ((), ())),
        preferred_element_type=jnp.float32,
    )
    result = (layer_mult + row_scale * per_token).astype(jnp.bfloat16)
    return result[None, None]


def solution(mesh):
    in_specs = (
        P("dp", "expert", None, None),
        P("dp", "expert", None, None),
        P("dp", "expert", None, None),
        P("dp", "expert", None, None),
        P("dp", "expert", None, None),
        P("dp", "expert"),
        P("dp", "expert", None),
        P("dp", "expert", None),
        P("dp", "expert", None),
        P(),
        P("expert", None, "dp"),
        P("expert", None, "dp"),
        P(),
    )
    out_specs = P("dp", "expert", None, None)
    return jax.shard_map(body, mesh=mesh, in_specs=in_specs, out_specs=out_specs, check_vma=False)
```

```python
import functools
import math

import jax
import jax.numpy as jnp
from jax import lax
from jax.experimental import pallas as pl
from jax.experimental.pallas import tpu as pltpu
from jax.sharding import PartitionSpec as P

HEADS = 16
HEAD_DIM = 64


def rescale(pre_act, base_act):
    upper_part = jnp.maximum(jnp.maximum(pre_act, base_act), 0.0)
    lower_part = jnp.maximum(-jnp.minimum(pre_act, base_act), 0.0)
    return upper_part / (upper_part + lower_part + jnp.where(upper_part > 0.0, 0.0, 1.0))


def attend(query_rows, key_rows, mult_rows, length, w_value):
    enc_len = key_rows.shape[0]
    dec_len = query_rows.shape[0]
    queries = query_rows.reshape(dec_len, HEADS, HEAD_DIM)
    keys = key_rows.reshape(enc_len, HEADS, HEAD_DIM)
    mults = mult_rows.reshape(dec_len, HEADS, HEAD_DIM)
    scores = jnp.einsum("qhd,khd->hqk", queries, keys, preferred_element_type=jnp.float32) * (
        1.0 / math.sqrt(HEAD_DIM)
    )
    valid = jnp.arange(enc_len, dtype=jnp.int32) < length
    scores = jnp.where(valid[None, None, :], scores, -jnp.inf)
    top_score = jnp.max(scores, axis=-1, keepdims=True)
    expo = jnp.exp(scores - top_score)
    attn = (expo / jnp.sum(expo, axis=-1, keepdims=True)).astype(jnp.bfloat16)
    value_mult = jnp.einsum("hqk,qhd->khd", attn, mults, preferred_element_type=jnp.float32).astype(
        jnp.bfloat16
    )
    return lax.dot_general(
        value_mult.reshape(enc_len, HEADS * HEAD_DIM),
        w_value,
        (((1,), (1,)), ((), ())),
        preferred_element_type=jnp.float32,
    )


def expert_terms(rows_in, rows_base, rows_mult, part_in, part_out):
    pre_act = jnp.einsum("erd,edf->erf", rows_in, part_in, preferred_element_type=jnp.float32)
    base_act = jnp.einsum("erd,edf->erf", rows_base, part_in, preferred_element_type=jnp.float32)
    hidden_mult = jnp.einsum(
        "erd,edf->erf", rows_mult, part_out, preferred_element_type=jnp.float32
    )
    act_mult = (rescale(pre_act, base_act) * hidden_mult).astype(jnp.bfloat16)
    return jnp.einsum("erf,edf->erd", act_mult, part_in, preferred_element_type=jnp.float32)


def times_t(left, right):
    return lax.dot_general(left, right, (((1,), (1,)), ((), ())), preferred_element_type=jnp.float32)


def whole_kernel(
    n_peers,
    n_dp,
    cap,
    chunk,
    state_at,
    base_at,
    expert_at,
    place_at,
    gate_at,
    gain_at,
    length_at,
    keys_at,
    queries_at,
    mults_at,
    value_at,
    w_in,
    w_out,
    out,
    state,
    base_state,
    expert_row,
    place_row,
    gate,
    gain,
    length,
    keys,
    queries,
    mults,
    value,
    value_mult,
    layer,
    scale,
    sends,
    all_in,
    all_out,
    held,
    ratio,
    act,
    near_sum,
    far_sum,
    far_got,
    slot_sum,
    back,
    load_sem,
    weight_sem,
    swap_send,
    swap_recv,
    row_send,
    row_recv,
    hop_send,
    hop_recv,
    part_send,
    part_recv,
    back_send,
    back_recv,
):
    n_local = w_in.shape[0]
    tokens, width = state.shape
    rows = n_peers * cap
    half = n_peers // 2
    half_rows = half * cap
    n_chunks = width // chunk
    bf16, f32 = jnp.bfloat16, jnp.float32
    me = lax.axis_index("expert")
    dp = lax.axis_index("dp")
    pair = dp + 1 - 2 * lax.rem(dp, 2)
    across = lax.rem(dp + 2, n_dp)
    mesh_id = pl.DeviceIdType.MESH
    my_half = me // half
    inner = lax.rem(my_half + lax.rem(me // (half // 2), 2), 2)

    def peer_at(step):
        peer, bit = 0, 1
        while bit < n_peers:
            digit = lax.rem(me // bit, 2)
            flip = (step // bit) % 2
            peer = peer + bit * (digit + flip - 2 * digit * flip)
            bit *= 2
        return peer

    barrier = pltpu.get_barrier_semaphore()
    for step in range(1, n_peers):
        pl.semaphore_signal(barrier, inc=1, device_id={"expert": peer_at(step)}, device_id_type=mesh_id)
    for other in (pair, across):
        pl.semaphore_signal(barrier, inc=1, device_id={"dp": other}, device_id_type=mesh_id)

    def load(pairs, first_sem):
        copies = []
        for at, (ref, held_at) in enumerate(pairs):
            copy = pltpu.make_async_copy(ref, held_at, load_sem.at[first_sem + at])
            copy.start()
            copies.append(copy)
        return copies

    small = load(
        (
            (state_at, state),
            (gain_at, gain),
            (expert_at, expert_row),
            (place_at, place_row),
            (base_at, base_state),
            (gate_at, gate),
            (length_at, length),
        ),
        0,
    )
    loads = load(((queries_at, queries), (keys_at, keys), (mults_at, mults), (value_at, value)), len(small))
    own_weights = []
    for at, (ref, held_at) in enumerate(((w_in, all_in), (w_out, all_out))):
        copy = pltpu.make_async_copy(ref, held_at.at[0], weight_sem.at[at])
        copy.start()
        own_weights.append(copy)
    for copy in small[:4]:
        copy.wait()

    expert = expert_row[...]
    owner = lax.div(expert, n_local)
    slot_row = lax.rem(expert, n_local) * rows + owner * cap + place_row[...]

    def column(row):
        return jnp.transpose(jnp.broadcast_to(row, (128, tokens)))[:, :1]

    def place_rows(a, l, values):
        at = lax.broadcasted_iota(jnp.int32, (rows, tokens), 0) + l * rows
        onehot = jnp.where(at == slot_row, 1.0, 0.0).astype(bf16)
        sends[a, l] = jnp.dot(onehot, values, preferred_element_type=f32).astype(bf16)

    def block_of(src):
        return pl.ds(pl.multiple_of(src * cap, cap), cap)

    def near_block(src):
        return block_of(lax.rem(src, half))

    def far_block(src):
        return pl.ds(pl.multiple_of(half_rows + lax.rem(src, half) * cap, cap), cap)

    same, cross = 0, 1

    def row_copy(a, l, step):
        peer = peer_at(step)
        kind = step // half
        return pltpu.make_async_remote_copy(
            src_ref=sends.at[a, l, block_of(peer), :],
            dst_ref=held.at[a, l, kind, near_block(me), :],
            send_sem=row_send.at[0],
            recv_sem=row_recv.at[a, l, step],
            device_id={"expert": peer},
            device_id_type=mesh_id,
        )

    def keep_own(a, l):
        held[a, l, same, near_block(me), :] = sends[a, l, block_of(me), :]

    def hop_copy(a, l, kind, step):
        src = peer_at(step)
        return pltpu.make_async_remote_copy(
            src_ref=held.at[a, l, kind, near_block(src), :],
            dst_ref=held.at[a, l, kind, far_block(src), :],
            send_sem=hop_send.at[0],
            recv_sem=hop_recv.at[a, l, kind],
            device_id={"dp": across},
            device_id_type=mesh_id,
        )

    def own_hop(a, l):
        return pltpu.make_async_remote_copy(
            src_ref=sends.at[a, l, block_of(me), :],
            dst_ref=held.at[a, l, same, far_block(me), :],
            send_sem=hop_send.at[0],
            recv_sem=hop_recv.at[a, l, same],
            device_id={"dp": across},
            device_id_type=mesh_id,
        )

    def await_bytes(ref, sem):
        pltpu.make_async_copy(ref, ref, sem).wait()

    cross_steps = [*range(n_peers - 2, half - 1, -2), *range(n_peers - 1, half, -2)]
    first, later = cross_steps[: half // 2], cross_steps[half // 2 :]

    def send_same(a, l):
        for step in range(1, half):
            row_copy(a, l, step).start()

    def send_cross(a, l):
        for step in cross_steps:
            row_copy(a, l, step).start()

    def relay(a, l, steps):
        for step in steps:
            kind = step // half
            await_bytes(held.at[a, l, kind, pl.ds(0, cap), :], row_recv.at[a, l, step])
            hop_copy(a, l, kind, step).start()

    def relay_same(a, l):
        relay(a, l, range(1, half))

    def wait_unit(a, l, kind):
        await_bytes(held.at[a, l, kind, pl.ds(half_rows, half_rows), :], hop_recv.at[a, l, kind])

    token_rows = state[...].astype(f32)
    scale[...] = gain[...] * lax.rsqrt(
        jnp.mean(token_rows * token_rows, axis=-1, keepdims=True) + 1e-06
    )
    inputs = (token_rows * scale[...]).astype(bf16)
    for l in range(n_local):
        place_rows(0, l, inputs)
    small[4].wait()
    base_inputs = (base_state[...].astype(f32) * scale[...]).astype(bf16)
    for l in range(n_local):
        place_rows(1, l, base_inputs)
        for a in range(2):
            keep_own(a, l)
    for copy in small[5:]:
        copy.wait()
    with jax.named_scope("barr"):
        pl.semaphore_wait(barrier, n_peers + 1)
    for l in range(n_local):
        for a in range(2):
            own_hop(a, l).start()
    send_same(0, 0)
    send_cross(0, 0)
    send_same(1, 0)
    send_same(0, 1)
    send_cross(1, 0)
    send_same(1, 1)

    swaps = []
    for at, (ref, held_at) in enumerate(((w_in, all_in), (w_out, all_out))):
        swap = pltpu.make_async_remote_copy(
            src_ref=ref,
            dst_ref=held_at.at[1],
            send_sem=swap_send.at[at],
            recv_sem=swap_recv.at[at],
            device_id={"dp": pair},
            device_id_type=mesh_id,
        )
        swap.start()
        swaps.append(swap)

    for copy in loads:
        copy.wait()

    def two_heads(both):
        cols = pl.ds(pl.multiple_of(both * 2 * HEAD_DIM, 2 * HEAD_DIM), 2 * HEAD_DIM)
        query, key, mult = queries[:, cols], keys[:, cols], mults[:, cols]
        first_head = lax.broadcasted_iota(jnp.int32, query.shape, 1) < HEAD_DIM
        zero = jnp.zeros_like(query)
        found = []
        for head in range(2):
            mine = jnp.where(first_head, query, zero) if head == 0 else jnp.where(first_head, zero, query)
            scores = times_t(key, mine) * (1.0 / math.sqrt(HEAD_DIM))
            at = lax.broadcasted_iota(jnp.int32, scores.shape, 0)
            scores = jnp.where(at < length[...], scores, -jnp.inf)
            expo = jnp.exp(scores - jnp.max(scores, axis=0, keepdims=True))
            attn = (expo / jnp.sum(expo, axis=0, keepdims=True)).astype(bf16)
            found.append(jnp.dot(attn, mult, preferred_element_type=f32))
        left = lax.broadcasted_iota(jnp.int32, found[0].shape, 1) < HEAD_DIM
        value_mult[:, cols] = jnp.where(left, found[0], found[1]).astype(bf16)

    pieces = width // (2 * HEAD_DIM)
    bounds = [pieces * at // 4 for at in range(5)]
    for at in range(4):
        with jax.named_scope(f"attn{at}"):
            pl.loop(bounds[at], bounds[at + 1])(two_heads)
    with jax.named_scope("r_s00"):
        relay(0, 0, range(1, half - 1))
    with jax.named_scope("r_c00a"):
        relay(0, 0, first[:1])

    def chunk_of(c):
        return pl.ds(pl.multiple_of(c * chunk, chunk), chunk)

    with jax.named_scope("layer"):

        @pl.loop(0, n_chunks)
        def _(c):
            layer[:, chunk_of(c)] = times_t(value_mult[...], value[chunk_of(c), :])

    with jax.named_scope("r_s00b"):
        relay(0, 0, [half - 1])
    scaled = (column(gate[...]) * layer[...]).astype(bf16)
    for l in range(n_local):
        place_rows(2, l, scaled)
        keep_own(2, l)
        own_hop(2, l).start()
        send_same(2, l)

    def ratio_of(l, kind):
        @pl.loop(0, 2)
        def _(shard):
            weight = all_in[shard, l]
            pre = times_t(held[0, l, kind], weight)
            base = times_t(held[1, l, kind], weight)
            ratio[l, kind, shard] = rescale(pre, base)

    def part_copy(l, kind, c):
        return pltpu.make_async_remote_copy(
            src_ref=far_sum.at[l, kind, :, chunk_of(c)],
            dst_ref=far_got.at[l, kind, :, chunk_of(c)],
            send_sem=part_send.at[0],
            recv_sem=part_recv.at[l, kind, c],
            device_id={"dp": across},
            device_id_type=mesh_id,
        )

    def sums_of(l, kind, then=None):
        @pl.loop(0, 2)
        def _(shard):
            hidden = times_t(held[2, l, kind], all_out[shard, l])
            act[shard] = (ratio[l, kind, shard] * hidden).astype(bf16)

        @pl.loop(0, n_chunks)
        def _(c):
            cols = chunk_of(c)
            total = jnp.dot(act[0], all_in[0, l, :, cols], preferred_element_type=f32) + jnp.dot(
                act[1], all_in[1, l, :, cols], preferred_element_type=f32
            )
            near_sum[l, kind, :, cols] = total[:half_rows]
            far_sum[l, kind, :, cols] = total[half_rows:].astype(bf16)
            part_copy(l, kind, c).start()
            if then is not None:
                then(c)

    def steps_of(kind):
        return range(1, half) if kind == same else range(half, n_peers)

    def back_copy(l, kind, c, step):
        peer = peer_at(step)
        return pltpu.make_async_remote_copy(
            src_ref=slot_sum.at[l, kind, near_block(peer), chunk_of(c)],
            dst_ref=back.at[kind, l, near_block(me), chunk_of(c)],
            send_sem=back_send.at[0],
            recv_sem=back_recv.at[kind, c],
            device_id={"expert": peer},
            device_id_type=mesh_id,
        )

    def back_chunk(l, kind, c):
        part_copy(l, kind, c).wait_recv()
        cols = chunk_of(c)
        slot_sum[l, kind, :, cols] = (
            near_sum[l, kind, :, cols] + far_got[l, kind, :, cols].astype(f32)
        ).astype(bf16)
        for step in steps_of(kind)[::-1]:
            back_copy(l, kind, c, step).start()
        if kind == same:
            mine = near_block(me)
            back[same, l, mine, cols] = (
                near_sum[l, same, mine, cols] + far_got[l, same, mine, cols].astype(f32)
            ).astype(bf16)

    def send_back(l, kind):
        pl.loop(0, n_chunks)(functools.partial(back_chunk, l, kind))

    def scoped(name, call, *args):
        with jax.named_scope(name):
            call(*args)

    scoped("r_c00b", relay, 0, 0, first[1:])
    scoped("r_c00c", relay, 0, 0, later)
    send_cross(2, 0)
    scoped("r_s10", relay_same, 1, 0)
    scoped("r_s01", relay_same, 0, 1)
    with jax.named_scope("weights"):
        for copy in own_weights:
            copy.wait()
        for swap in swaps:
            swap.wait_recv()
    scoped("w_s00", wait_unit, 0, 0, same)
    scoped("w_s10", wait_unit, 1, 0, same)
    scoped("ratio0s", ratio_of, 0, same)
    scoped("r_c10a", relay, 1, 0, first)
    scoped("r_c10b", relay, 1, 0, later)
    send_cross(0, 1)
    scoped("r_s11", relay_same, 1, 1)
    scoped("r_s20", relay_same, 2, 0)
    scoped("r_c20a", relay, 2, 0, first)
    scoped("r_c20b", relay, 2, 0, later)
    send_cross(1, 1)
    scoped("w_s20", wait_unit, 2, 0, same)
    scoped("sums0s", sums_of, 0, same)
    scoped("r_c01a", relay, 0, 1, first)
    scoped("w_c00", wait_unit, 0, 0, cross)
    scoped("w_c10", wait_unit, 1, 0, cross)
    scoped("ratio0c", ratio_of, 0, cross)
    scoped("r_c01b", relay, 0, 1, later)
    send_cross(2, 1)
    scoped("w_c20", wait_unit, 2, 0, cross)
    scoped("sums0c", sums_of, 0, cross)
    scoped("w_s01", wait_unit, 0, 1, same)
    scoped("w_s11", wait_unit, 1, 1, same)
    scoped("ratio1s", ratio_of, 1, same)
    scoped("r_c11a", relay, 1, 1, first)
    scoped("r_c11b", relay, 1, 1, later)
    scoped("back0s", send_back, 0, same)
    scoped("r_c21a", relay, 2, 1, first)
    scoped("back0c", send_back, 0, cross)
    scoped("w_c01", wait_unit, 0, 1, cross)
    scoped("w_c11", wait_unit, 1, 1, cross)
    scoped("ratio1c", ratio_of, 1, cross)
    scoped("r_c21b", relay, 2, 1, later)
    scoped("r_s21", relay_same, 2, 1)
    scoped("w_c21", wait_unit, 2, 1, cross)
    scoped("sums1c", sums_of, 1, cross)
    scoped("w_s21", wait_unit, 2, 1, same)
    scoped("sums1s", sums_of, 1, same, functools.partial(back_chunk, 1, cross))
    scoped("back1s", send_back, 1, same)

    group = owner // half
    other = group + my_half - 2 * group * my_half
    in_half = lax.rem(expert, n_local) * half_rows + lax.rem(owner, half) * cap + place_row[...]
    got_row = other * (n_local * half_rows) + in_half
    got_col = column(got_row.astype(f32))

    def pick_of(kind):
        shape = (tokens, n_local * half_rows)
        at = lax.broadcasted_iota(jnp.int32, shape, 1) + kind * n_local * half_rows
        return jnp.where(at.astype(f32) == got_col, 1.0, 0.0).astype(bf16)

    def wait_back(kind, c):
        remote = len(steps_of(kind)) * cap
        await_bytes(back.at[kind, :, pl.ds(0, remote), chunk_of(c)], back_recv.at[kind, c])

    def got_of(kind, cols):
        return back[kind, :, :, cols].reshape(n_local * half_rows, chunk)

    with jax.named_scope("pick_c"):
        pick = pick_of(cross)
        for c in range(n_chunks):
            wait_back(cross, c)
            cols = chunk_of(c)
            layer[:, cols] += scale[:, cols] * jnp.dot(pick, got_of(cross, cols), preferred_element_type=f32)
    with jax.named_scope("pick_s"):
        pick = pick_of(same)
        for c in range(n_chunks):
            cols = chunk_of(c)
            with jax.named_scope(f"w_{c}"):
                wait_back(same, c)
            out[:, cols] = (
                layer[:, cols] + scale[:, cols] * jnp.dot(pick, got_of(same, cols), preferred_element_type=f32)
            ).astype(bf16)

    with jax.named_scope("drain"):
        for swap in swaps:
            swap.wait_send()
        remote = (n_peers - 1) * cap
        await_bytes(sends.at[:, :, pl.ds(0, remote), :], row_send.at[0])
        await_bytes(sends, hop_send.at[0])
        await_bytes(far_sum, part_send.at[0])
        await_bytes(sends.at[0, :, pl.ds(0, remote), :], back_send.at[0])


def whole_pass(
    state, base_state, keys, queries, mults, length, expert, place, gate, gain, w_in, w_out_t, value, n_peers, n_dp, cap
):
    tokens, width = state.shape
    n_local, _, part = w_in.shape
    w_in, w_out_t = jnp.swapaxes(w_in, 1, 2), jnp.swapaxes(w_out_t, 1, 2)
    rows = n_peers * cap
    half_rows = rows // 2
    chunk = width // 4
    n_chunks = width // chunk
    bf16, f32 = jnp.bfloat16, jnp.float32
    dma = pltpu.SemaphoreType.DMA
    vmem = pl.BlockSpec(memory_space=pltpu.VMEM)
    anyw = pl.BlockSpec(memory_space=pl.ANY)
    halves = (n_local, 2, half_rows, width)
    return pl.pallas_call(
        functools.partial(whole_kernel, n_peers, n_dp, cap, chunk),
        out_shape=pltpu.VMEM((tokens, width), bf16),
        in_specs=[anyw] * 13,
        out_specs=vmem,
        scratch_shapes=[
            pltpu.VMEM(state.shape, bf16),
            pltpu.VMEM(base_state.shape, bf16),
            pltpu.VMEM(expert.shape, expert.dtype),
            pltpu.VMEM(place.shape, place.dtype),
            pltpu.VMEM(gate.shape, f32),
            pltpu.VMEM((1, width), f32),
            pltpu.VMEM(length.shape, length.dtype),
            pltpu.VMEM(keys.shape, bf16),
            pltpu.VMEM(queries.shape, bf16),
            pltpu.VMEM(mults.shape, bf16),
            pltpu.VMEM(value.shape, bf16),
            pltpu.VMEM((tokens, width), bf16),
            pltpu.VMEM((tokens, width), f32),
            pltpu.VMEM((tokens, width), f32),
            pltpu.VMEM((3, n_local, rows, width), bf16),
            pltpu.VMEM((2, n_local, part, width), bf16),
            pltpu.VMEM((2, n_local, part, width), bf16),
            pltpu.VMEM((3, n_local, 2, 2 * half_rows, width), bf16),
            pltpu.VMEM((n_local, 2, 2, 2 * half_rows, part), f32),
            pltpu.VMEM((2, 2 * half_rows, part), bf16),
            pltpu.VMEM(halves, f32),
            pltpu.VMEM(halves, bf16),
            pltpu.VMEM(halves, bf16),
            pltpu.VMEM(halves, bf16),
            pltpu.VMEM((2, n_local, half_rows, width), bf16),
            dma((11,)),
            dma((2,)),
            dma((2,)),
            dma((2,)),
            dma((1,)),
            dma((3, n_local, n_peers)),
            dma((1,)),
            dma((3, n_local, 2)),
            dma((1,)),
            dma((n_local, 2, n_chunks)),
            dma((1,)),
            dma((2, n_chunks)),
        ],
        compiler_params=pltpu.CompilerParams(
            collective_id=0, has_side_effects=True, vmem_limit_bytes=60 * 1024 * 1024
        ),
        name="whole_pass",
    )(
        state,
        base_state,
        expert,
        place,
        gate,
        gain[None, :],
        length,
        keys,
        queries,
        mults,
        value,
        w_in,
        w_out_t,
    )


def plain_pass(sent, w_in, w_out_t, n_peers, n_dp):
    near = 2 if n_dp % 2 == 0 else 1
    shards = [(w_in, w_out_t)]
    if near == 2:
        swap = [(i, i ^ 1) for i in range(n_dp)]
        shards.append((lax.ppermute(w_in, "dp", swap), lax.ppermute(w_out_t, "dp", swap)))
    own_rows = tuple(
        lax.all_to_all(a, "expert", split_axis=0, concat_axis=1, tiled=True) for a in sent
    )

    def partial_sum(rows):
        total = expert_terms(*rows, *shards[0])
        for part in shards[1:]:
            total = total + expert_terms(*rows, *part)
        return total

    far = n_dp // near
    far_rows = []
    for hop in range(1, far):
        ahead = [(i, (i + hop * near) % n_dp) for i in range(n_dp)]
        far_rows.append(tuple(lax.ppermute(a, "dp", ahead) for a in own_rows))
    slot_mult = partial_sum(own_rows)
    for hop in range(1, far):
        back = [((i + hop * near) % n_dp, i) for i in range(n_dp)]
        far_part = partial_sum(far_rows[hop - 1]).astype(jnp.bfloat16)
        slot_mult = slot_mult + lax.ppermute(far_part, "dp", back).astype(jnp.float32)

    return lax.all_to_all(
        slot_mult.astype(jnp.bfloat16), "expert", split_axis=1, concat_axis=0, tiled=True
    )


def body(
    enc_state,
    baseline,
    enc_keys,
    dec_queries,
    out_mult,
    doc_lengths,
    expert_ids,
    slot_ids,
    gate_prob,
    norm_gain,
    w_in,
    w_out_t,
    w_value,
):
    enc_len = enc_state.shape[2]
    feature_width = enc_state.shape[3]
    local_experts = w_in.shape[0]
    n_experts = local_experts * lax.axis_size("expert")
    n_dp = lax.axis_size("dp")
    capacity = max(2, 2 * enc_len // n_experts)

    n_peers = lax.axis_size("expert")
    if n_dp == 4 and local_experts == 2 and capacity % 16 == 0 and n_peers >= 4 and n_peers & (n_peers - 1) == 0 and feature_width % 512 == 0:
        return whole_pass(
            enc_state[0, 0],
            baseline[0, 0],
            enc_keys[0, 0],
            dec_queries[0, 0],
            out_mult[0, 0],
            doc_lengths,
            expert_ids[0],
            slot_ids[0],
            gate_prob[0],
            norm_gain,
            w_in,
            w_out_t,
            w_value,
            n_peers,
            n_dp,
            capacity,
        )[None, None]

    tokens = enc_state[0, 0].astype(jnp.float32)
    row_scale = norm_gain * lax.rsqrt(jnp.mean(tokens * tokens, axis=-1, keepdims=True) + 1e-06)
    inputs = (tokens * row_scale).astype(jnp.bfloat16)
    base_inputs = (baseline[0, 0].astype(jnp.float32) * row_scale).astype(jnp.bfloat16)
    flat_slot = expert_ids[0, 0] * capacity + slot_ids[0, 0]
    onehot = (
        flat_slot[None, :] == jnp.arange(n_experts * capacity, dtype=jnp.int32)[:, None]
    ).astype(jnp.bfloat16)

    def dispatch(values):
        placed = jnp.dot(onehot, values, preferred_element_type=jnp.float32).astype(jnp.bfloat16)
        return placed.reshape(n_experts, capacity, feature_width)

    layer_mult = attend(
        dec_queries[0, 0], enc_keys[0, 0], out_mult[0, 0], doc_lengths[0, 0], w_value
    )
    scaled_mult = (gate_prob[0, 0][:, None] * layer_mult).astype(jnp.bfloat16)
    sent = (dispatch(inputs), dispatch(base_inputs), dispatch(scaled_mult))
    returned = plain_pass(sent, w_in, w_out_t, n_peers, n_dp)
    per_token = lax.dot_general(
        onehot,
        returned.reshape(n_experts * capacity, feature_width),
        (((0,), (0,)), ((), ())),
        preferred_element_type=jnp.float32,
    )
    result = (layer_mult + row_scale * per_token).astype(jnp.bfloat16)
    return result[None, None]


def solution(mesh):
    in_specs = (
        P("dp", "expert", None, None),
        P("dp", "expert", None, None),
        P("dp", "expert", None, None),
        P("dp", "expert", None, None),
        P("dp", "expert", None, None),
        P("dp", "expert"),
        P("dp", "expert", None),
        P("dp", "expert", None),
        P("dp", "expert", None),
        P(),
        P("expert", None, "dp"),
        P("expert", None, "dp"),
        P(),
    )
    out_specs = P("dp", "expert", None, None)
    return jax.shard_map(body, mesh=mesh, in_specs=in_specs, out_specs=out_specs, check_vma=False)
```

```python
import functools
import math

import jax
import jax.numpy as jnp
from jax import lax
from jax.experimental import pallas as pl
from jax.experimental.pallas import tpu as pltpu
from jax.sharding import PartitionSpec as P

HEADS = 16
HEAD_DIM = 64


def rescale(pre_act, base_act):
    upper_part = jnp.maximum(jnp.maximum(pre_act, base_act), 0.0)
    lower_part = jnp.maximum(-jnp.minimum(pre_act, base_act), 0.0)
    return upper_part / (upper_part + lower_part + jnp.where(upper_part > 0.0, 0.0, 1.0))


def attend(query_rows, key_rows, mult_rows, length, w_value):
    enc_len = key_rows.shape[0]
    dec_len = query_rows.shape[0]
    queries = query_rows.reshape(dec_len, HEADS, HEAD_DIM)
    keys = key_rows.reshape(enc_len, HEADS, HEAD_DIM)
    mults = mult_rows.reshape(dec_len, HEADS, HEAD_DIM)
    scores = jnp.einsum("qhd,khd->hqk", queries, keys, preferred_element_type=jnp.float32) * (
        1.0 / math.sqrt(HEAD_DIM)
    )
    valid = jnp.arange(enc_len, dtype=jnp.int32) < length
    scores = jnp.where(valid[None, None, :], scores, -jnp.inf)
    top_score = jnp.max(scores, axis=-1, keepdims=True)
    expo = jnp.exp(scores - top_score)
    attn = (expo / jnp.sum(expo, axis=-1, keepdims=True)).astype(jnp.bfloat16)
    value_mult = jnp.einsum("hqk,qhd->khd", attn, mults, preferred_element_type=jnp.float32).astype(
        jnp.bfloat16
    )
    return lax.dot_general(
        value_mult.reshape(enc_len, HEADS * HEAD_DIM),
        w_value,
        (((1,), (1,)), ((), ())),
        preferred_element_type=jnp.float32,
    )


def expert_terms(rows_in, rows_base, rows_mult, part_in, part_out):
    pre_act = jnp.einsum("erd,edf->erf", rows_in, part_in, preferred_element_type=jnp.float32)
    base_act = jnp.einsum("erd,edf->erf", rows_base, part_in, preferred_element_type=jnp.float32)
    hidden_mult = jnp.einsum(
        "erd,edf->erf", rows_mult, part_out, preferred_element_type=jnp.float32
    )
    act_mult = (rescale(pre_act, base_act) * hidden_mult).astype(jnp.bfloat16)
    return jnp.einsum("erf,edf->erd", act_mult, part_in, preferred_element_type=jnp.float32)


def times_t(left, right):
    return lax.dot_general(left, right, (((1,), (1,)), ((), ())), preferred_element_type=jnp.float32)


def whole_kernel(
    n_peers,
    n_dp,
    cap,
    chunk,
    state_at,
    base_at,
    expert_at,
    place_at,
    gate_at,
    gain_at,
    length_at,
    keys_at,
    queries_at,
    mults_at,
    value_at,
    w_in,
    w_out,
    out,
    state,
    base_state,
    expert_row,
    place_row,
    gate,
    gain,
    length,
    keys,
    queries,
    mults,
    value,
    value_mult,
    layer,
    scale,
    sends,
    all_in,
    all_out,
    held,
    ratio,
    act,
    near_sum,
    far_sum,
    far_got,
    slot_sum,
    back,
    load_sem,
    weight_sem,
    swap_send,
    swap_recv,
    row_send,
    row_recv,
    hop_send,
    hop_recv,
    part_send,
    part_recv,
    back_send,
    back_recv,
):
    n_local = w_in.shape[0]
    tokens, width = state.shape
    rows = n_peers * cap
    half = n_peers // 2
    half_rows = half * cap
    n_chunks = width // chunk
    bf16, f32 = jnp.bfloat16, jnp.float32
    me = lax.axis_index("expert")
    dp = lax.axis_index("dp")
    pair = dp + 1 - 2 * lax.rem(dp, 2)
    across = lax.rem(dp + 2, n_dp)
    mesh_id = pl.DeviceIdType.MESH
    my_half = me // half
    inner = lax.rem(my_half + lax.rem(me // (half // 2), 2), 2)

    def peer_at(step):
        peer, bit = 0, 1
        while bit < n_peers:
            digit = lax.rem(me // bit, 2)
            flip = (step // bit) % 2
            peer = peer + bit * (digit + flip - 2 * digit * flip)
            bit *= 2
        return peer

    barrier = pltpu.get_barrier_semaphore()
    for step in range(1, n_peers):
        pl.semaphore_signal(barrier, inc=1, device_id={"expert": peer_at(step)}, device_id_type=mesh_id)
    for other in (pair, across):
        pl.semaphore_signal(barrier, inc=1, device_id={"dp": other}, device_id_type=mesh_id)

    def load(pairs, first_sem):
        copies = []
        for at, (ref, held_at) in enumerate(pairs):
            copy = pltpu.make_async_copy(ref, held_at, load_sem.at[first_sem + at])
            copy.start()
            copies.append(copy)
        return copies

    small = load(
        (
            (state_at, state),
            (gain_at, gain),
            (expert_at, expert_row),
            (place_at, place_row),
            (base_at, base_state),
            (gate_at, gate),
            (length_at, length),
        ),
        0,
    )
    loads = load(((queries_at, queries), (keys_at, keys), (mults_at, mults), (value_at, value)), len(small))
    own_weights = []
    for at, (ref, held_at) in enumerate(((w_in, all_in), (w_out, all_out))):
        copy = pltpu.make_async_copy(ref, held_at.at[0], weight_sem.at[at])
        copy.start()
        own_weights.append(copy)
    for copy in small[:4]:
        copy.wait()

    expert = expert_row[...]
    owner = lax.div(expert, n_local)
    slot_row = lax.rem(expert, n_local) * rows + owner * cap + place_row[...]

    def column(row):
        return jnp.transpose(jnp.broadcast_to(row, (128, tokens)))[:, :1]

    def place_rows(a, l, values):
        at = lax.broadcasted_iota(jnp.int32, (rows, tokens), 0) + l * rows
        onehot = jnp.where(at == slot_row, 1.0, 0.0).astype(bf16)
        sends[a, l] = jnp.dot(onehot, values, preferred_element_type=f32).astype(bf16)

    def block_of(src):
        return pl.ds(pl.multiple_of(src * cap, cap), cap)

    def near_block(src):
        return block_of(lax.rem(src, half))

    def far_block(src):
        return pl.ds(pl.multiple_of(half_rows + lax.rem(src, half) * cap, cap), cap)

    same, cross = 0, 1

    def arrival_of(a, l, step):
        at = a + 3 * l
        if step >= half:
            return at * half + step - half
        apart = 3 * n_local * half
        return apart + at if at or step == 1 else apart + 3 * n_local + step - 2

    def row_copy(a, l, step):
        peer = peer_at(step)
        kind = step // half
        return pltpu.make_async_remote_copy(
            src_ref=sends.at[a, l, block_of(peer), :],
            dst_ref=held.at[a, l, kind, near_block(me), :],
            send_sem=row_send.at[0],
            recv_sem=row_recv.at[arrival_of(a, l, step)],
            device_id={"expert": peer},
            device_id_type=mesh_id,
        )

    def keep_own(a, l):
        held[a, l, same, near_block(me), :] = sends[a, l, block_of(me), :]

    def hop_copy(a, l, kind, step):
        src = peer_at(step)
        return pltpu.make_async_remote_copy(
            src_ref=held.at[a, l, kind, near_block(src), :],
            dst_ref=held.at[a, l, kind, far_block(src), :],
            send_sem=hop_send.at[0],
            recv_sem=hop_recv.at[a, l, kind],
            device_id={"dp": across},
            device_id_type=mesh_id,
        )

    def own_hop(a, l):
        return pltpu.make_async_remote_copy(
            src_ref=sends.at[a, l, block_of(me), :],
            dst_ref=held.at[a, l, same, far_block(me), :],
            send_sem=hop_send.at[0],
            recv_sem=hop_recv.at[a, l, same],
            device_id={"dp": across},
            device_id_type=mesh_id,
        )

    def await_bytes(ref, sem):
        pltpu.make_async_copy(ref, ref, sem).wait()

    cross_steps = [*range(n_peers - 2, half - 1, -2), *range(n_peers - 1, half, -2)]
    first, later = cross_steps[: half // 2], cross_steps[half // 2 :]

    def send_same(a, l):
        for step in range(1, half):
            row_copy(a, l, step).start()

    def send_cross(a, l):
        for step in cross_steps:
            row_copy(a, l, step).start()

    order = [(a, l) for l in range(n_local) for a in range(3)]

    def next_cross(at):
        for ahead, mine in ((1, 0), (2, 1)):
            if at + ahead < len(order):

                @pl.when(inner == mine)
                def _():
                    send_cross(*order[at + ahead])

    def relay_same(a, l, steps=range(1, half)):
        if 1 in steps:
            await_bytes(held.at[a, l, same, pl.ds(0, (half - 1) * cap), :], row_recv.at[arrival_of(a, l, 1)])
        for step in steps:
            hop_copy(a, l, same, step).start()

    def relay(a, l, steps):
        for step in steps:
            kind = step // half
            await_bytes(held.at[a, l, kind, pl.ds(0, cap), :], row_recv.at[arrival_of(a, l, step)])
            hop_copy(a, l, kind, step).start()

    def wait_unit(a, l, kind):
        await_bytes(held.at[a, l, kind, pl.ds(half_rows, half_rows), :], hop_recv.at[a, l, kind])

    token_rows = state[...].astype(f32)
    scale[...] = gain[...] * lax.rsqrt(
        jnp.mean(token_rows * token_rows, axis=-1, keepdims=True) + 1e-06
    )
    inputs = (token_rows * scale[...]).astype(bf16)
    place_rows(0, 0, inputs)
    with jax.named_scope("barr"):
        pl.semaphore_wait(barrier, n_peers + 1)
    own_hop(0, 0).start()
    send_same(0, 0)
    send_cross(0, 0)
    small[4].wait()
    base_inputs = (base_state[...].astype(f32) * scale[...]).astype(bf16)
    place_rows(1, 0, base_inputs)
    own_hop(1, 0).start()
    send_same(1, 0)
    place_rows(0, 1, inputs)
    own_hop(0, 1).start()
    send_same(0, 1)

    @pl.when(inner == 1)
    def _():
        send_cross(1, 0)

    place_rows(1, 1, base_inputs)
    own_hop(1, 1).start()
    send_same(1, 1)
    for l in range(n_local):
        for a in range(2):
            keep_own(a, l)
    for copy in small[5:]:
        copy.wait()

    swaps = []
    for at, (ref, held_at) in enumerate(((w_in, all_in), (w_out, all_out))):
        swap = pltpu.make_async_remote_copy(
            src_ref=ref,
            dst_ref=held_at.at[1],
            send_sem=swap_send.at[at],
            recv_sem=swap_recv.at[at],
            device_id={"dp": pair},
            device_id_type=mesh_id,
        )
        swap.start()
        swaps.append(swap)

    for copy in loads:
        copy.wait()

    def two_heads(both):
        cols = pl.ds(pl.multiple_of(both * 2 * HEAD_DIM, 2 * HEAD_DIM), 2 * HEAD_DIM)
        query, key, mult = queries[:, cols], keys[:, cols], mults[:, cols]
        first_head = lax.broadcasted_iota(jnp.int32, query.shape, 1) < HEAD_DIM
        zero = jnp.zeros_like(query)
        found = []
        for head in range(2):
            mine = jnp.where(first_head, query, zero) if head == 0 else jnp.where(first_head, zero, query)
            scores = times_t(key, mine) * (1.0 / math.sqrt(HEAD_DIM))
            at = lax.broadcasted_iota(jnp.int32, scores.shape, 0)
            scores = jnp.where(at < length[...], scores, -jnp.inf)
            expo = jnp.exp(scores - jnp.max(scores, axis=0, keepdims=True))
            attn = (expo / jnp.sum(expo, axis=0, keepdims=True)).astype(bf16)
            found.append(jnp.dot(attn, mult, preferred_element_type=f32))
        left = lax.broadcasted_iota(jnp.int32, found[0].shape, 1) < HEAD_DIM
        value_mult[:, cols] = jnp.where(left, found[0], found[1]).astype(bf16)

    pieces = width // (2 * HEAD_DIM)
    with jax.named_scope("attn0"):
        pl.loop(0, pieces - 1)(two_heads)
    with jax.named_scope("r_s00"):
        relay(0, 0, range(1, half - 1))
    with jax.named_scope("attn1"):
        pl.loop(pieces - 1, pieces)(two_heads)

    def chunk_of(c):
        return pl.ds(pl.multiple_of(c * chunk, chunk), chunk)

    with jax.named_scope("layer"):

        @pl.loop(0, n_chunks)
        def _(c):
            layer[:, chunk_of(c)] = times_t(value_mult[...], value[chunk_of(c), :])

    with jax.named_scope("r_c00a"):
        relay(0, 0, first[:1])
    with jax.named_scope("r_s00b"):
        relay(0, 0, [half - 1])
    scaled = (column(gate[...]) * layer[...]).astype(bf16)
    for l in range(n_local):
        place_rows(2, l, scaled)
        keep_own(2, l)
        own_hop(2, l).start()
        send_same(2, l)

    def ratio_of(l, kind):
        @pl.loop(0, 2)
        def _(shard):
            weight = all_in[shard, l]
            pre = times_t(held[0, l, kind], weight)
            base = times_t(held[1, l, kind], weight)
            ratio[l, kind, shard] = rescale(pre, base)

    last = n_local - 1

    def part_copy(l, kind, c):
        return pltpu.make_async_remote_copy(
            src_ref=far_sum.at[l, kind, :, chunk_of(c)],
            dst_ref=far_got.at[l, kind, :, chunk_of(c)],
            send_sem=part_send.at[0],
            recv_sem=part_recv.at[kind if l < last else 2 + kind * n_chunks + c],
            device_id={"dp": across},
            device_id_type=mesh_id,
        )

    def sums_of(l, kind, then=None, once=None):
        @pl.loop(0, 2)
        def _(shard):
            hidden = times_t(held[2, l, kind], all_out[shard, l])
            act[shard] = (ratio[l, kind, shard] * hidden).astype(bf16)

        def sum_chunk(c):
            cols = chunk_of(c)
            total = jnp.dot(act[0], all_in[0, l, :, cols], preferred_element_type=f32) + jnp.dot(
                act[1], all_in[1, l, :, cols], preferred_element_type=f32
            )
            near_sum[l, kind, :, cols] = total[:half_rows]
            far_sum[l, kind, :, cols] = total[half_rows:].astype(bf16)
            part_copy(l, kind, c).start()

        if once is not None:
            sum_chunk(0)
            once()
        if then is None:
            pl.loop(0 if once is None else 1, n_chunks)(sum_chunk)
        else:

            @pl.loop(1, n_chunks)
            def _(c):
                sum_chunk(c - 1)
                then(c)

            sum_chunk(n_chunks - 1)

    def steps_of(kind):
        return range(1, half) if kind == same else range(half, n_peers)

    def back_copy(l, kind, c, step):
        peer = peer_at(step)
        return pltpu.make_async_remote_copy(
            src_ref=slot_sum.at[l, kind, near_block(peer), chunk_of(c)],
            dst_ref=back.at[kind, l, near_block(me), chunk_of(c)],
            send_sem=back_send.at[0],
            recv_sem=back_recv.at[kind, c],
            device_id={"expert": peer},
            device_id_type=mesh_id,
        )

    def back_chunk(l, kind, c):
        if l == last:
            part_copy(l, kind, c).wait_recv()
        cols = chunk_of(c)
        slot_sum[l, kind, :, cols] = (
            near_sum[l, kind, :, cols] + far_got[l, kind, :, cols].astype(f32)
        ).astype(bf16)
        for step in steps_of(kind)[::-1]:
            back_copy(l, kind, c, step).start()
        if kind == same:
            mine = near_block(me)
            back[same, l, mine, cols] = (
                near_sum[l, same, mine, cols] + far_got[l, same, mine, cols].astype(f32)
            ).astype(bf16)

    def send_back(l, kind, begin=0, end=n_chunks):
        if l < last and begin == 0:
            await_bytes(far_got.at[l, kind], part_recv.at[kind])
        pl.loop(begin, end)(functools.partial(back_chunk, l, kind))

    def scoped(name, call, *args):
        with jax.named_scope(name):
            call(*args)

    scoped("r_c00b", relay, 0, 0, first[1:])
    scoped("r_c00c", relay, 0, 0, later)
    next_cross(0)
    scoped("r_s10", relay_same, 1, 0)
    scoped("r_s01", relay_same, 0, 1)
    scoped("r_s11", relay_same, 1, 1)
    with jax.named_scope("weights"):
        for copy in own_weights:
            copy.wait()
        for swap in swaps:
            swap.wait_recv()
    scoped("w_s00", wait_unit, 0, 0, same)
    scoped("w_s10", wait_unit, 1, 0, same)
    scoped("ratio0s", ratio_of, 0, same)
    scoped("r_c10a", relay, 1, 0, first)
    scoped("r_c10b", relay, 1, 0, later)
    next_cross(1)
    scoped("r_s20", relay_same, 2, 0)
    scoped("r_c20a", relay, 2, 0, first)
    scoped("r_c20b", relay, 2, 0, later)
    next_cross(2)
    scoped("w_s20", wait_unit, 2, 0, same)
    scoped("sums0s", sums_of, 0, same)
    scoped("r_c01a", relay, 0, 1, first)
    scoped("w_c00", wait_unit, 0, 0, cross)
    scoped("w_c10", wait_unit, 1, 0, cross)
    scoped("ratio0c", ratio_of, 0, cross)
    scoped("r_c01b", relay, 0, 1, later)
    next_cross(3)
    scoped("w_c20", wait_unit, 2, 0, cross)
    scoped("sums0c", sums_of, 0, cross)
    scoped("w_s01", wait_unit, 0, 1, same)
    scoped("w_s11", wait_unit, 1, 1, same)
    scoped("ratio1s", ratio_of, 1, same)
    scoped("r_c11a", relay, 1, 1, first)
    scoped("r_c11b", relay, 1, 1, later)
    next_cross(4)
    scoped("back0s", send_back, 0, same)
    scoped("r_c21a", relay, 2, 1, first)
    scoped("back0c", send_back, 0, cross, 0, 1)
    scoped("r_c21b", relay, 2, 1, later)
    scoped("r_s21", relay_same, 2, 1, range(1, half - 1))
    scoped("back0c2", send_back, 0, cross, 1)
    scoped("w_c01", wait_unit, 0, 1, cross)
    scoped("w_c11", wait_unit, 1, 1, cross)
    scoped("ratio1c", ratio_of, 1, cross)
    scoped("w_c21", wait_unit, 2, 1, cross)
    scoped("sums1c", sums_of, 1, cross, None, functools.partial(relay_same, 2, 1, [half - 1]))
    scoped("back1c", back_chunk, 1, cross, 0)
    scoped("w_s21", wait_unit, 2, 1, same)
    scoped("sums1s", sums_of, 1, same, functools.partial(back_chunk, 1, cross))
    scoped("back1s", send_back, 1, same)

    group = owner // half
    other = group + my_half - 2 * group * my_half
    in_half = lax.rem(expert, n_local) * half_rows + lax.rem(owner, half) * cap + place_row[...]
    got_row = other * (n_local * half_rows) + in_half
    got_col = column(got_row.astype(f32))

    at = lax.broadcasted_iota(jnp.int32, (tokens, n_local * rows), 1)
    pick = jnp.where(at.astype(f32) == got_col, 1.0, 0.0).astype(bf16)

    def wait_back(kind, c):
        remote = len(steps_of(kind)) * cap
        await_bytes(back.at[kind, :, pl.ds(0, remote), chunk_of(c)], back_recv.at[kind, c])

    for c in range(n_chunks):
        cols = chunk_of(c)
        for kind in (cross, same):
            with jax.named_scope(f"w_{kind}{c}"):
                wait_back(kind, c)
        got = back[:, :, :, cols].reshape(n_local * rows, chunk)
        with jax.named_scope(f"pick{c}"):
            out[:, cols] = (
                layer[:, cols] + scale[:, cols] * jnp.dot(pick, got, preferred_element_type=f32)
            ).astype(bf16)

    with jax.named_scope("drain"):
        for swap in swaps:
            swap.wait_send()
        remote = (n_peers - 1) * cap
        await_bytes(sends.at[:, :, pl.ds(0, remote), :], row_send.at[0])
        await_bytes(sends, hop_send.at[0])
        await_bytes(far_sum, part_send.at[0])
        await_bytes(sends.at[0, :, pl.ds(0, remote), :], back_send.at[0])


def whole_pass(
    state, base_state, keys, queries, mults, length, expert, place, gate, gain, w_in, w_out_t, value, n_peers, n_dp, cap
):
    tokens, width = state.shape
    n_local, _, part = w_in.shape
    w_in, w_out_t = jnp.swapaxes(w_in, 1, 2), jnp.swapaxes(w_out_t, 1, 2)
    rows = n_peers * cap
    half_rows = rows // 2
    chunk = width // 4
    n_chunks = width // chunk
    bf16, f32 = jnp.bfloat16, jnp.float32
    dma = pltpu.SemaphoreType.DMA
    vmem = pl.BlockSpec(memory_space=pltpu.VMEM)
    anyw = pl.BlockSpec(memory_space=pl.ANY)
    halves = (n_local, 2, half_rows, width)
    return pl.pallas_call(
        functools.partial(whole_kernel, n_peers, n_dp, cap, chunk),
        out_shape=pltpu.VMEM((tokens, width), bf16),
        in_specs=[anyw] * 13,
        out_specs=vmem,
        scratch_shapes=[
            pltpu.VMEM(state.shape, bf16),
            pltpu.VMEM(base_state.shape, bf16),
            pltpu.VMEM(expert.shape, expert.dtype),
            pltpu.VMEM(place.shape, place.dtype),
            pltpu.VMEM(gate.shape, f32),
            pltpu.VMEM((1, width), f32),
            pltpu.VMEM(length.shape, length.dtype),
            pltpu.VMEM(keys.shape, bf16),
            pltpu.VMEM(queries.shape, bf16),
            pltpu.VMEM(mults.shape, bf16),
            pltpu.VMEM(value.shape, bf16),
            pltpu.VMEM((tokens, width), bf16),
            pltpu.VMEM((tokens, width), f32),
            pltpu.VMEM((tokens, width), f32),
            pltpu.VMEM((3, n_local, rows, width), bf16),
            pltpu.VMEM((2, n_local, part, width), bf16),
            pltpu.VMEM((2, n_local, part, width), bf16),
            pltpu.VMEM((3, n_local, 2, 2 * half_rows, width), bf16),
            pltpu.VMEM((n_local, 2, 2, 2 * half_rows, part), f32),
            pltpu.VMEM((2, 2 * half_rows, part), bf16),
            pltpu.VMEM(halves, f32),
            pltpu.VMEM(halves, bf16),
            pltpu.VMEM(halves, bf16),
            pltpu.VMEM(halves, bf16),
            pltpu.VMEM((2, n_local, half_rows, width), bf16),
            dma((11,)),
            dma((2,)),
            dma((2,)),
            dma((2,)),
            dma((1,)),
            dma((3 * n_local * (n_peers // 2 + 1) + n_peers // 2 - 2,)),
            dma((1,)),
            dma((3, n_local, 2)),
            dma((1,)),
            dma((2 + 2 * n_chunks,)),
            dma((1,)),
            dma((2, n_chunks)),
        ],
        compiler_params=pltpu.CompilerParams(
            collective_id=0, has_side_effects=True, vmem_limit_bytes=60 * 1024 * 1024
        ),
        name="whole_pass",
    )(
        state,
        base_state,
        expert,
        place,
        gate,
        gain[None, :],
        length,
        keys,
        queries,
        mults,
        value,
        w_in,
        w_out_t,
    )


def plain_pass(sent, w_in, w_out_t, n_peers, n_dp):
    near = 2 if n_dp % 2 == 0 else 1
    shards = [(w_in, w_out_t)]
    if near == 2:
        swap = [(i, i ^ 1) for i in range(n_dp)]
        shards.append((lax.ppermute(w_in, "dp", swap), lax.ppermute(w_out_t, "dp", swap)))
    own_rows = tuple(
        lax.all_to_all(a, "expert", split_axis=0, concat_axis=1, tiled=True) for a in sent
    )

    def partial_sum(rows):
        total = expert_terms(*rows, *shards[0])
        for part in shards[1:]:
            total = total + expert_terms(*rows, *part)
        return total

    far = n_dp // near
    far_rows = []
    for hop in range(1, far):
        ahead = [(i, (i + hop * near) % n_dp) for i in range(n_dp)]
        far_rows.append(tuple(lax.ppermute(a, "dp", ahead) for a in own_rows))
    slot_mult = partial_sum(own_rows)
    for hop in range(1, far):
        back = [((i + hop * near) % n_dp, i) for i in range(n_dp)]
        far_part = partial_sum(far_rows[hop - 1]).astype(jnp.bfloat16)
        slot_mult = slot_mult + lax.ppermute(far_part, "dp", back).astype(jnp.float32)

    return lax.all_to_all(
        slot_mult.astype(jnp.bfloat16), "expert", split_axis=1, concat_axis=0, tiled=True
    )


def body(
    enc_state,
    baseline,
    enc_keys,
    dec_queries,
    out_mult,
    doc_lengths,
    expert_ids,
    slot_ids,
    gate_prob,
    norm_gain,
    w_in,
    w_out_t,
    w_value,
):
    enc_len = enc_state.shape[2]
    feature_width = enc_state.shape[3]
    local_experts = w_in.shape[0]
    n_experts = local_experts * lax.axis_size("expert")
    n_dp = lax.axis_size("dp")
    capacity = max(2, 2 * enc_len // n_experts)

    n_peers = lax.axis_size("expert")
    if n_dp == 4 and local_experts == 2 and capacity % 16 == 0 and n_peers >= 4 and n_peers & (n_peers - 1) == 0 and feature_width % 512 == 0:
        return whole_pass(
            enc_state[0, 0],
            baseline[0, 0],
            enc_keys[0, 0],
            dec_queries[0, 0],
            out_mult[0, 0],
            doc_lengths,
            expert_ids[0],
            slot_ids[0],
            gate_prob[0],
            norm_gain,
            w_in,
            w_out_t,
            w_value,
            n_peers,
            n_dp,
            capacity,
        )[None, None]

    tokens = enc_state[0, 0].astype(jnp.float32)
    row_scale = norm_gain * lax.rsqrt(jnp.mean(tokens * tokens, axis=-1, keepdims=True) + 1e-06)
    inputs = (tokens * row_scale).astype(jnp.bfloat16)
    base_inputs = (baseline[0, 0].astype(jnp.float32) * row_scale).astype(jnp.bfloat16)
    flat_slot = expert_ids[0, 0] * capacity + slot_ids[0, 0]
    onehot = (
        flat_slot[None, :] == jnp.arange(n_experts * capacity, dtype=jnp.int32)[:, None]
    ).astype(jnp.bfloat16)

    def dispatch(values):
        placed = jnp.dot(onehot, values, preferred_element_type=jnp.float32).astype(jnp.bfloat16)
        return placed.reshape(n_experts, capacity, feature_width)

    layer_mult = attend(
        dec_queries[0, 0], enc_keys[0, 0], out_mult[0, 0], doc_lengths[0, 0], w_value
    )
    scaled_mult = (gate_prob[0, 0][:, None] * layer_mult).astype(jnp.bfloat16)
    sent = (dispatch(inputs), dispatch(base_inputs), dispatch(scaled_mult))
    returned = plain_pass(sent, w_in, w_out_t, n_peers, n_dp)
    per_token = lax.dot_general(
        onehot,
        returned.reshape(n_experts * capacity, feature_width),
        (((0,), (0,)), ((), ())),
        preferred_element_type=jnp.float32,
    )
    result = (layer_mult + row_scale * per_token).astype(jnp.bfloat16)
    return result[None, None]


def solution(mesh):
    in_specs = (
        P("dp", "expert", None, None),
        P("dp", "expert", None, None),
        P("dp", "expert", None, None),
        P("dp", "expert", None, None),
        P("dp", "expert", None, None),
        P("dp", "expert"),
        P("dp", "expert", None),
        P("dp", "expert", None),
        P("dp", "expert", None),
        P(),
        P("expert", None, "dp"),
        P("expert", None, "dp"),
        P(),
    )
    out_specs = P("dp", "expert", None, None)
    return jax.shard_map(body, mesh=mesh, in_specs=in_specs, out_specs=out_specs, check_vma=False)
```

```python
import functools
import math

import jax
import jax.numpy as jnp
from jax import lax
from jax.experimental import pallas as pl
from jax.experimental.pallas import tpu as pltpu
from jax.sharding import PartitionSpec as P

HEADS = 16
HEAD_DIM = 64


def rescale(pre_act, base_act):
    upper_part = jnp.maximum(jnp.maximum(pre_act, base_act), 0.0)
    lower_part = jnp.maximum(-jnp.minimum(pre_act, base_act), 0.0)
    return upper_part / (upper_part + lower_part + jnp.where(upper_part > 0.0, 0.0, 1.0))


def attend(query_rows, key_rows, mult_rows, length, w_value):
    enc_len = key_rows.shape[0]
    dec_len = query_rows.shape[0]
    queries = query_rows.reshape(dec_len, HEADS, HEAD_DIM)
    keys = key_rows.reshape(enc_len, HEADS, HEAD_DIM)
    mults = mult_rows.reshape(dec_len, HEADS, HEAD_DIM)
    scores = jnp.einsum("qhd,khd->hqk", queries, keys, preferred_element_type=jnp.float32) * (
        1.0 / math.sqrt(HEAD_DIM)
    )
    valid = jnp.arange(enc_len, dtype=jnp.int32) < length
    scores = jnp.where(valid[None, None, :], scores, -jnp.inf)
    top_score = jnp.max(scores, axis=-1, keepdims=True)
    expo = jnp.exp(scores - top_score)
    attn = (expo / jnp.sum(expo, axis=-1, keepdims=True)).astype(jnp.bfloat16)
    value_mult = jnp.einsum("hqk,qhd->khd", attn, mults, preferred_element_type=jnp.float32).astype(
        jnp.bfloat16
    )
    return lax.dot_general(
        value_mult.reshape(enc_len, HEADS * HEAD_DIM),
        w_value,
        (((1,), (1,)), ((), ())),
        preferred_element_type=jnp.float32,
    )


def expert_terms(rows_in, rows_base, rows_mult, part_in, part_out):
    pre_act = jnp.einsum("erd,edf->erf", rows_in, part_in, preferred_element_type=jnp.float32)
    base_act = jnp.einsum("erd,edf->erf", rows_base, part_in, preferred_element_type=jnp.float32)
    hidden_mult = jnp.einsum(
        "erd,edf->erf", rows_mult, part_out, preferred_element_type=jnp.float32
    )
    act_mult = (rescale(pre_act, base_act) * hidden_mult).astype(jnp.bfloat16)
    return jnp.einsum("erf,edf->erd", act_mult, part_in, preferred_element_type=jnp.float32)


def times_t(left, right):
    return lax.dot_general(left, right, (((1,), (1,)), ((), ())), preferred_element_type=jnp.float32)


def whole_kernel(
    n_peers,
    n_dp,
    cap,
    chunk,
    state_at,
    base_at,
    expert_at,
    place_at,
    gate_at,
    gain_at,
    length_at,
    keys_at,
    queries_at,
    mults_at,
    value_at,
    w_in,
    w_out,
    out,
    state,
    base_state,
    expert_row,
    place_row,
    gate,
    gain,
    length,
    keys,
    queries,
    mults,
    value,
    value_mult,
    layer,
    scale,
    sends,
    all_in,
    all_out,
    held,
    ratio,
    act,
    near_sum,
    far_sum,
    far_got,
    slot_sum,
    back,
    load_sem,
    weight_sem,
    swap_send,
    swap_recv,
    row_send,
    row_recv,
    hop_send,
    hop_recv,
    part_send,
    part_recv,
    back_send,
    back_recv,
):
    n_local = w_in.shape[0]
    tokens, width = state.shape
    rows = n_peers * cap
    half = n_peers // 2
    half_rows = half * cap
    n_chunks = width // chunk
    bf16, f32 = jnp.bfloat16, jnp.float32
    me = lax.axis_index("expert")
    dp = lax.axis_index("dp")
    pair = dp + 1 - 2 * lax.rem(dp, 2)
    across = lax.rem(dp + 2, n_dp)
    mesh_id = pl.DeviceIdType.MESH
    my_half = me // half
    inner = lax.rem(my_half + lax.rem(me // (half // 2), 2), 2)

    def peer_at(step):
        peer, bit = 0, 1
        while bit < n_peers:
            digit = lax.rem(me // bit, 2)
            flip = (step // bit) % 2
            peer = peer + bit * (digit + flip - 2 * digit * flip)
            bit *= 2
        return peer

    barrier = pltpu.get_barrier_semaphore()
    for step in range(1, n_peers):
        pl.semaphore_signal(barrier, inc=1, device_id={"expert": peer_at(step)}, device_id_type=mesh_id)
    for other in (pair, across):
        pl.semaphore_signal(barrier, inc=1, device_id={"dp": other}, device_id_type=mesh_id)

    def load(pairs, first_sem):
        copies = []
        for at, (ref, held_at) in enumerate(pairs):
            if at + first_sem == 0:
                quarter = tokens // 4
                for part in range(4):
                    some = pl.ds(part * quarter, quarter)
                    pltpu.make_async_copy(ref.at[some], held_at.at[some], load_sem.at[0]).start()
                copies.append(pltpu.make_async_copy(ref, held_at, load_sem.at[0]))
                continue
            copy = pltpu.make_async_copy(ref, held_at, load_sem.at[first_sem + at])
            copy.start()
            copies.append(copy)
        return copies

    small = load(
        (
            (state_at, state),
            (gain_at, gain),
            (expert_at, expert_row),
            (place_at, place_row),
            (base_at, base_state),
            (gate_at, gate),
            (length_at, length),
        ),
        0,
    )
    loads = load(((queries_at, queries), (keys_at, keys), (mults_at, mults), (value_at, value)), len(small))
    own_weights = []
    for at, (ref, held_at) in enumerate(((w_in, all_in), (w_out, all_out))):
        copy = pltpu.make_async_copy(ref, held_at.at[0], weight_sem.at[at])
        copy.start()
        own_weights.append(copy)
    for copy in small[:4]:
        copy.wait()

    expert = expert_row[...]
    owner = lax.div(expert, n_local)
    slot_row = lax.rem(expert, n_local) * rows + owner * cap + place_row[...]

    def column(row):
        return jnp.transpose(jnp.broadcast_to(row, (128, tokens)))[:, :1]

    def place_rows(a, l, values):
        at = lax.broadcasted_iota(jnp.int32, (rows, tokens), 0) + l * rows
        onehot = jnp.where(at == slot_row, 1.0, 0.0).astype(bf16)
        sends[a, l] = jnp.dot(onehot, values, preferred_element_type=f32).astype(bf16)

    def block_of(src):
        return pl.ds(pl.multiple_of(src * cap, cap), cap)

    def near_block(src):
        return block_of(lax.rem(src, half))

    def far_block(src):
        return pl.ds(pl.multiple_of(half_rows + lax.rem(src, half) * cap, cap), cap)

    same, cross = 0, 1

    def arrival_of(a, l, step):
        at = a + 3 * l
        if step >= half:
            return at * half + step - half
        apart = 3 * n_local * half
        return apart + at if at or step == 1 else apart + 3 * n_local + step - 2

    def row_copy(a, l, step):
        peer = peer_at(step)
        kind = step // half
        return pltpu.make_async_remote_copy(
            src_ref=sends.at[a, l, block_of(peer), :],
            dst_ref=held.at[a, l, kind, near_block(me), :],
            send_sem=row_send.at[0],
            recv_sem=row_recv.at[arrival_of(a, l, step)],
            device_id={"expert": peer},
            device_id_type=mesh_id,
        )

    def keep_own(a, l):
        held[a, l, same, near_block(me), :] = sends[a, l, block_of(me), :]

    def hop_copy(a, l, kind, step):
        src = peer_at(step)
        return pltpu.make_async_remote_copy(
            src_ref=held.at[a, l, kind, near_block(src), :],
            dst_ref=held.at[a, l, kind, far_block(src), :],
            send_sem=hop_send.at[0],
            recv_sem=hop_recv.at[a, l, kind],
            device_id={"dp": across},
            device_id_type=mesh_id,
        )

    def own_hop(a, l):
        return pltpu.make_async_remote_copy(
            src_ref=sends.at[a, l, block_of(me), :],
            dst_ref=held.at[a, l, same, far_block(me), :],
            send_sem=hop_send.at[0],
            recv_sem=hop_recv.at[a, l, same],
            device_id={"dp": across},
            device_id_type=mesh_id,
        )

    def await_bytes(ref, sem):
        pltpu.make_async_copy(ref, ref, sem).wait()

    cross_steps = [*range(n_peers - 2, half - 1, -2), *range(n_peers - 1, half, -2)]
    first, later = cross_steps[: half // 2], cross_steps[half // 2 :]

    def send_same(a, l):
        for step in range(1, half):
            row_copy(a, l, step).start()

    def send_cross(a, l):
        for step in cross_steps:
            row_copy(a, l, step).start()

    order = [(a, l) for l in range(n_local) for a in range(3)]

    def next_cross(at):
        for ahead, mine in ((1, 0), (2, 1)):
            if at + ahead < len(order):

                @pl.when(inner == mine)
                def _():
                    send_cross(*order[at + ahead])

    def relay_same(a, l, steps=range(1, half)):
        if 1 in steps:
            await_bytes(held.at[a, l, same, pl.ds(0, (half - 1) * cap), :], row_recv.at[arrival_of(a, l, 1)])
        for step in steps:
            hop_copy(a, l, same, step).start()

    def relay(a, l, steps):
        for step in steps:
            kind = step // half
            await_bytes(held.at[a, l, kind, pl.ds(0, cap), :], row_recv.at[arrival_of(a, l, step)])
            hop_copy(a, l, kind, step).start()

    def wait_unit(a, l, kind):
        await_bytes(held.at[a, l, kind, pl.ds(half_rows, half_rows), :], hop_recv.at[a, l, kind])

    token_rows = state[...].astype(f32)
    scale[...] = gain[...] * lax.rsqrt(
        jnp.mean(token_rows * token_rows, axis=-1, keepdims=True) + 1e-06
    )
    inputs = (token_rows * scale[...]).astype(bf16)
    place_rows(0, 0, inputs)
    with jax.named_scope("barr"):
        pl.semaphore_wait(barrier, n_peers + 1)
    own_hop(0, 0).start()
    send_same(0, 0)
    send_cross(0, 0)
    small[4].wait()
    base_inputs = (base_state[...].astype(f32) * scale[...]).astype(bf16)
    place_rows(1, 0, base_inputs)
    own_hop(1, 0).start()
    send_same(1, 0)
    place_rows(0, 1, inputs)
    own_hop(0, 1).start()
    place_rows(1, 1, base_inputs)
    own_hop(1, 1).start()
    for l in range(n_local):
        for a in range(2):
            keep_own(a, l)
    for copy in small[5:]:
        copy.wait()

    swaps = []
    for at, (ref, held_at) in enumerate(((w_in, all_in), (w_out, all_out))):
        swap = pltpu.make_async_remote_copy(
            src_ref=ref,
            dst_ref=held_at.at[1],
            send_sem=swap_send.at[at],
            recv_sem=swap_recv.at[at],
            device_id={"dp": pair},
            device_id_type=mesh_id,
        )
        swap.start()
        swaps.append(swap)

    for copy in loads:
        copy.wait()

    def two_heads(both):
        cols = pl.ds(pl.multiple_of(both * 2 * HEAD_DIM, 2 * HEAD_DIM), 2 * HEAD_DIM)
        query, key, mult = queries[:, cols], keys[:, cols], mults[:, cols]
        first_head = lax.broadcasted_iota(jnp.int32, query.shape, 1) < HEAD_DIM
        zero = jnp.zeros_like(query)
        found = []
        for head in range(2):
            mine = jnp.where(first_head, query, zero) if head == 0 else jnp.where(first_head, zero, query)
            scores = times_t(key, mine) * (1.0 / math.sqrt(HEAD_DIM))
            at = lax.broadcasted_iota(jnp.int32, scores.shape, 0)
            scores = jnp.where(at < length[...], scores, -jnp.inf)
            expo = jnp.exp(scores - jnp.max(scores, axis=0, keepdims=True))
            attn = (expo / jnp.sum(expo, axis=0, keepdims=True)).astype(bf16)
            found.append(jnp.dot(attn, mult, preferred_element_type=f32))
        left = lax.broadcasted_iota(jnp.int32, found[0].shape, 1) < HEAD_DIM
        value_mult[:, cols] = jnp.where(left, found[0], found[1]).astype(bf16)

    pieces = width // (2 * HEAD_DIM)
    with jax.named_scope("attn0"):
        pl.loop(0, pieces - 2)(two_heads)
    with jax.named_scope("r_s00"):
        relay(0, 0, range(1, half - 1))
    send_same(0, 1)

    @pl.when(inner == 1)
    def _():
        send_cross(1, 0)

    with jax.named_scope("attn1"):
        pl.loop(pieces - 2, pieces)(two_heads)

    def chunk_of(c):
        return pl.ds(pl.multiple_of(c * chunk, chunk), chunk)

    with jax.named_scope("layer"):

        @pl.loop(0, n_chunks)
        def _(c):
            layer[:, chunk_of(c)] = times_t(value_mult[...], value[chunk_of(c), :])

    with jax.named_scope("r_c00a"):
        relay(0, 0, first[:1])
    send_same(1, 1)
    scaled = (column(gate[...]) * layer[...]).astype(bf16)
    for l in range(n_local):
        place_rows(2, l, scaled)
        keep_own(2, l)
        own_hop(2, l).start()
        send_same(2, l)

    def ratio_of(l, kind):
        @pl.loop(0, 2)
        def _(shard):
            weight = all_in[shard, l]
            pre = times_t(held[0, l, kind], weight)
            base = times_t(held[1, l, kind], weight)
            ratio[l, kind, shard] = rescale(pre, base)

    last = n_local - 1

    def part_copy(l, kind, c):
        return pltpu.make_async_remote_copy(
            src_ref=far_sum.at[l, kind, :, chunk_of(c)],
            dst_ref=far_got.at[l, kind, :, chunk_of(c)],
            send_sem=part_send.at[0],
            recv_sem=part_recv.at[kind if l < last else 2 + kind * n_chunks + c],
            device_id={"dp": across},
            device_id_type=mesh_id,
        )

    def sums_of(l, kind, then=None, once=None):
        @pl.loop(0, 2)
        def _(shard):
            hidden = times_t(held[2, l, kind], all_out[shard, l])
            act[shard] = (ratio[l, kind, shard] * hidden).astype(bf16)

        def sum_chunk(c):
            cols = chunk_of(c)
            total = jnp.dot(act[0], all_in[0, l, :, cols], preferred_element_type=f32) + jnp.dot(
                act[1], all_in[1, l, :, cols], preferred_element_type=f32
            )
            near_sum[l, kind, :, cols] = total[:half_rows]
            far_sum[l, kind, :, cols] = total[half_rows:].astype(bf16)
            part_copy(l, kind, c).start()

        if once is not None:
            sum_chunk(0)
            once()
        if then is None:
            pl.loop(0 if once is None else 1, n_chunks)(sum_chunk)
        else:

            @pl.loop(1, n_chunks)
            def _(c):
                sum_chunk(c - 1)
                then(c)

            sum_chunk(n_chunks - 1)

    def steps_of(kind):
        return range(1, half) if kind == same else range(half, n_peers)

    def back_copy(l, kind, c, step):
        peer = peer_at(step)
        return pltpu.make_async_remote_copy(
            src_ref=slot_sum.at[l, kind, near_block(peer), chunk_of(c)],
            dst_ref=back.at[kind, l, near_block(me), chunk_of(c)],
            send_sem=back_send.at[0],
            recv_sem=back_recv.at[kind, c],
            device_id={"expert": peer},
            device_id_type=mesh_id,
        )

    def back_chunk(l, kind, c):
        if l == last:
            part_copy(l, kind, c).wait_recv()
        cols = chunk_of(c)
        slot_sum[l, kind, :, cols] = (
            near_sum[l, kind, :, cols] + far_got[l, kind, :, cols].astype(f32)
        ).astype(bf16)
        for step in steps_of(kind)[::-1]:
            back_copy(l, kind, c, step).start()
        if kind == same:
            mine = near_block(me)
            back[same, l, mine, cols] = (
                near_sum[l, same, mine, cols] + far_got[l, same, mine, cols].astype(f32)
            ).astype(bf16)

    def send_back(l, kind, begin=0, end=n_chunks):
        if l < last and begin == 0:
            await_bytes(far_got.at[l, kind], part_recv.at[kind])
        pl.loop(begin, end)(functools.partial(back_chunk, l, kind))

    def scoped(name, call, *args):
        with jax.named_scope(name):
            call(*args)

    scoped("r_s00b", relay, 0, 0, [half - 1])
    scoped("r_c00b", relay, 0, 0, first[1:])
    scoped("r_c00c", relay, 0, 0, later)
    next_cross(0)
    scoped("r_s10", relay_same, 1, 0)
    scoped("r_s01", relay_same, 0, 1)
    scoped("r_s11", relay_same, 1, 1)
    with jax.named_scope("weights"):
        for copy in own_weights:
            copy.wait()
        for swap in swaps:
            swap.wait_recv()
    scoped("w_s00", wait_unit, 0, 0, same)
    scoped("w_s10", wait_unit, 1, 0, same)
    scoped("ratio0s", ratio_of, 0, same)
    scoped("r_c10a", relay, 1, 0, first)
    scoped("r_c10b", relay, 1, 0, later)
    next_cross(1)
    scoped("r_s20", relay_same, 2, 0)
    scoped("r_c20a", relay, 2, 0, first)
    scoped("r_c20b", relay, 2, 0, later)
    next_cross(2)
    scoped("w_s20", wait_unit, 2, 0, same)
    scoped("sums0s", sums_of, 0, same)
    scoped("r_c01a", relay, 0, 1, first)
    scoped("w_c00", wait_unit, 0, 0, cross)
    scoped("w_c10", wait_unit, 1, 0, cross)
    scoped("ratio0c", ratio_of, 0, cross)
    scoped("r_c01b", relay, 0, 1, later)
    next_cross(3)
    scoped("w_c20", wait_unit, 2, 0, cross)
    scoped("sums0c", sums_of, 0, cross)
    scoped("w_s01", wait_unit, 0, 1, same)
    scoped("w_s11", wait_unit, 1, 1, same)
    scoped("ratio1s", ratio_of, 1, same)
    scoped("r_c11a", relay, 1, 1, first)
    scoped("r_c11b", relay, 1, 1, later)
    next_cross(4)
    scoped("back0s", send_back, 0, same)
    scoped("r_c21a", relay, 2, 1, first)
    scoped("back0c", send_back, 0, cross, 0, 1)
    scoped("r_c21b", relay, 2, 1, later)
    scoped("r_s21", relay_same, 2, 1, range(1, half - 1))
    scoped("back0c2", send_back, 0, cross, 1)
    scoped("w_c01", wait_unit, 0, 1, cross)
    scoped("w_c11", wait_unit, 1, 1, cross)
    scoped("ratio1c", ratio_of, 1, cross)
    scoped("w_c21", wait_unit, 2, 1, cross)
    scoped("sums1c", sums_of, 1, cross, None, functools.partial(relay_same, 2, 1, [half - 1]))
    scoped("back1c", back_chunk, 1, cross, 0)
    scoped("w_s21", wait_unit, 2, 1, same)
    scoped("sums1s", sums_of, 1, same, functools.partial(back_chunk, 1, cross))
    scoped("back1s", send_back, 1, same)

    group = owner // half
    other = group + my_half - 2 * group * my_half
    in_half = lax.rem(expert, n_local) * half_rows + lax.rem(owner, half) * cap + place_row[...]
    got_row = other * (n_local * half_rows) + in_half
    got_col = column(got_row.astype(f32))

    at = lax.broadcasted_iota(jnp.int32, (tokens, n_local * rows), 1)
    pick = jnp.where(at.astype(f32) == got_col, 1.0, 0.0).astype(bf16)

    def wait_back(kind, c):
        remote = len(steps_of(kind)) * cap
        await_bytes(back.at[kind, :, pl.ds(0, remote), chunk_of(c)], back_recv.at[kind, c])

    for c in range(n_chunks):
        cols = chunk_of(c)
        for kind in (cross, same):
            with jax.named_scope(f"w_{kind}{c}"):
                wait_back(kind, c)
        got = back[:, :, :, cols].reshape(n_local * rows, chunk)
        with jax.named_scope(f"pick{c}"):
            out[:, cols] = (
                layer[:, cols] + scale[:, cols] * jnp.dot(pick, got, preferred_element_type=f32)
            ).astype(bf16)

    with jax.named_scope("drain"):
        for swap in swaps:
            swap.wait_send()
        remote = (n_peers - 1) * cap
        await_bytes(sends.at[:, :, pl.ds(0, remote), :], row_send.at[0])
        await_bytes(sends, hop_send.at[0])
        await_bytes(far_sum, part_send.at[0])
        await_bytes(sends.at[0, :, pl.ds(0, remote), :], back_send.at[0])


def whole_pass(
    state, base_state, keys, queries, mults, length, expert, place, gate, gain, w_in, w_out_t, value, n_peers, n_dp, cap
):
    tokens, width = state.shape
    n_local, _, part = w_in.shape
    w_in, w_out_t = jnp.swapaxes(w_in, 1, 2), jnp.swapaxes(w_out_t, 1, 2)
    rows = n_peers * cap
    half_rows = rows // 2
    chunk = width // 4
    n_chunks = width // chunk
    bf16, f32 = jnp.bfloat16, jnp.float32
    dma = pltpu.SemaphoreType.DMA
    vmem = pl.BlockSpec(memory_space=pltpu.VMEM)
    anyw = pl.BlockSpec(memory_space=pl.ANY)
    halves = (n_local, 2, half_rows, width)
    return pl.pallas_call(
        functools.partial(whole_kernel, n_peers, n_dp, cap, chunk),
        out_shape=pltpu.VMEM((tokens, width), bf16),
        in_specs=[anyw] * 13,
        out_specs=vmem,
        scratch_shapes=[
            pltpu.VMEM(state.shape, bf16),
            pltpu.VMEM(base_state.shape, bf16),
            pltpu.VMEM(expert.shape, expert.dtype),
            pltpu.VMEM(place.shape, place.dtype),
            pltpu.VMEM(gate.shape, f32),
            pltpu.VMEM((1, width), f32),
            pltpu.VMEM(length.shape, length.dtype),
            pltpu.VMEM(keys.shape, bf16),
            pltpu.VMEM(queries.shape, bf16),
            pltpu.VMEM(mults.shape, bf16),
            pltpu.VMEM(value.shape, bf16),
            pltpu.VMEM((tokens, width), bf16),
            pltpu.VMEM((tokens, width), f32),
            pltpu.VMEM((tokens, width), f32),
            pltpu.VMEM((3, n_local, rows, width), bf16),
            pltpu.VMEM((2, n_local, part, width), bf16),
            pltpu.VMEM((2, n_local, part, width), bf16),
            pltpu.VMEM((3, n_local, 2, 2 * half_rows, width), bf16),
            pltpu.VMEM((n_local, 2, 2, 2 * half_rows, part), f32),
            pltpu.VMEM((2, 2 * half_rows, part), bf16),
            pltpu.VMEM(halves, f32),
            pltpu.VMEM(halves, bf16),
            pltpu.VMEM(halves, bf16),
            pltpu.VMEM(halves, bf16),
            pltpu.VMEM((2, n_local, half_rows, width), bf16),
            dma((11,)),
            dma((2,)),
            dma((2,)),
            dma((2,)),
            dma((1,)),
            dma((3 * n_local * (n_peers // 2 + 1) + n_peers // 2 - 2,)),
            dma((1,)),
            dma((3, n_local, 2)),
            dma((1,)),
            dma((2 + 2 * n_chunks,)),
            dma((1,)),
            dma((2, n_chunks)),
        ],
        compiler_params=pltpu.CompilerParams(
            collective_id=0, has_side_effects=True, vmem_limit_bytes=60 * 1024 * 1024
        ),
        name="whole_pass",
    )(
        state,
        base_state,
        expert,
        place,
        gate,
        gain[None, :],
        length,
        keys,
        queries,
        mults,
        value,
        w_in,
        w_out_t,
    )


def plain_pass(sent, w_in, w_out_t, n_peers, n_dp):
    near = 2 if n_dp % 2 == 0 else 1
    shards = [(w_in, w_out_t)]
    if near == 2:
        swap = [(i, i ^ 1) for i in range(n_dp)]
        shards.append((lax.ppermute(w_in, "dp", swap), lax.ppermute(w_out_t, "dp", swap)))
    own_rows = tuple(
        lax.all_to_all(a, "expert", split_axis=0, concat_axis=1, tiled=True) for a in sent
    )

    def partial_sum(rows):
        total = expert_terms(*rows, *shards[0])
        for part in shards[1:]:
            total = total + expert_terms(*rows, *part)
        return total

    far = n_dp // near
    far_rows = []
    for hop in range(1, far):
        ahead = [(i, (i + hop * near) % n_dp) for i in range(n_dp)]
        far_rows.append(tuple(lax.ppermute(a, "dp", ahead) for a in own_rows))
    slot_mult = partial_sum(own_rows)
    for hop in range(1, far):
        back = [((i + hop * near) % n_dp, i) for i in range(n_dp)]
        far_part = partial_sum(far_rows[hop - 1]).astype(jnp.bfloat16)
        slot_mult = slot_mult + lax.ppermute(far_part, "dp", back).astype(jnp.float32)

    return lax.all_to_all(
        slot_mult.astype(jnp.bfloat16), "expert", split_axis=1, concat_axis=0, tiled=True
    )


def body(
    enc_state,
    baseline,
    enc_keys,
    dec_queries,
    out_mult,
    doc_lengths,
    expert_ids,
    slot_ids,
    gate_prob,
    norm_gain,
    w_in,
    w_out_t,
    w_value,
):
    enc_len = enc_state.shape[2]
    feature_width = enc_state.shape[3]
    local_experts = w_in.shape[0]
    n_experts = local_experts * lax.axis_size("expert")
    n_dp = lax.axis_size("dp")
    capacity = max(2, 2 * enc_len // n_experts)

    n_peers = lax.axis_size("expert")
    if n_dp == 4 and local_experts == 2 and capacity % 16 == 0 and n_peers >= 4 and n_peers & (n_peers - 1) == 0 and feature_width % 512 == 0:
        return whole_pass(
            enc_state[0, 0],
            baseline[0, 0],
            enc_keys[0, 0],
            dec_queries[0, 0],
            out_mult[0, 0],
            doc_lengths,
            expert_ids[0],
            slot_ids[0],
            gate_prob[0],
            norm_gain,
            w_in,
            w_out_t,
            w_value,
            n_peers,
            n_dp,
            capacity,
        )[None, None]

    tokens = enc_state[0, 0].astype(jnp.float32)
    row_scale = norm_gain * lax.rsqrt(jnp.mean(tokens * tokens, axis=-1, keepdims=True) + 1e-06)
    inputs = (tokens * row_scale).astype(jnp.bfloat16)
    base_inputs = (baseline[0, 0].astype(jnp.float32) * row_scale).astype(jnp.bfloat16)
    flat_slot = expert_ids[0, 0] * capacity + slot_ids[0, 0]
    onehot = (
        flat_slot[None, :] == jnp.arange(n_experts * capacity, dtype=jnp.int32)[:, None]
    ).astype(jnp.bfloat16)

    def dispatch(values):
        placed = jnp.dot(onehot, values, preferred_element_type=jnp.float32).astype(jnp.bfloat16)
        return placed.reshape(n_experts, capacity, feature_width)

    layer_mult = attend(
        dec_queries[0, 0], enc_keys[0, 0], out_mult[0, 0], doc_lengths[0, 0], w_value
    )
    scaled_mult = (gate_prob[0, 0][:, None] * layer_mult).astype(jnp.bfloat16)
    sent = (dispatch(inputs), dispatch(base_inputs), dispatch(scaled_mult))
    returned = plain_pass(sent, w_in, w_out_t, n_peers, n_dp)
    per_token = lax.dot_general(
        onehot,
        returned.reshape(n_experts * capacity, feature_width),
        (((0,), (0,)), ((), ())),
        preferred_element_type=jnp.float32,
    )
    result = (layer_mult + row_scale * per_token).astype(jnp.bfloat16)
    return result[None, None]


def solution(mesh):
    in_specs = (
        P("dp", "expert", None, None),
        P("dp", "expert", None, None),
        P("dp", "expert", None, None),
        P("dp", "expert", None, None),
        P("dp", "expert", None, None),
        P("dp", "expert"),
        P("dp", "expert", None),
        P("dp", "expert", None),
        P("dp", "expert", None),
        P(),
        P("expert", None, "dp"),
        P("expert", None, "dp"),
        P(),
    )
    out_specs = P("dp", "expert", None, None)
    return jax.shard_map(body, mesh=mesh, in_specs=in_specs, out_specs=out_specs, check_vma=False)
```

```python
import functools
import math

import jax
import jax.numpy as jnp
from jax import lax
from jax.experimental import pallas as pl
from jax.experimental.pallas import tpu as pltpu
from jax.sharding import PartitionSpec as P

HEADS = 16
HEAD_DIM = 64


def rescale(pre_act, base_act):
    upper_part = jnp.maximum(jnp.maximum(pre_act, base_act), 0.0)
    lower_part = jnp.maximum(-jnp.minimum(pre_act, base_act), 0.0)
    return upper_part / (upper_part + lower_part + jnp.where(upper_part > 0.0, 0.0, 1.0))


def attend(query_rows, key_rows, mult_rows, length, w_value):
    enc_len = key_rows.shape[0]
    dec_len = query_rows.shape[0]
    queries = query_rows.reshape(dec_len, HEADS, HEAD_DIM)
    keys = key_rows.reshape(enc_len, HEADS, HEAD_DIM)
    mults = mult_rows.reshape(dec_len, HEADS, HEAD_DIM)
    scores = jnp.einsum("qhd,khd->hqk", queries, keys, preferred_element_type=jnp.float32) * (
        1.0 / math.sqrt(HEAD_DIM)
    )
    valid = jnp.arange(enc_len, dtype=jnp.int32) < length
    scores = jnp.where(valid[None, None, :], scores, -jnp.inf)
    top_score = jnp.max(scores, axis=-1, keepdims=True)
    expo = jnp.exp(scores - top_score)
    attn = (expo / jnp.sum(expo, axis=-1, keepdims=True)).astype(jnp.bfloat16)
    value_mult = jnp.einsum("hqk,qhd->khd", attn, mults, preferred_element_type=jnp.float32).astype(
        jnp.bfloat16
    )
    return lax.dot_general(
        value_mult.reshape(enc_len, HEADS * HEAD_DIM),
        w_value,
        (((1,), (1,)), ((), ())),
        preferred_element_type=jnp.float32,
    )


def expert_terms(rows_in, rows_base, rows_mult, part_in, part_out):
    pre_act = jnp.einsum("erd,edf->erf", rows_in, part_in, preferred_element_type=jnp.float32)
    base_act = jnp.einsum("erd,edf->erf", rows_base, part_in, preferred_element_type=jnp.float32)
    hidden_mult = jnp.einsum(
        "erd,edf->erf", rows_mult, part_out, preferred_element_type=jnp.float32
    )
    act_mult = (rescale(pre_act, base_act) * hidden_mult).astype(jnp.bfloat16)
    return jnp.einsum("erf,edf->erd", act_mult, part_in, preferred_element_type=jnp.float32)


def times_t(left, right):
    return lax.dot_general(left, right, (((1,), (1,)), ((), ())), preferred_element_type=jnp.float32)


def whole_kernel(
    n_peers,
    n_dp,
    cap,
    chunk,
    state_at,
    base_at,
    expert_at,
    place_at,
    gate_at,
    gain_at,
    length_at,
    keys_at,
    queries_at,
    mults_at,
    value_at,
    w_in,
    w_out,
    out,
    state,
    base_state,
    expert_row,
    place_row,
    gate,
    gain,
    length,
    keys,
    queries,
    mults,
    value,
    value_mult,
    layer,
    scale,
    sends,
    all_in,
    all_out,
    held,
    ratio,
    act,
    near_sum,
    far_sum,
    far_got,
    slot_sum,
    back,
    load_sem,
    weight_sem,
    swap_send,
    swap_recv,
    row_send,
    row_recv,
    hop_send,
    hop_recv,
    part_send,
    part_recv,
    back_send,
    back_recv,
):
    n_local = w_in.shape[0]
    tokens, width = state.shape
    rows = n_peers * cap
    half = n_peers // 2
    half_rows = half * cap
    n_chunks = width // chunk
    bf16, f32 = jnp.bfloat16, jnp.float32
    me = lax.axis_index("expert")
    dp = lax.axis_index("dp")
    pair = dp + 1 - 2 * lax.rem(dp, 2)
    across = lax.rem(dp + 2, n_dp)
    mesh_id = pl.DeviceIdType.MESH
    my_half = me // half
    inner = lax.rem(my_half + lax.rem(me // (half // 2), 2), 2)

    def peer_at(step):
        peer, bit = 0, 1
        while bit < n_peers:
            digit = lax.rem(me // bit, 2)
            flip = (step // bit) % 2
            peer = peer + bit * (digit + flip - 2 * digit * flip)
            bit *= 2
        return peer

    barrier = pltpu.get_barrier_semaphore()
    for step in range(1, n_peers):
        pl.semaphore_signal(barrier, inc=1, device_id={"expert": peer_at(step)}, device_id_type=mesh_id)
    for other in (pair, across):
        pl.semaphore_signal(barrier, inc=1, device_id={"dp": other}, device_id_type=mesh_id)

    def load(pairs, first_sem):
        copies = []
        for at, (ref, held_at) in enumerate(pairs):
            if at + first_sem == 0:
                quarter = tokens // 4
                for part in range(4):
                    some = pl.ds(part * quarter, quarter)
                    pltpu.make_async_copy(ref.at[some], held_at.at[some], load_sem.at[0]).start()
                copies.append(pltpu.make_async_copy(ref, held_at, load_sem.at[0]))
                continue
            copy = pltpu.make_async_copy(ref, held_at, load_sem.at[first_sem + at])
            copy.start()
            copies.append(copy)
        return copies

    small = load(
        (
            (state_at, state),
            (gain_at, gain),
            (expert_at, expert_row),
            (place_at, place_row),
            (base_at, base_state),
            (gate_at, gate),
            (length_at, length),
        ),
        0,
    )
    loads = load(((queries_at, queries), (keys_at, keys), (mults_at, mults), (value_at, value)), len(small))
    own_weights = []
    for at, (ref, held_at) in enumerate(((w_in, all_in), (w_out, all_out))):
        copy = pltpu.make_async_copy(ref, held_at.at[0], weight_sem.at[at])
        copy.start()
        own_weights.append(copy)
    for copy in small[:4]:
        copy.wait()

    expert = expert_row[...]
    owner = lax.div(expert, n_local)
    slot_row = lax.rem(expert, n_local) * rows + owner * cap + place_row[...]

    def column(row):
        return jnp.transpose(jnp.broadcast_to(row, (128, tokens)))[:, :1]

    def place_rows(a, l, values):
        at = lax.broadcasted_iota(jnp.int32, (rows, tokens), 0) + l * rows
        onehot = jnp.where(at == slot_row, 1.0, 0.0).astype(bf16)
        sends[a, l] = jnp.dot(onehot, values, preferred_element_type=f32).astype(bf16)

    def block_of(src):
        return pl.ds(pl.multiple_of(src * cap, cap), cap)

    def near_block(src):
        return block_of(lax.rem(src, half))

    def far_block(src):
        return pl.ds(pl.multiple_of(half_rows + lax.rem(src, half) * cap, cap), cap)

    same, cross = 0, 1

    def arrival_of(a, l, step):
        at = a + 3 * l
        if step >= half:
            return at * half + step - half
        apart = 3 * n_local * half
        return apart + at if at or step == 1 else apart + 3 * n_local + step - 2

    def row_copy(a, l, step):
        peer = peer_at(step)
        kind = step // half
        return pltpu.make_async_remote_copy(
            src_ref=sends.at[a, l, block_of(peer), :],
            dst_ref=held.at[a, l, kind, near_block(me), :],
            send_sem=row_send.at[0],
            recv_sem=row_recv.at[arrival_of(a, l, step)],
            device_id={"expert": peer},
            device_id_type=mesh_id,
        )

    def keep_own(a, l):
        held[a, l, same, near_block(me), :] = sends[a, l, block_of(me), :]

    def hop_copy(a, l, kind, step):
        src = peer_at(step)
        return pltpu.make_async_remote_copy(
            src_ref=held.at[a, l, kind, near_block(src), :],
            dst_ref=held.at[a, l, kind, far_block(src), :],
            send_sem=hop_send.at[0],
            recv_sem=hop_recv.at[a, l, kind],
            device_id={"dp": across},
            device_id_type=mesh_id,
        )

    def own_hop(a, l):
        return pltpu.make_async_remote_copy(
            src_ref=sends.at[a, l, block_of(me), :],
            dst_ref=held.at[a, l, same, far_block(me), :],
            send_sem=hop_send.at[0],
            recv_sem=hop_recv.at[a, l, same],
            device_id={"dp": across},
            device_id_type=mesh_id,
        )

    def await_bytes(ref, sem):
        pltpu.make_async_copy(ref, ref, sem).wait()

    cross_steps = [*range(n_peers - 2, half - 1, -2), *range(n_peers - 1, half, -2)]
    first, later = cross_steps[: half // 2], cross_steps[half // 2 :]

    def send_same(a, l):
        for step in range(1, half):
            row_copy(a, l, step).start()

    def send_cross(a, l):
        for step in cross_steps:
            row_copy(a, l, step).start()

    order = [(a, l) for l in range(n_local) for a in range(3)]

    def next_cross(at):
        for ahead, mine in ((1, 0), (2, 1)):
            if at + ahead < len(order):

                @pl.when(inner == mine)
                def _():
                    send_cross(*order[at + ahead])

    def relay_same(a, l, steps=range(1, half)):
        if 1 in steps:
            await_bytes(held.at[a, l, same, pl.ds(0, (half - 1) * cap), :], row_recv.at[arrival_of(a, l, 1)])
        for step in steps:
            hop_copy(a, l, same, step).start()

    def relay(a, l, steps):
        for step in steps:
            kind = step // half
            await_bytes(held.at[a, l, kind, pl.ds(0, cap), :], row_recv.at[arrival_of(a, l, step)])
            hop_copy(a, l, kind, step).start()

    def wait_unit(a, l, kind):
        await_bytes(held.at[a, l, kind, pl.ds(half_rows, half_rows), :], hop_recv.at[a, l, kind])

    token_rows = state[...].astype(f32)
    scale[...] = gain[...] * lax.rsqrt(
        jnp.mean(token_rows * token_rows, axis=-1, keepdims=True) + 1e-06
    )
    inputs = (token_rows * scale[...]).astype(bf16)
    place_rows(0, 0, inputs)
    with jax.named_scope("barr"):
        pl.semaphore_wait(barrier, n_peers + 1)
    own_hop(0, 0).start()
    send_same(0, 0)
    send_cross(0, 0)
    small[4].wait()
    base_inputs = (base_state[...].astype(f32) * scale[...]).astype(bf16)
    place_rows(1, 0, base_inputs)
    own_hop(1, 0).start()
    send_same(1, 0)
    place_rows(0, 1, inputs)
    own_hop(0, 1).start()
    place_rows(1, 1, base_inputs)
    own_hop(1, 1).start()
    for l in range(n_local):
        for a in range(2):
            keep_own(a, l)
    for copy in small[5:]:
        copy.wait()

    swaps = []
    for at, (ref, held_at) in enumerate(((w_in, all_in), (w_out, all_out))):
        swap = pltpu.make_async_remote_copy(
            src_ref=ref,
            dst_ref=held_at.at[1],
            send_sem=swap_send.at[at],
            recv_sem=swap_recv.at[at],
            device_id={"dp": pair},
            device_id_type=mesh_id,
        )
        swap.start()
        swaps.append(swap)

    for copy in loads:
        copy.wait()

    def two_heads(both):
        cols = pl.ds(pl.multiple_of(both * 2 * HEAD_DIM, 2 * HEAD_DIM), 2 * HEAD_DIM)
        query, key, mult = queries[:, cols], keys[:, cols], mults[:, cols]
        first_head = lax.broadcasted_iota(jnp.int32, query.shape, 1) < HEAD_DIM
        zero = jnp.zeros_like(query)
        found = []
        for head in range(2):
            mine = jnp.where(first_head, query, zero) if head == 0 else jnp.where(first_head, zero, query)
            scores = times_t(key, mine) * (1.0 / math.sqrt(HEAD_DIM))
            at = lax.broadcasted_iota(jnp.int32, scores.shape, 0)
            scores = jnp.where(at < length[...], scores, -jnp.inf)
            expo = jnp.exp(scores - jnp.max(scores, axis=0, keepdims=True))
            attn = (expo / jnp.sum(expo, axis=0, keepdims=True)).astype(bf16)
            found.append(jnp.dot(attn, mult, preferred_element_type=f32))
        left = lax.broadcasted_iota(jnp.int32, found[0].shape, 1) < HEAD_DIM
        value_mult[:, cols] = jnp.where(left, found[0], found[1]).astype(bf16)

    pieces = width // (2 * HEAD_DIM)
    with jax.named_scope("attn0"):
        pl.loop(0, pieces - 2)(two_heads)
    with jax.named_scope("r_s00"):
        relay(0, 0, range(1, half - 1))
    send_same(0, 1)

    @pl.when(inner == 1)
    def _():
        send_cross(1, 0)

    with jax.named_scope("attn1"):
        pl.loop(pieces - 2, pieces)(two_heads)

    def chunk_of(c):
        return pl.ds(pl.multiple_of(c * chunk, chunk), chunk)

    with jax.named_scope("layer"):

        @pl.loop(0, n_chunks)
        def _(c):
            layer[:, chunk_of(c)] = times_t(value_mult[...], value[chunk_of(c), :])

    with jax.named_scope("r_c00a"):
        relay(0, 0, first[:1])
    send_same(1, 1)
    scaled = (column(gate[...]) * layer[...]).astype(bf16)
    for l in range(n_local):
        place_rows(2, l, scaled)
        keep_own(2, l)
        own_hop(2, l).start()
        send_same(2, l)

    def ratio_of(l, kind):
        @pl.loop(0, 2)
        def _(shard):
            weight = all_in[shard, l]
            pre = times_t(held[0, l, kind], weight)
            base = times_t(held[1, l, kind], weight)
            ratio[l, kind, shard] = rescale(pre, base)

    last = n_local - 1

    def part_copy(l, kind, c):
        return pltpu.make_async_remote_copy(
            src_ref=far_sum.at[l, kind, :, chunk_of(c)],
            dst_ref=far_got.at[l, kind, :, chunk_of(c)],
            send_sem=part_send.at[0],
            recv_sem=part_recv.at[kind if l < last else 2 + kind * n_chunks + c],
            device_id={"dp": across},
            device_id_type=mesh_id,
        )

    def sums_of(l, kind, then=None, once=None):
        @pl.loop(0, 2)
        def _(shard):
            hidden = times_t(held[2, l, kind], all_out[shard, l])
            act[shard] = (ratio[l, kind, shard] * hidden).astype(bf16)

        def sum_chunk(c):
            cols = chunk_of(c)
            total = jnp.dot(act[0], all_in[0, l, :, cols], preferred_element_type=f32) + jnp.dot(
                act[1], all_in[1, l, :, cols], preferred_element_type=f32
            )
            near_sum[l, kind, :, cols] = total[:half_rows]
            far_sum[l, kind, :, cols] = total[half_rows:].astype(bf16)
            part_copy(l, kind, c).start()

        if once is not None:
            sum_chunk(0)
            once()
        if then is None:
            pl.loop(0 if once is None else 1, n_chunks)(sum_chunk)
        else:

            @pl.loop(1, n_chunks)
            def _(c):
                sum_chunk(c - 1)
                then(c)

            sum_chunk(n_chunks - 1)

    def steps_of(kind):
        return range(1, half) if kind == same else range(half, n_peers)

    def back_copy(l, kind, c, step):
        peer = peer_at(step)
        return pltpu.make_async_remote_copy(
            src_ref=slot_sum.at[l, kind, near_block(peer), chunk_of(c)],
            dst_ref=back.at[kind, l, near_block(me), chunk_of(c)],
            send_sem=back_send.at[0],
            recv_sem=back_recv.at[kind, c],
            device_id={"expert": peer},
            device_id_type=mesh_id,
        )

    def back_chunk(l, kind, c):
        if l == last:
            part_copy(l, kind, c).wait_recv()
        cols = chunk_of(c)
        slot_sum[l, kind, :, cols] = (
            near_sum[l, kind, :, cols] + far_got[l, kind, :, cols].astype(f32)
        ).astype(bf16)
        for step in steps_of(kind)[::-1]:
            back_copy(l, kind, c, step).start()
        if kind == same:
            mine = near_block(me)
            back[same, l, mine, cols] = (
                near_sum[l, same, mine, cols] + far_got[l, same, mine, cols].astype(f32)
            ).astype(bf16)

    def send_back(l, kind, begin=0, end=n_chunks):
        if l < last and begin == 0:
            await_bytes(far_got.at[l, kind], part_recv.at[kind])
        pl.loop(begin, end)(functools.partial(back_chunk, l, kind))

    def scoped(name, call, *args):
        with jax.named_scope(name):
            call(*args)

    scoped("r_s00b", relay, 0, 0, [half - 1])
    scoped("r_c00b", relay, 0, 0, first[1:])
    scoped("r_c00c", relay, 0, 0, later)
    next_cross(0)
    scoped("r_s10", relay_same, 1, 0)
    scoped("r_s01", relay_same, 0, 1)
    scoped("r_s11", relay_same, 1, 1)
    with jax.named_scope("weights"):
        for copy in own_weights:
            copy.wait()
        for swap in swaps:
            swap.wait_recv()
    scoped("w_s00", wait_unit, 0, 0, same)
    scoped("w_s10", wait_unit, 1, 0, same)
    scoped("ratio0s", ratio_of, 0, same)
    scoped("r_c10a", relay, 1, 0, first)
    scoped("r_c10b", relay, 1, 0, later)
    next_cross(1)
    scoped("r_s20", relay_same, 2, 0)
    scoped("r_c20a", relay, 2, 0, first)
    scoped("r_c20b", relay, 2, 0, later)
    next_cross(2)
    scoped("w_s20", wait_unit, 2, 0, same)
    scoped("sums0s", sums_of, 0, same)
    scoped("r_c01a", relay, 0, 1, first)
    scoped("w_c00", wait_unit, 0, 0, cross)
    scoped("w_c10", wait_unit, 1, 0, cross)
    scoped("ratio0c", ratio_of, 0, cross)
    scoped("r_c01b", relay, 0, 1, later)
    next_cross(3)
    scoped("w_c20", wait_unit, 2, 0, cross)
    scoped("sums0c", sums_of, 0, cross)
    scoped("w_s01", wait_unit, 0, 1, same)
    scoped("w_s11", wait_unit, 1, 1, same)
    scoped("ratio1s", ratio_of, 1, same)
    scoped("r_c11a", relay, 1, 1, first)
    scoped("r_c11b", relay, 1, 1, later)
    next_cross(4)
    scoped("back0s", send_back, 0, same)
    scoped("r_c21a", relay, 2, 1, first)

    @pl.when(inner == 1)
    def _():
        scoped("back0c", send_back, 0, cross, 0, 4)

    scoped("r_c21b", relay, 2, 1, later)
    scoped("r_s21", relay_same, 2, 1, range(1, half - 1))

    @pl.when(inner == 0)
    def _():
        scoped("back0c2", send_back, 0, cross)

    scoped("w_c01", wait_unit, 0, 1, cross)
    scoped("w_c11", wait_unit, 1, 1, cross)
    scoped("ratio1c", ratio_of, 1, cross)
    scoped("w_c21", wait_unit, 2, 1, cross)
    scoped("sums1c", sums_of, 1, cross, None, functools.partial(relay_same, 2, 1, [half - 1]))
    scoped("back1c", back_chunk, 1, cross, 0)
    scoped("w_s21", wait_unit, 2, 1, same)
    scoped("sums1s", sums_of, 1, same, functools.partial(back_chunk, 1, cross))
    scoped("back1s", send_back, 1, same)

    group = owner // half
    other = group + my_half - 2 * group * my_half
    in_half = lax.rem(expert, n_local) * half_rows + lax.rem(owner, half) * cap + place_row[...]
    got_row = other * (n_local * half_rows) + in_half
    got_col = column(got_row.astype(f32))

    at = lax.broadcasted_iota(jnp.int32, (tokens, n_local * rows), 1)
    pick = jnp.where(at.astype(f32) == got_col, 1.0, 0.0).astype(bf16)

    def wait_back(kind, c):
        remote = len(steps_of(kind)) * cap
        await_bytes(back.at[kind, :, pl.ds(0, remote), chunk_of(c)], back_recv.at[kind, c])

    for c in range(n_chunks):
        cols = chunk_of(c)
        for kind in (cross, same):
            with jax.named_scope(f"w_{kind}{c}"):
                wait_back(kind, c)
        got = back[:, :, :, cols].reshape(n_local * rows, chunk)
        with jax.named_scope(f"pick{c}"):
            out[:, cols] = (
                layer[:, cols] + scale[:, cols] * jnp.dot(pick, got, preferred_element_type=f32)
            ).astype(bf16)

    with jax.named_scope("drain"):
        for swap in swaps:
            swap.wait_send()
        remote = (n_peers - 1) * cap
        await_bytes(sends.at[:, :, pl.ds(0, remote), :], row_send.at[0])
        await_bytes(sends, hop_send.at[0])
        await_bytes(far_sum, part_send.at[0])
        await_bytes(sends.at[0, :, pl.ds(0, remote), :], back_send.at[0])


def whole_pass(
    state, base_state, keys, queries, mults, length, expert, place, gate, gain, w_in, w_out_t, value, n_peers, n_dp, cap
):
    tokens, width = state.shape
    n_local, _, part = w_in.shape
    w_in, w_out_t = jnp.swapaxes(w_in, 1, 2), jnp.swapaxes(w_out_t, 1, 2)
    rows = n_peers * cap
    half_rows = rows // 2
    chunk = width // 4
    n_chunks = width // chunk
    bf16, f32 = jnp.bfloat16, jnp.float32
    dma = pltpu.SemaphoreType.DMA
    vmem = pl.BlockSpec(memory_space=pltpu.VMEM)
    anyw = pl.BlockSpec(memory_space=pl.ANY)
    halves = (n_local, 2, half_rows, width)
    return pl.pallas_call(
        functools.partial(whole_kernel, n_peers, n_dp, cap, chunk),
        out_shape=pltpu.VMEM((tokens, width), bf16),
        in_specs=[anyw] * 13,
        out_specs=vmem,
        scratch_shapes=[
            pltpu.VMEM(state.shape, bf16),
            pltpu.VMEM(base_state.shape, bf16),
            pltpu.VMEM(expert.shape, expert.dtype),
            pltpu.VMEM(place.shape, place.dtype),
            pltpu.VMEM(gate.shape, f32),
            pltpu.VMEM((1, width), f32),
            pltpu.VMEM(length.shape, length.dtype),
            pltpu.VMEM(keys.shape, bf16),
            pltpu.VMEM(queries.shape, bf16),
            pltpu.VMEM(mults.shape, bf16),
            pltpu.VMEM(value.shape, bf16),
            pltpu.VMEM((tokens, width), bf16),
            pltpu.VMEM((tokens, width), f32),
            pltpu.VMEM((tokens, width), f32),
            pltpu.VMEM((3, n_local, rows, width), bf16),
            pltpu.VMEM((2, n_local, part, width), bf16),
            pltpu.VMEM((2, n_local, part, width), bf16),
            pltpu.VMEM((3, n_local, 2, 2 * half_rows, width), bf16),
            pltpu.VMEM((n_local, 2, 2, 2 * half_rows, part), f32),
            pltpu.VMEM((2, 2 * half_rows, part), bf16),
            pltpu.VMEM(halves, f32),
            pltpu.VMEM(halves, bf16),
            pltpu.VMEM(halves, bf16),
            pltpu.VMEM(halves, bf16),
            pltpu.VMEM((2, n_local, half_rows, width), bf16),
            dma((11,)),
            dma((2,)),
            dma((2,)),
            dma((2,)),
            dma((1,)),
            dma((3 * n_local * (n_peers // 2 + 1) + n_peers // 2 - 2,)),
            dma((1,)),
            dma((3, n_local, 2)),
            dma((1,)),
            dma((2 + 2 * n_chunks,)),
            dma((1,)),
            dma((2, n_chunks)),
        ],
        compiler_params=pltpu.CompilerParams(
            collective_id=0, has_side_effects=True, vmem_limit_bytes=60 * 1024 * 1024
        ),
        name="whole_pass",
    )(
        state,
        base_state,
        expert,
        place,
        gate,
        gain[None, :],
        length,
        keys,
        queries,
        mults,
        value,
        w_in,
        w_out_t,
    )


def plain_pass(sent, w_in, w_out_t, n_peers, n_dp):
    near = 2 if n_dp % 2 == 0 else 1
    shards = [(w_in, w_out_t)]
    if near == 2:
        swap = [(i, i ^ 1) for i in range(n_dp)]
        shards.append((lax.ppermute(w_in, "dp", swap), lax.ppermute(w_out_t, "dp", swap)))
    own_rows = tuple(
        lax.all_to_all(a, "expert", split_axis=0, concat_axis=1, tiled=True) for a in sent
    )

    def partial_sum(rows):
        total = expert_terms(*rows, *shards[0])
        for part in shards[1:]:
            total = total + expert_terms(*rows, *part)
        return total

    far = n_dp // near
    far_rows = []
    for hop in range(1, far):
        ahead = [(i, (i + hop * near) % n_dp) for i in range(n_dp)]
        far_rows.append(tuple(lax.ppermute(a, "dp", ahead) for a in own_rows))
    slot_mult = partial_sum(own_rows)
    for hop in range(1, far):
        back = [((i + hop * near) % n_dp, i) for i in range(n_dp)]
        far_part = partial_sum(far_rows[hop - 1]).astype(jnp.bfloat16)
        slot_mult = slot_mult + lax.ppermute(far_part, "dp", back).astype(jnp.float32)

    return lax.all_to_all(
        slot_mult.astype(jnp.bfloat16), "expert", split_axis=1, concat_axis=0, tiled=True
    )


def body(
    enc_state,
    baseline,
    enc_keys,
    dec_queries,
    out_mult,
    doc_lengths,
    expert_ids,
    slot_ids,
    gate_prob,
    norm_gain,
    w_in,
    w_out_t,
    w_value,
):
    enc_len = enc_state.shape[2]
    feature_width = enc_state.shape[3]
    local_experts = w_in.shape[0]
    n_experts = local_experts * lax.axis_size("expert")
    n_dp = lax.axis_size("dp")
    capacity = max(2, 2 * enc_len // n_experts)

    n_peers = lax.axis_size("expert")
    if n_dp == 4 and local_experts == 2 and capacity % 16 == 0 and n_peers >= 4 and n_peers & (n_peers - 1) == 0 and feature_width % 512 == 0:
        return whole_pass(
            enc_state[0, 0],
            baseline[0, 0],
            enc_keys[0, 0],
            dec_queries[0, 0],
            out_mult[0, 0],
            doc_lengths,
            expert_ids[0],
            slot_ids[0],
            gate_prob[0],
            norm_gain,
            w_in,
            w_out_t,
            w_value,
            n_peers,
            n_dp,
            capacity,
        )[None, None]

    tokens = enc_state[0, 0].astype(jnp.float32)
    row_scale = norm_gain * lax.rsqrt(jnp.mean(tokens * tokens, axis=-1, keepdims=True) + 1e-06)
    inputs = (tokens * row_scale).astype(jnp.bfloat16)
    base_inputs = (baseline[0, 0].astype(jnp.float32) * row_scale).astype(jnp.bfloat16)
    flat_slot = expert_ids[0, 0] * capacity + slot_ids[0, 0]
    onehot = (
        flat_slot[None, :] == jnp.arange(n_experts * capacity, dtype=jnp.int32)[:, None]
    ).astype(jnp.bfloat16)

    def dispatch(values):
        placed = jnp.dot(onehot, values, preferred_element_type=jnp.float32).astype(jnp.bfloat16)
        return placed.reshape(n_experts, capacity, feature_width)

    layer_mult = attend(
        dec_queries[0, 0], enc_keys[0, 0], out_mult[0, 0], doc_lengths[0, 0], w_value
    )
    scaled_mult = (gate_prob[0, 0][:, None] * layer_mult).astype(jnp.bfloat16)
    sent = (dispatch(inputs), dispatch(base_inputs), dispatch(scaled_mult))
    returned = plain_pass(sent, w_in, w_out_t, n_peers, n_dp)
    per_token = lax.dot_general(
        onehot,
        returned.reshape(n_experts * capacity, feature_width),
        (((0,), (0,)), ((), ())),
        preferred_element_type=jnp.float32,
    )
    result = (layer_mult + row_scale * per_token).astype(jnp.bfloat16)
    return result[None, None]


def solution(mesh):
    in_specs = (
        P("dp", "expert", None, None),
        P("dp", "expert", None, None),
        P("dp", "expert", None, None),
        P("dp", "expert", None, None),
        P("dp", "expert", None, None),
        P("dp", "expert"),
        P("dp", "expert", None),
        P("dp", "expert", None),
        P("dp", "expert", None),
        P(),
        P("expert", None, "dp"),
        P("expert", None, "dp"),
        P(),
    )
    out_specs = P("dp", "expert", None, None)
    return jax.shard_map(body, mesh=mesh, in_specs=in_specs, out_specs=out_specs, check_vma=False)
```

```python
import functools
import math

import jax
import jax.numpy as jnp
from jax import lax
from jax.experimental import pallas as pl
from jax.experimental.pallas import tpu as pltpu
from jax.sharding import PartitionSpec as P

HEADS = 16
HEAD_DIM = 64


def rescale(pre_act, base_act):
    upper_part = jnp.maximum(jnp.maximum(pre_act, base_act), 0.0)
    lower_part = jnp.maximum(-jnp.minimum(pre_act, base_act), 0.0)
    return upper_part / (upper_part + lower_part + jnp.where(upper_part > 0.0, 0.0, 1.0))


def attend(query_rows, key_rows, mult_rows, length, w_value):
    enc_len = key_rows.shape[0]
    dec_len = query_rows.shape[0]
    queries = query_rows.reshape(dec_len, HEADS, HEAD_DIM)
    keys = key_rows.reshape(enc_len, HEADS, HEAD_DIM)
    mults = mult_rows.reshape(dec_len, HEADS, HEAD_DIM)
    scores = jnp.einsum("qhd,khd->hqk", queries, keys, preferred_element_type=jnp.float32) * (
        1.0 / math.sqrt(HEAD_DIM)
    )
    valid = jnp.arange(enc_len, dtype=jnp.int32) < length
    scores = jnp.where(valid[None, None, :], scores, -jnp.inf)
    top_score = jnp.max(scores, axis=-1, keepdims=True)
    expo = jnp.exp(scores - top_score)
    attn = (expo / jnp.sum(expo, axis=-1, keepdims=True)).astype(jnp.bfloat16)
    value_mult = jnp.einsum("hqk,qhd->khd", attn, mults, preferred_element_type=jnp.float32).astype(
        jnp.bfloat16
    )
    return lax.dot_general(
        value_mult.reshape(enc_len, HEADS * HEAD_DIM),
        w_value,
        (((1,), (1,)), ((), ())),
        preferred_element_type=jnp.float32,
    )


def expert_terms(rows_in, rows_base, rows_mult, part_in, part_out):
    pre_act = jnp.einsum("erd,edf->erf", rows_in, part_in, preferred_element_type=jnp.float32)
    base_act = jnp.einsum("erd,edf->erf", rows_base, part_in, preferred_element_type=jnp.float32)
    hidden_mult = jnp.einsum(
        "erd,edf->erf", rows_mult, part_out, preferred_element_type=jnp.float32
    )
    act_mult = (rescale(pre_act, base_act) * hidden_mult).astype(jnp.bfloat16)
    return jnp.einsum("erf,edf->erd", act_mult, part_in, preferred_element_type=jnp.float32)


def times_t(left, right):
    return lax.dot_general(left, right, (((1,), (1,)), ((), ())), preferred_element_type=jnp.float32)


def whole_kernel(
    n_peers,
    n_dp,
    cap,
    chunk,
    state_at,
    base_at,
    expert_at,
    place_at,
    gate_at,
    gain_at,
    length_at,
    keys_at,
    queries_at,
    mults_at,
    value_at,
    w_in,
    w_out,
    out,
    state,
    base_state,
    expert_row,
    place_row,
    gate,
    gain,
    length,
    keys,
    queries,
    mults,
    value,
    value_mult,
    layer,
    scale,
    sends,
    all_in,
    all_out,
    held,
    ratio,
    act,
    near_sum,
    far_sum,
    far_got,
    slot_sum,
    back,
    load_sem,
    weight_sem,
    swap_send,
    swap_recv,
    row_send,
    row_recv,
    hop_send,
    hop_recv,
    part_send,
    part_recv,
    back_send,
    back_recv,
):
    n_local = w_in.shape[0]
    tokens, width = state.shape
    rows = n_peers * cap
    half = n_peers // 2
    half_rows = half * cap
    n_chunks = width // chunk
    bf16, f32 = jnp.bfloat16, jnp.float32
    me = lax.axis_index("expert")
    dp = lax.axis_index("dp")
    pair = dp + 1 - 2 * lax.rem(dp, 2)
    across = lax.rem(dp + 2, n_dp)
    mesh_id = pl.DeviceIdType.MESH
    my_half = me // half
    inner = lax.rem(my_half + lax.rem(me // (half // 2), 2), 2)

    def peer_at(step):
        peer, bit = 0, 1
        while bit < n_peers:
            digit = lax.rem(me // bit, 2)
            flip = (step // bit) % 2
            peer = peer + bit * (digit + flip - 2 * digit * flip)
            bit *= 2
        return peer

    barrier = pltpu.get_barrier_semaphore()
    for step in range(1, n_peers):
        pl.semaphore_signal(barrier, inc=1, device_id={"expert": peer_at(step)}, device_id_type=mesh_id)
    for other in (pair, across):
        pl.semaphore_signal(barrier, inc=1, device_id={"dp": other}, device_id_type=mesh_id)

    def load(pairs, first_sem):
        copies = []
        for at, (ref, held_at) in enumerate(pairs):
            if at + first_sem == 0:
                quarter = tokens // 4
                for part in range(4):
                    some = pl.ds(part * quarter, quarter)
                    pltpu.make_async_copy(ref.at[some], held_at.at[some], load_sem.at[0]).start()
                copies.append(pltpu.make_async_copy(ref, held_at, load_sem.at[0]))
                continue
            copy = pltpu.make_async_copy(ref, held_at, load_sem.at[first_sem + at])
            copy.start()
            copies.append(copy)
        return copies

    small = load(
        (
            (state_at, state),
            (gain_at, gain),
            (expert_at, expert_row),
            (place_at, place_row),
            (base_at, base_state),
            (gate_at, gate),
            (length_at, length),
        ),
        0,
    )
    loads = load(((queries_at, queries), (keys_at, keys), (mults_at, mults), (value_at, value)), len(small))
    own_weights = []
    for at, (ref, held_at) in enumerate(((w_in, all_in), (w_out, all_out))):
        copy = pltpu.make_async_copy(ref, held_at.at[0], weight_sem.at[at])
        copy.start()
        own_weights.append(copy)
    for copy in small[:4]:
        copy.wait()

    expert = expert_row[...]
    owner = lax.div(expert, n_local)
    slot_row = lax.rem(expert, n_local) * rows + owner * cap + place_row[...]

    def column(row):
        return jnp.transpose(jnp.broadcast_to(row, (128, tokens)))[:, :1]

    def place_rows(a, l, values):
        at = lax.broadcasted_iota(jnp.int32, (rows, tokens), 0) + l * rows
        onehot = jnp.where(at == slot_row, 1.0, 0.0).astype(bf16)
        sends[a, l] = jnp.dot(onehot, values, preferred_element_type=f32).astype(bf16)

    def block_of(src):
        return pl.ds(pl.multiple_of(src * cap, cap), cap)

    def near_block(src):
        return block_of(lax.rem(src, half))

    def far_block(src):
        return pl.ds(pl.multiple_of(half_rows + lax.rem(src, half) * cap, cap), cap)

    same, cross = 0, 1

    def arrival_of(a, l, step):
        at = a + 3 * l
        if step >= half:
            return at * 2 + (half - 2 + step % 2 if at else step - half)
        apart = 3 * n_local * 2 + half - 2
        return apart + at if at or step == 1 else apart + 3 * n_local + step - 2

    def row_copy(a, l, step):
        peer = peer_at(step)
        kind = step // half
        return pltpu.make_async_remote_copy(
            src_ref=sends.at[a, l, block_of(peer), :],
            dst_ref=held.at[a, l, kind, near_block(me), :],
            send_sem=row_send.at[0],
            recv_sem=row_recv.at[arrival_of(a, l, step)],
            device_id={"expert": peer},
            device_id_type=mesh_id,
        )

    def keep_own(a, l):
        held[a, l, same, near_block(me), :] = sends[a, l, block_of(me), :]

    def hop_copy(a, l, kind, step):
        src = peer_at(step)
        return pltpu.make_async_remote_copy(
            src_ref=held.at[a, l, kind, near_block(src), :],
            dst_ref=held.at[a, l, kind, far_block(src), :],
            send_sem=hop_send.at[0],
            recv_sem=hop_recv.at[a // 2, l, kind],
            device_id={"dp": across},
            device_id_type=mesh_id,
        )

    def own_hop(a, l):
        return pltpu.make_async_remote_copy(
            src_ref=sends.at[a, l, block_of(me), :],
            dst_ref=held.at[a, l, same, far_block(me), :],
            send_sem=hop_send.at[0],
            recv_sem=hop_recv.at[a // 2, l, same],
            device_id={"dp": across},
            device_id_type=mesh_id,
        )

    def await_bytes(ref, sem):
        pltpu.make_async_copy(ref, ref, sem).wait()

    cross_steps = [*range(n_peers - 2, half - 1, -2), *range(n_peers - 1, half, -2)]
    first, later = cross_steps[: half // 2], cross_steps[half // 2 :]

    def send_same(a, l):
        for step in range(1, half):
            row_copy(a, l, step).start()

    def send_cross(a, l):
        for step in cross_steps:
            row_copy(a, l, step).start()

    order = [(a, l) for l in range(n_local) for a in range(3)]

    def next_cross(at):
        for ahead, mine in ((1, 0), (2, 1)):
            if at + ahead < len(order):

                @pl.when(inner == mine)
                def _():
                    send_cross(*order[at + ahead])

    def relay_same(a, l, steps=range(1, half)):
        if 1 in steps:
            await_bytes(held.at[a, l, same, pl.ds(0, (half - 1) * cap), :], row_recv.at[arrival_of(a, l, 1)])
        for step in steps:
            hop_copy(a, l, same, step).start()

    def relay(a, l, steps):
        if a + 3 * l:
            size = len(steps) * cap
            await_bytes(held.at[a, l, cross, pl.ds(0, size), :], row_recv.at[arrival_of(a, l, steps[0])])
            for step in steps:
                hop_copy(a, l, cross, step).start()
            return
        for step in steps:
            kind = step // half
            await_bytes(held.at[a, l, kind, pl.ds(0, cap), :], row_recv.at[arrival_of(a, l, step)])
            hop_copy(a, l, kind, step).start()

    def wait_unit(a, l, kind):
        arrays = pl.ds(0, 2) if a < 2 else pl.ds(2, 1)
        await_bytes(held.at[arrays, l, kind, pl.ds(half_rows, half_rows), :], hop_recv.at[a // 2, l, kind])

    token_rows = state[...].astype(f32)
    scale[...] = gain[...] * lax.rsqrt(
        jnp.mean(token_rows * token_rows, axis=-1, keepdims=True) + 1e-06
    )
    inputs = (token_rows * scale[...]).astype(bf16)
    place_rows(0, 0, inputs)
    with jax.named_scope("barr"):
        pl.semaphore_wait(barrier, n_peers + 1)
    own_hop(0, 0).start()
    send_same(0, 0)
    send_cross(0, 0)
    small[4].wait()
    base_inputs = (base_state[...].astype(f32) * scale[...]).astype(bf16)
    place_rows(1, 0, base_inputs)
    own_hop(1, 0).start()
    send_same(1, 0)
    place_rows(0, 1, inputs)
    own_hop(0, 1).start()
    place_rows(1, 1, base_inputs)
    own_hop(1, 1).start()
    for l in range(n_local):
        for a in range(2):
            keep_own(a, l)
    for copy in small[5:]:
        copy.wait()

    swaps = []
    for at, (ref, held_at) in enumerate(((w_in, all_in), (w_out, all_out))):
        swap = pltpu.make_async_remote_copy(
            src_ref=ref,
            dst_ref=held_at.at[1],
            send_sem=swap_send.at[at],
            recv_sem=swap_recv.at[at],
            device_id={"dp": pair},
            device_id_type=mesh_id,
        )
        swap.start()
        swaps.append(swap)

    for copy in loads:
        copy.wait()

    def two_heads(both):
        cols = pl.ds(pl.multiple_of(both * 2 * HEAD_DIM, 2 * HEAD_DIM), 2 * HEAD_DIM)
        query, key, mult = queries[:, cols], keys[:, cols], mults[:, cols]
        first_head = lax.broadcasted_iota(jnp.int32, query.shape, 1) < HEAD_DIM
        zero = jnp.zeros_like(query)
        found = []
        for head in range(2):
            mine = jnp.where(first_head, query, zero) if head == 0 else jnp.where(first_head, zero, query)
            scores = times_t(key, mine) * (1.0 / math.sqrt(HEAD_DIM))
            at = lax.broadcasted_iota(jnp.int32, scores.shape, 0)
            scores = jnp.where(at < length[...], scores, -jnp.inf)
            expo = jnp.exp(scores - jnp.max(scores, axis=0, keepdims=True))
            attn = (expo / jnp.sum(expo, axis=0, keepdims=True)).astype(bf16)
            found.append(jnp.dot(attn, mult, preferred_element_type=f32))
        left = lax.broadcasted_iota(jnp.int32, found[0].shape, 1) < HEAD_DIM
        value_mult[:, cols] = jnp.where(left, found[0], found[1]).astype(bf16)

    pieces = width // (2 * HEAD_DIM)
    with jax.named_scope("attn0"):
        pl.loop(0, pieces - 2)(two_heads)
    with jax.named_scope("r_s00"):
        relay(0, 0, range(1, half - 1))
    send_same(0, 1)

    @pl.when(inner == 1)
    def _():
        send_cross(1, 0)

    with jax.named_scope("attn1"):
        pl.loop(pieces - 2, pieces)(two_heads)

    def chunk_of(c):
        return pl.ds(pl.multiple_of(c * chunk, chunk), chunk)

    with jax.named_scope("layer"):

        @pl.loop(0, n_chunks)
        def _(c):
            layer[:, chunk_of(c)] = times_t(value_mult[...], value[chunk_of(c), :])

    with jax.named_scope("r_c00a"):
        relay(0, 0, first[:1])
    send_same(1, 1)
    scaled = (column(gate[...]) * layer[...]).astype(bf16)
    for l in range(n_local):
        place_rows(2, l, scaled)
        keep_own(2, l)
        own_hop(2, l).start()
        send_same(2, l)

    def ratio_of(l, kind):
        @pl.loop(0, 2)
        def _(shard):
            weight = all_in[shard, l]
            pre = times_t(held[0, l, kind], weight)
            base = times_t(held[1, l, kind], weight)
            ratio[l, kind, shard] = rescale(pre, base)

    last = n_local - 1

    def part_copy(l, kind, c):
        return pltpu.make_async_remote_copy(
            src_ref=far_sum.at[l, kind, :, chunk_of(c)],
            dst_ref=far_got.at[l, kind, :, chunk_of(c)],
            send_sem=part_send.at[0],
            recv_sem=part_recv.at[kind if l < last else 2 + kind * n_chunks + c],
            device_id={"dp": across},
            device_id_type=mesh_id,
        )

    def sums_of(l, kind, then=None, once=None):
        @pl.loop(0, 2)
        def _(shard):
            hidden = times_t(held[2, l, kind], all_out[shard, l])
            act[shard] = (ratio[l, kind, shard] * hidden).astype(bf16)

        def sum_chunk(c):
            cols = chunk_of(c)
            total = jnp.dot(act[0], all_in[0, l, :, cols], preferred_element_type=f32) + jnp.dot(
                act[1], all_in[1, l, :, cols], preferred_element_type=f32
            )
            near_sum[l, kind, :, cols] = total[:half_rows]
            far_sum[l, kind, :, cols] = total[half_rows:].astype(bf16)
            part_copy(l, kind, c).start()

        if once is not None:
            sum_chunk(0)
            once()
        if then is None:
            pl.loop(0 if once is None else 1, n_chunks)(sum_chunk)
        else:

            @pl.loop(1, n_chunks)
            def _(c):
                sum_chunk(c - 1)
                then(c)

            sum_chunk(n_chunks - 1)

    def steps_of(kind):
        return range(1, half) if kind == same else range(half, n_peers)

    def back_copy(l, kind, c, step):
        peer = peer_at(step)
        return pltpu.make_async_remote_copy(
            src_ref=slot_sum.at[l, kind, near_block(peer), chunk_of(c)],
            dst_ref=back.at[kind, l, near_block(me), chunk_of(c)],
            send_sem=back_send.at[0],
            recv_sem=back_recv.at[kind, c],
            device_id={"expert": peer},
            device_id_type=mesh_id,
        )

    def back_chunk(l, kind, c):
        if l == last:
            part_copy(l, kind, c).wait_recv()
        cols = chunk_of(c)
        slot_sum[l, kind, :, cols] = (
            near_sum[l, kind, :, cols] + far_got[l, kind, :, cols].astype(f32)
        ).astype(bf16)
        for step in steps_of(kind)[::-1]:
            back_copy(l, kind, c, step).start()
        if kind == same:
            mine = near_block(me)
            back[same, l, mine, cols] = (
                near_sum[l, same, mine, cols] + far_got[l, same, mine, cols].astype(f32)
            ).astype(bf16)

    def send_back(l, kind, begin=0, end=n_chunks):
        if l < last and begin == 0:
            await_bytes(far_got.at[l, kind], part_recv.at[kind])
        pl.loop(begin, end)(functools.partial(back_chunk, l, kind))

    def scoped(name, call, *args):
        with jax.named_scope(name):
            call(*args)

    scoped("r_s00b", relay, 0, 0, [half - 1])
    scoped("r_c00b", relay, 0, 0, first[1:])
    scoped("r_c00c", relay, 0, 0, later)
    next_cross(0)
    scoped("r_s10", relay_same, 1, 0)
    scoped("r_s01", relay_same, 0, 1)
    scoped("r_s11", relay_same, 1, 1)
    with jax.named_scope("weights"):
        for copy in own_weights:
            copy.wait()
        for swap in swaps:
            swap.wait_recv()
    scoped("w_s10", wait_unit, 1, 0, same)
    scoped("ratio0s", ratio_of, 0, same)
    scoped("r_c10a", relay, 1, 0, first)
    scoped("r_c10b", relay, 1, 0, later)
    next_cross(1)
    scoped("r_s20", relay_same, 2, 0)
    scoped("r_c20a", relay, 2, 0, first)
    scoped("r_c20b", relay, 2, 0, later)
    next_cross(2)
    scoped("w_s20", wait_unit, 2, 0, same)
    scoped("sums0s", sums_of, 0, same)
    scoped("r_c01a", relay, 0, 1, first)
    scoped("w_c10", wait_unit, 1, 0, cross)
    scoped("ratio0c", ratio_of, 0, cross)
    scoped("r_c01b", relay, 0, 1, later)
    next_cross(3)
    scoped("w_c20", wait_unit, 2, 0, cross)
    scoped("sums0c", sums_of, 0, cross)
    scoped("w_s11", wait_unit, 1, 1, same)
    scoped("ratio1s", ratio_of, 1, same)
    scoped("r_c11a", relay, 1, 1, first)
    scoped("r_c11b", relay, 1, 1, later)
    next_cross(4)
    scoped("back0s", send_back, 0, same)
    scoped("r_c21a", relay, 2, 1, first)

    @pl.when(inner == 1)
    def _():
        scoped("back0c", send_back, 0, cross, 0, 4)

    scoped("r_c21b", relay, 2, 1, later)
    scoped("r_s21", relay_same, 2, 1, range(1, half - 1))

    @pl.when(inner == 0)
    def _():
        scoped("back0c2", send_back, 0, cross)

    scoped("w_c11", wait_unit, 1, 1, cross)
    scoped("ratio1c", ratio_of, 1, cross)
    scoped("w_c21", wait_unit, 2, 1, cross)
    scoped("sums1c", sums_of, 1, cross, None, functools.partial(relay_same, 2, 1, [half - 1]))
    scoped("back1c", back_chunk, 1, cross, 0)
    scoped("w_s21", wait_unit, 2, 1, same)
    scoped("sums1s", sums_of, 1, same, functools.partial(back_chunk, 1, cross))
    scoped("back1s", send_back, 1, same)

    group = owner // half
    other = group + my_half - 2 * group * my_half
    in_half = lax.rem(expert, n_local) * half_rows + lax.rem(owner, half) * cap + place_row[...]
    got_row = other * (n_local * half_rows) + in_half
    got_col = column(got_row.astype(f32))

    at = lax.broadcasted_iota(jnp.int32, (tokens, n_local * rows), 1)
    pick = jnp.where(at.astype(f32) == got_col, 1.0, 0.0).astype(bf16)

    def wait_back(kind, c):
        remote = len(steps_of(kind)) * cap
        await_bytes(back.at[kind, :, pl.ds(0, remote), chunk_of(c)], back_recv.at[kind, c])

    for c in range(n_chunks):
        cols = chunk_of(c)
        for kind in (cross, same):
            with jax.named_scope(f"w_{kind}{c}"):
                wait_back(kind, c)
        got = back[:, :, :, cols].reshape(n_local * rows, chunk)
        with jax.named_scope(f"pick{c}"):
            out[:, cols] = (
                layer[:, cols] + scale[:, cols] * jnp.dot(pick, got, preferred_element_type=f32)
            ).astype(bf16)

    with jax.named_scope("drain"):
        for swap in swaps:
            swap.wait_send()
        remote = (n_peers - 1) * cap
        await_bytes(sends.at[:, :, pl.ds(0, remote), :], row_send.at[0])
        await_bytes(sends, hop_send.at[0])
        await_bytes(far_sum, part_send.at[0])
        await_bytes(sends.at[0, :, pl.ds(0, remote), :], back_send.at[0])


def whole_pass(
    state, base_state, keys, queries, mults, length, expert, place, gate, gain, w_in, w_out_t, value, n_peers, n_dp, cap
):
    tokens, width = state.shape
    n_local, _, part = w_in.shape
    w_in, w_out_t = jnp.swapaxes(w_in, 1, 2), jnp.swapaxes(w_out_t, 1, 2)
    rows = n_peers * cap
    half_rows = rows // 2
    chunk = width // 4
    n_chunks = width // chunk
    bf16, f32 = jnp.bfloat16, jnp.float32
    dma = pltpu.SemaphoreType.DMA
    vmem = pl.BlockSpec(memory_space=pltpu.VMEM)
    anyw = pl.BlockSpec(memory_space=pl.ANY)
    halves = (n_local, 2, half_rows, width)
    return pl.pallas_call(
        functools.partial(whole_kernel, n_peers, n_dp, cap, chunk),
        out_shape=pltpu.VMEM((tokens, width), bf16),
        in_specs=[anyw] * 13,
        out_specs=vmem,
        scratch_shapes=[
            pltpu.VMEM(state.shape, bf16),
            pltpu.VMEM(base_state.shape, bf16),
            pltpu.VMEM(expert.shape, expert.dtype),
            pltpu.VMEM(place.shape, place.dtype),
            pltpu.VMEM(gate.shape, f32),
            pltpu.VMEM((1, width), f32),
            pltpu.VMEM(length.shape, length.dtype),
            pltpu.VMEM(keys.shape, bf16),
            pltpu.VMEM(queries.shape, bf16),
            pltpu.VMEM(mults.shape, bf16),
            pltpu.VMEM(value.shape, bf16),
            pltpu.VMEM((tokens, width), bf16),
            pltpu.VMEM((tokens, width), f32),
            pltpu.VMEM((tokens, width), f32),
            pltpu.VMEM((3, n_local, rows, width), bf16),
            pltpu.VMEM((2, n_local, part, width), bf16),
            pltpu.VMEM((2, n_local, part, width), bf16),
            pltpu.VMEM((3, n_local, 2, 2 * half_rows, width), bf16),
            pltpu.VMEM((n_local, 2, 2, 2 * half_rows, part), f32),
            pltpu.VMEM((2, 2 * half_rows, part), bf16),
            pltpu.VMEM(halves, f32),
            pltpu.VMEM(halves, bf16),
            pltpu.VMEM(halves, bf16),
            pltpu.VMEM(halves, bf16),
            pltpu.VMEM((2, n_local, half_rows, width), bf16),
            dma((11,)),
            dma((2,)),
            dma((2,)),
            dma((2,)),
            dma((1,)),
            dma((3 * n_local * 3 + 2 * (n_peers // 2 - 2),)),
            dma((1,)),
            dma((2, n_local, 2)),
            dma((1,)),
            dma((2 + 2 * n_chunks,)),
            dma((1,)),
            dma((2, n_chunks)),
        ],
        compiler_params=pltpu.CompilerParams(
            collective_id=0, has_side_effects=True, vmem_limit_bytes=60 * 1024 * 1024
        ),
        name="whole_pass",
    )(
        state,
        base_state,
        expert,
        place,
        gate,
        gain[None, :],
        length,
        keys,
        queries,
        mults,
        value,
        w_in,
        w_out_t,
    )


def plain_pass(sent, w_in, w_out_t, n_peers, n_dp):
    near = 2 if n_dp % 2 == 0 else 1
    shards = [(w_in, w_out_t)]
    if near == 2:
        swap = [(i, i ^ 1) for i in range(n_dp)]
        shards.append((lax.ppermute(w_in, "dp", swap), lax.ppermute(w_out_t, "dp", swap)))
    own_rows = tuple(
        lax.all_to_all(a, "expert", split_axis=0, concat_axis=1, tiled=True) for a in sent
    )

    def partial_sum(rows):
        total = expert_terms(*rows, *shards[0])
        for part in shards[1:]:
            total = total + expert_terms(*rows, *part)
        return total

    far = n_dp // near
    far_rows = []
    for hop in range(1, far):
        ahead = [(i, (i + hop * near) % n_dp) for i in range(n_dp)]
        far_rows.append(tuple(lax.ppermute(a, "dp", ahead) for a in own_rows))
    slot_mult = partial_sum(own_rows)
    for hop in range(1, far):
        back = [((i + hop * near) % n_dp, i) for i in range(n_dp)]
        far_part = partial_sum(far_rows[hop - 1]).astype(jnp.bfloat16)
        slot_mult = slot_mult + lax.ppermute(far_part, "dp", back).astype(jnp.float32)

    return lax.all_to_all(
        slot_mult.astype(jnp.bfloat16), "expert", split_axis=1, concat_axis=0, tiled=True
    )


def body(
    enc_state,
    baseline,
    enc_keys,
    dec_queries,
    out_mult,
    doc_lengths,
    expert_ids,
    slot_ids,
    gate_prob,
    norm_gain,
    w_in,
    w_out_t,
    w_value,
):
    enc_len = enc_state.shape[2]
    feature_width = enc_state.shape[3]
    local_experts = w_in.shape[0]
    n_experts = local_experts * lax.axis_size("expert")
    n_dp = lax.axis_size("dp")
    capacity = max(2, 2 * enc_len // n_experts)

    n_peers = lax.axis_size("expert")
    if n_dp == 4 and local_experts == 2 and capacity % 16 == 0 and n_peers >= 4 and n_peers & (n_peers - 1) == 0 and feature_width % 512 == 0:
        return whole_pass(
            enc_state[0, 0],
            baseline[0, 0],
            enc_keys[0, 0],
            dec_queries[0, 0],
            out_mult[0, 0],
            doc_lengths,
            expert_ids[0],
            slot_ids[0],
            gate_prob[0],
            norm_gain,
            w_in,
            w_out_t,
            w_value,
            n_peers,
            n_dp,
            capacity,
        )[None, None]

    tokens = enc_state[0, 0].astype(jnp.float32)
    row_scale = norm_gain * lax.rsqrt(jnp.mean(tokens * tokens, axis=-1, keepdims=True) + 1e-06)
    inputs = (tokens * row_scale).astype(jnp.bfloat16)
    base_inputs = (baseline[0, 0].astype(jnp.float32) * row_scale).astype(jnp.bfloat16)
    flat_slot = expert_ids[0, 0] * capacity + slot_ids[0, 0]
    onehot = (
        flat_slot[None, :] == jnp.arange(n_experts * capacity, dtype=jnp.int32)[:, None]
    ).astype(jnp.bfloat16)

    def dispatch(values):
        placed = jnp.dot(onehot, values, preferred_element_type=jnp.float32).astype(jnp.bfloat16)
        return placed.reshape(n_experts, capacity, feature_width)

    layer_mult = attend(
        dec_queries[0, 0], enc_keys[0, 0], out_mult[0, 0], doc_lengths[0, 0], w_value
    )
    scaled_mult = (gate_prob[0, 0][:, None] * layer_mult).astype(jnp.bfloat16)
    sent = (dispatch(inputs), dispatch(base_inputs), dispatch(scaled_mult))
    returned = plain_pass(sent, w_in, w_out_t, n_peers, n_dp)
    per_token = lax.dot_general(
        onehot,
        returned.reshape(n_experts * capacity, feature_width),
        (((0,), (0,)), ((), ())),
        preferred_element_type=jnp.float32,
    )
    result = (layer_mult + row_scale * per_token).astype(jnp.bfloat16)
    return result[None, None]


def solution(mesh):
    in_specs = (
        P("dp", "expert", None, None),
        P("dp", "expert", None, None),
        P("dp", "expert", None, None),
        P("dp", "expert", None, None),
        P("dp", "expert", None, None),
        P("dp", "expert"),
        P("dp", "expert", None),
        P("dp", "expert", None),
        P("dp", "expert", None),
        P(),
        P("expert", None, "dp"),
        P("expert", None, "dp"),
        P(),
    )
    out_specs = P("dp", "expert", None, None)
    return jax.shard_map(body, mesh=mesh, in_specs=in_specs, out_specs=out_specs, check_vma=False)
```

```python
import functools
import math

import jax
import jax.numpy as jnp
from jax import lax
from jax.experimental import pallas as pl
from jax.experimental.pallas import tpu as pltpu
from jax.sharding import PartitionSpec as P

HEADS = 16
HEAD_DIM = 64


def rescale(pre_act, base_act):
    upper_part = jnp.maximum(jnp.maximum(pre_act, base_act), 0.0)
    lower_part = jnp.maximum(-jnp.minimum(pre_act, base_act), 0.0)
    return upper_part / (upper_part + lower_part + jnp.where(upper_part > 0.0, 0.0, 1.0))


def attend(query_rows, key_rows, mult_rows, length, w_value):
    enc_len = key_rows.shape[0]
    dec_len = query_rows.shape[0]
    queries = query_rows.reshape(dec_len, HEADS, HEAD_DIM)
    keys = key_rows.reshape(enc_len, HEADS, HEAD_DIM)
    mults = mult_rows.reshape(dec_len, HEADS, HEAD_DIM)
    scores = jnp.einsum("qhd,khd->hqk", queries, keys, preferred_element_type=jnp.float32) * (
        1.0 / math.sqrt(HEAD_DIM)
    )
    valid = jnp.arange(enc_len, dtype=jnp.int32) < length
    scores = jnp.where(valid[None, None, :], scores, -jnp.inf)
    top_score = jnp.max(scores, axis=-1, keepdims=True)
    expo = jnp.exp(scores - top_score)
    attn = (expo / jnp.sum(expo, axis=-1, keepdims=True)).astype(jnp.bfloat16)
    value_mult = jnp.einsum("hqk,qhd->khd", attn, mults, preferred_element_type=jnp.float32).astype(
        jnp.bfloat16
    )
    return lax.dot_general(
        value_mult.reshape(enc_len, HEADS * HEAD_DIM),
        w_value,
        (((1,), (1,)), ((), ())),
        preferred_element_type=jnp.float32,
    )


def expert_terms(rows_in, rows_base, rows_mult, part_in, part_out):
    pre_act = jnp.einsum("erd,edf->erf", rows_in, part_in, preferred_element_type=jnp.float32)
    base_act = jnp.einsum("erd,edf->erf", rows_base, part_in, preferred_element_type=jnp.float32)
    hidden_mult = jnp.einsum(
        "erd,edf->erf", rows_mult, part_out, preferred_element_type=jnp.float32
    )
    act_mult = (rescale(pre_act, base_act) * hidden_mult).astype(jnp.bfloat16)
    return jnp.einsum("erf,edf->erd", act_mult, part_in, preferred_element_type=jnp.float32)


def times_t(left, right):
    return lax.dot_general(left, right, (((1,), (1,)), ((), ())), preferred_element_type=jnp.float32)


def whole_kernel(
    n_peers,
    n_dp,
    cap,
    chunk,
    state_at,
    base_at,
    expert_at,
    place_at,
    gate_at,
    gain_at,
    length_at,
    keys_at,
    queries_at,
    mults_at,
    value_at,
    w_in,
    w_out,
    out,
    state,
    base_state,
    expert_row,
    place_row,
    gate,
    gain,
    length,
    keys,
    queries,
    mults,
    value,
    value_mult,
    layer,
    scale,
    sends,
    all_in,
    all_out,
    held,
    ratio,
    act,
    near_sum,
    far_sum,
    far_got,
    slot_sum,
    back,
    load_sem,
    weight_sem,
    swap_send,
    swap_recv,
    row_send,
    row_recv,
    hop_send,
    hop_recv,
    part_send,
    part_recv,
    back_send,
    back_recv,
):
    n_local = w_in.shape[0]
    tokens, width = state.shape
    rows = n_peers * cap
    half = n_peers // 2
    half_rows = half * cap
    n_chunks = width // chunk
    bf16, f32 = jnp.bfloat16, jnp.float32
    me = lax.axis_index("expert")
    dp = lax.axis_index("dp")
    pair = dp + 1 - 2 * lax.rem(dp, 2)
    across = lax.rem(dp + 2, n_dp)
    mesh_id = pl.DeviceIdType.MESH
    my_half = me // half
    inner = lax.rem(my_half + lax.rem(me // (half // 2), 2), 2)

    def peer_at(step):
        peer, bit = 0, 1
        while bit < n_peers:
            digit = lax.rem(me // bit, 2)
            flip = (step // bit) % 2
            peer = peer + bit * (digit + flip - 2 * digit * flip)
            bit *= 2
        return peer

    barrier = pltpu.get_barrier_semaphore()
    for step in range(1, n_peers):
        pl.semaphore_signal(barrier, inc=1, device_id={"expert": peer_at(step)}, device_id_type=mesh_id)
    for other in (pair, across):
        pl.semaphore_signal(barrier, inc=1, device_id={"dp": other}, device_id_type=mesh_id)

    def load(pairs, first_sem):
        copies = []
        for at, (ref, held_at) in enumerate(pairs):
            if at + first_sem == 0:
                quarter = tokens // 4
                for part in range(4):
                    some = pl.ds(part * quarter, quarter)
                    pltpu.make_async_copy(ref.at[some], held_at.at[some], load_sem.at[0]).start()
                copies.append(pltpu.make_async_copy(ref, held_at, load_sem.at[0]))
                continue
            copy = pltpu.make_async_copy(ref, held_at, load_sem.at[first_sem + at])
            copy.start()
            copies.append(copy)
        return copies

    small = load(
        (
            (state_at, state),
            (gain_at, gain),
            (expert_at, expert_row),
            (place_at, place_row),
            (base_at, base_state),
            (gate_at, gate),
            (length_at, length),
        ),
        0,
    )
    loads = load(((queries_at, queries), (keys_at, keys), (mults_at, mults), (value_at, value)), len(small))
    own_weights = []
    for at, (ref, held_at) in enumerate(((w_in, all_in), (w_out, all_out))):
        copy = pltpu.make_async_copy(ref, held_at.at[0], weight_sem.at[at])
        copy.start()
        own_weights.append(copy)
    for copy in small[:4]:
        copy.wait()

    expert = expert_row[...]
    owner = lax.div(expert, n_local)
    slot_row = lax.rem(expert, n_local) * rows + owner * cap + place_row[...]

    def column(row):
        return jnp.transpose(jnp.broadcast_to(row, (128, tokens)))[:, :1]

    def place_rows(a, l, values):
        at = lax.broadcasted_iota(jnp.int32, (rows, tokens), 0) + l * rows
        onehot = jnp.where(at == slot_row, 1.0, 0.0).astype(bf16)
        sends[a, l] = jnp.dot(onehot, values, preferred_element_type=f32).astype(bf16)

    def block_of(src):
        return pl.ds(pl.multiple_of(src * cap, cap), cap)

    def near_block(src):
        return block_of(lax.rem(src, half))

    def far_block(src):
        return pl.ds(pl.multiple_of(half_rows + lax.rem(src, half) * cap, cap), cap)

    same, cross = 0, 1

    def arrival_of(a, l, step):
        at = a + 3 * l
        if step >= half:
            return at * 2 + (half - 2 + step % 2 if at else step - half)
        apart = 3 * n_local * 2 + half - 2
        return apart + at if at or step == 1 else apart + 3 * n_local + step - 2

    def row_copy(a, l, step):
        peer = peer_at(step)
        kind = step // half
        return pltpu.make_async_remote_copy(
            src_ref=sends.at[a, l, block_of(peer), :],
            dst_ref=held.at[a, l, kind, near_block(me), :],
            send_sem=row_send.at[0],
            recv_sem=row_recv.at[arrival_of(a, l, step)],
            device_id={"expert": peer},
            device_id_type=mesh_id,
        )

    def keep_own(a, l):
        held[a, l, same, near_block(me), :] = sends[a, l, block_of(me), :]

    def hop_copy(a, l, kind, step):
        src = peer_at(step)
        return pltpu.make_async_remote_copy(
            src_ref=held.at[a, l, kind, near_block(src), :],
            dst_ref=held.at[a, l, kind, far_block(src), :],
            send_sem=hop_send.at[0],
            recv_sem=hop_recv.at[a // 2, l, kind],
            device_id={"dp": across},
            device_id_type=mesh_id,
        )

    def own_hop(a, l):
        return pltpu.make_async_remote_copy(
            src_ref=sends.at[a, l, block_of(me), :],
            dst_ref=held.at[a, l, same, far_block(me), :],
            send_sem=hop_send.at[0],
            recv_sem=hop_recv.at[a // 2, l, same],
            device_id={"dp": across},
            device_id_type=mesh_id,
        )

    def await_bytes(ref, sem):
        pltpu.make_async_copy(ref, ref, sem).wait()

    cross_steps = [*range(n_peers - 2, half - 1, -2), *range(n_peers - 1, half, -2)]
    first, later = cross_steps[: half // 2], cross_steps[half // 2 :]

    def send_same(a, l):
        for step in range(1, half):
            row_copy(a, l, step).start()

    def send_cross(a, l):
        for step in cross_steps:
            row_copy(a, l, step).start()

    order = [(a, l) for l in range(n_local) for a in range(3)]

    def next_cross(at):
        for ahead, mine in ((1, 0), (2, 1)):
            if at + ahead < len(order):

                @pl.when(inner == mine)
                def _():
                    send_cross(*order[at + ahead])

    def relay_same(a, l, steps=range(1, half)):
        if 1 in steps:
            await_bytes(held.at[a, l, same, pl.ds(0, (half - 1) * cap), :], row_recv.at[arrival_of(a, l, 1)])
        for step in steps:
            hop_copy(a, l, same, step).start()

    def relay(a, l, steps):
        if a + 3 * l:
            size = len(steps) * cap
            await_bytes(held.at[a, l, cross, pl.ds(0, size), :], row_recv.at[arrival_of(a, l, steps[0])])
            for step in steps:
                hop_copy(a, l, cross, step).start()
            return
        for step in steps:
            kind = step // half
            await_bytes(held.at[a, l, kind, pl.ds(0, cap), :], row_recv.at[arrival_of(a, l, step)])
            hop_copy(a, l, kind, step).start()

    def wait_unit(a, l, kind):
        arrays = pl.ds(0, 2) if a < 2 else pl.ds(2, 1)
        await_bytes(held.at[arrays, l, kind, pl.ds(half_rows, half_rows), :], hop_recv.at[a // 2, l, kind])

    token_rows = state[...].astype(f32)
    scale[...] = gain[...] * lax.rsqrt(
        jnp.mean(token_rows * token_rows, axis=-1, keepdims=True) + 1e-06
    )
    inputs = (token_rows * scale[...]).astype(bf16)
    place_rows(0, 0, inputs)
    with jax.named_scope("barr"):
        pl.semaphore_wait(barrier, n_peers + 1)
    own_hop(0, 0).start()
    send_same(0, 0)
    send_cross(0, 0)
    small[4].wait()
    base_inputs = (base_state[...].astype(f32) * scale[...]).astype(bf16)
    place_rows(1, 0, base_inputs)
    own_hop(1, 0).start()
    send_same(1, 0)
    place_rows(0, 1, inputs)
    own_hop(0, 1).start()
    place_rows(1, 1, base_inputs)
    own_hop(1, 1).start()
    for l in range(n_local):
        for a in range(2):
            keep_own(a, l)
    for copy in small[5:]:
        copy.wait()

    swaps = []
    for at, (ref, held_at) in enumerate(((w_in, all_in), (w_out, all_out))):
        swap = pltpu.make_async_remote_copy(
            src_ref=ref,
            dst_ref=held_at.at[1],
            send_sem=swap_send.at[at],
            recv_sem=swap_recv.at[at],
            device_id={"dp": pair},
            device_id_type=mesh_id,
        )
        swap.start()
        swaps.append(swap)

    for copy in loads:
        copy.wait()

    def two_heads(both):
        cols = pl.ds(pl.multiple_of(both * 2 * HEAD_DIM, 2 * HEAD_DIM), 2 * HEAD_DIM)
        query, key, mult = queries[:, cols], keys[:, cols], mults[:, cols]
        first_head = lax.broadcasted_iota(jnp.int32, query.shape, 1) < HEAD_DIM
        zero = jnp.zeros_like(query)
        found = []
        for head in range(2):
            mine = jnp.where(first_head, query, zero) if head == 0 else jnp.where(first_head, zero, query)
            scores = times_t(key, mine) * (1.0 / math.sqrt(HEAD_DIM))
            at = lax.broadcasted_iota(jnp.int32, scores.shape, 0)
            scores = jnp.where(at < length[...], scores, -jnp.inf)
            expo = jnp.exp(scores - jnp.max(scores, axis=0, keepdims=True))
            attn = (expo / jnp.sum(expo, axis=0, keepdims=True)).astype(bf16)
            found.append(jnp.dot(attn, mult, preferred_element_type=f32))
        left = lax.broadcasted_iota(jnp.int32, found[0].shape, 1) < HEAD_DIM
        value_mult[:, cols] = jnp.where(left, found[0], found[1]).astype(bf16)

    pieces = width // (2 * HEAD_DIM)
    with jax.named_scope("attn0"):
        pl.loop(0, pieces - 3)(two_heads)
    with jax.named_scope("r_s00"):
        relay(0, 0, range(1, half - 1))
    send_same(0, 1)

    @pl.when(inner == 1)
    def _():
        send_cross(1, 0)

    with jax.named_scope("attn1"):
        pl.loop(pieces - 3, pieces)(two_heads)

    def chunk_of(c):
        return pl.ds(pl.multiple_of(c * chunk, chunk), chunk)

    with jax.named_scope("layer"):

        @pl.loop(0, n_chunks)
        def _(c):
            layer[:, chunk_of(c)] = times_t(value_mult[...], value[chunk_of(c), :])

    with jax.named_scope("r_c00a"):
        relay(0, 0, first[:1])
    send_same(1, 1)
    scaled = (column(gate[...]) * layer[...]).astype(bf16)
    for l in range(n_local):
        place_rows(2, l, scaled)
        keep_own(2, l)
        own_hop(2, l).start()
        send_same(2, l)

    def ratio_of(l, kind):
        @pl.loop(0, 2)
        def _(shard):
            weight = all_in[shard, l]
            pre = times_t(held[0, l, kind], weight)
            base = times_t(held[1, l, kind], weight)
            ratio[l, kind, shard] = rescale(pre, base)

    last = n_local - 1

    def part_copy(l, kind, c):
        return pltpu.make_async_remote_copy(
            src_ref=far_sum.at[l, kind, :, chunk_of(c)],
            dst_ref=far_got.at[l, kind, :, chunk_of(c)],
            send_sem=part_send.at[0],
            recv_sem=part_recv.at[kind if l < last else 2 + kind * n_chunks + c],
            device_id={"dp": across},
            device_id_type=mesh_id,
        )

    def sums_of(l, kind, then=None, once=None):
        @pl.loop(0, 2)
        def _(shard):
            hidden = times_t(held[2, l, kind], all_out[shard, l])
            act[shard] = (ratio[l, kind, shard] * hidden).astype(bf16)

        def sum_chunk(c):
            cols = chunk_of(c)
            total = jnp.dot(act[0], all_in[0, l, :, cols], preferred_element_type=f32) + jnp.dot(
                act[1], all_in[1, l, :, cols], preferred_element_type=f32
            )
            near_sum[l, kind, :, cols] = total[:half_rows]
            far_sum[l, kind, :, cols] = total[half_rows:].astype(bf16)
            part_copy(l, kind, c).start()

        if once is not None:
            sum_chunk(0)
            once()
        if then is None:
            pl.loop(0 if once is None else 1, n_chunks)(sum_chunk)
        else:

            @pl.loop(1, n_chunks)
            def _(c):
                sum_chunk(c - 1)
                then(c)

            sum_chunk(n_chunks - 1)

    def steps_of(kind):
        return range(1, half) if kind == same else range(half, n_peers)

    def back_copy(l, kind, c, step):
        peer = peer_at(step)
        return pltpu.make_async_remote_copy(
            src_ref=slot_sum.at[l, kind, near_block(peer), chunk_of(c)],
            dst_ref=back.at[kind, l, near_block(me), chunk_of(c)],
            send_sem=back_send.at[0],
            recv_sem=back_recv.at[kind, c],
            device_id={"expert": peer},
            device_id_type=mesh_id,
        )

    def back_chunk(l, kind, c):
        if l == last:
            part_copy(l, kind, c).wait_recv()
        cols = chunk_of(c)
        slot_sum[l, kind, :, cols] = (
            near_sum[l, kind, :, cols] + far_got[l, kind, :, cols].astype(f32)
        ).astype(bf16)
        for step in steps_of(kind)[::-1]:
            back_copy(l, kind, c, step).start()
        if kind == same:
            mine = near_block(me)
            back[same, l, mine, cols] = (
                near_sum[l, same, mine, cols] + far_got[l, same, mine, cols].astype(f32)
            ).astype(bf16)

    def send_back(l, kind, begin=0, end=n_chunks):
        if l < last and begin == 0:
            await_bytes(far_got.at[l, kind], part_recv.at[kind])
        pl.loop(begin, end)(functools.partial(back_chunk, l, kind))

    def scoped(name, call, *args):
        with jax.named_scope(name):
            call(*args)

    scoped("r_s00b", relay, 0, 0, [half - 1])
    scoped("r_c00b", relay, 0, 0, first[1:])
    scoped("r_c00c", relay, 0, 0, later)
    next_cross(0)
    scoped("r_s10", relay_same, 1, 0)
    scoped("r_s01", relay_same, 0, 1)
    scoped("r_s11", relay_same, 1, 1)
    with jax.named_scope("weights"):
        for copy in own_weights:
            copy.wait()
        for swap in swaps:
            swap.wait_recv()
    scoped("w_s10", wait_unit, 1, 0, same)
    scoped("ratio0s", ratio_of, 0, same)
    scoped("r_c10a", relay, 1, 0, first)
    scoped("r_c10b", relay, 1, 0, later)
    next_cross(1)
    scoped("r_s20", relay_same, 2, 0)
    scoped("r_c20a", relay, 2, 0, first)
    scoped("r_c20b", relay, 2, 0, later)
    next_cross(2)
    scoped("w_s20", wait_unit, 2, 0, same)
    scoped("sums0s", sums_of, 0, same)
    scoped("r_c01a", relay, 0, 1, first)
    scoped("w_c10", wait_unit, 1, 0, cross)
    scoped("ratio0c", ratio_of, 0, cross)
    scoped("r_c01b", relay, 0, 1, later)
    next_cross(3)
    scoped("w_c20", wait_unit, 2, 0, cross)
    scoped("sums0c", sums_of, 0, cross)
    scoped("w_s11", wait_unit, 1, 1, same)
    scoped("ratio1s", ratio_of, 1, same)
    scoped("r_c11a", relay, 1, 1, first)
    scoped("r_c11b", relay, 1, 1, later)
    next_cross(4)
    scoped("back0s", send_back, 0, same)
    scoped("r_c21a", relay, 2, 1, first)

    @pl.when(inner == 1)
    def _():
        scoped("back0c", send_back, 0, cross, 0, 4)

    scoped("r_c21b", relay, 2, 1, later)
    scoped("r_s21", relay_same, 2, 1, range(1, half - 1))

    @pl.when(inner == 0)
    def _():
        scoped("back0c2", send_back, 0, cross)

    scoped("w_c11", wait_unit, 1, 1, cross)
    scoped("ratio1c", ratio_of, 1, cross)
    scoped("w_c21", wait_unit, 2, 1, cross)
    scoped("sums1c", sums_of, 1, cross, None, functools.partial(relay_same, 2, 1, [half - 1]))
    scoped("back1c", back_chunk, 1, cross, 0)
    scoped("w_s21", wait_unit, 2, 1, same)
    scoped("sums1s", sums_of, 1, same, functools.partial(back_chunk, 1, cross))
    scoped("back1s", send_back, 1, same)

    group = owner // half
    other = group + my_half - 2 * group * my_half
    in_half = lax.rem(expert, n_local) * half_rows + lax.rem(owner, half) * cap + place_row[...]
    got_row = other * (n_local * half_rows) + in_half
    got_col = column(got_row.astype(f32))

    at = lax.broadcasted_iota(jnp.int32, (tokens, n_local * rows), 1)
    pick = jnp.where(at.astype(f32) == got_col, 1.0, 0.0).astype(bf16)

    def wait_back(kind, c):
        remote = len(steps_of(kind)) * cap
        await_bytes(back.at[kind, :, pl.ds(0, remote), chunk_of(c)], back_recv.at[kind, c])

    for c in range(n_chunks):
        cols = chunk_of(c)
        for kind in (cross, same):
            with jax.named_scope(f"w_{kind}{c}"):
                wait_back(kind, c)
        got = back[:, :, :, cols].reshape(n_local * rows, chunk)
        with jax.named_scope(f"pick{c}"):
            out[:, cols] = (
                layer[:, cols] + scale[:, cols] * jnp.dot(pick, got, preferred_element_type=f32)
            ).astype(bf16)

    with jax.named_scope("drain"):
        for swap in swaps:
            swap.wait_send()
        remote = (n_peers - 1) * cap
        await_bytes(sends.at[:, :, pl.ds(0, remote), :], row_send.at[0])
        await_bytes(sends, hop_send.at[0])
        await_bytes(far_sum, part_send.at[0])
        await_bytes(sends.at[0, :, pl.ds(0, remote), :], back_send.at[0])


def whole_pass(
    state, base_state, keys, queries, mults, length, expert, place, gate, gain, w_in, w_out_t, value, n_peers, n_dp, cap
):
    tokens, width = state.shape
    n_local, _, part = w_in.shape
    w_in, w_out_t = jnp.swapaxes(w_in, 1, 2), jnp.swapaxes(w_out_t, 1, 2)
    rows = n_peers * cap
    half_rows = rows // 2
    chunk = width // 4
    n_chunks = width // chunk
    bf16, f32 = jnp.bfloat16, jnp.float32
    dma = pltpu.SemaphoreType.DMA
    vmem = pl.BlockSpec(memory_space=pltpu.VMEM)
    anyw = pl.BlockSpec(memory_space=pl.ANY)
    halves = (n_local, 2, half_rows, width)
    return pl.pallas_call(
        functools.partial(whole_kernel, n_peers, n_dp, cap, chunk),
        out_shape=pltpu.VMEM((tokens, width), bf16),
        in_specs=[anyw] * 13,
        out_specs=vmem,
        scratch_shapes=[
            pltpu.VMEM(state.shape, bf16),
            pltpu.VMEM(base_state.shape, bf16),
            pltpu.VMEM(expert.shape, expert.dtype),
            pltpu.VMEM(place.shape, place.dtype),
            pltpu.VMEM(gate.shape, f32),
            pltpu.VMEM((1, width), f32),
            pltpu.VMEM(length.shape, length.dtype),
            pltpu.VMEM(keys.shape, bf16),
            pltpu.VMEM(queries.shape, bf16),
            pltpu.VMEM(mults.shape, bf16),
            pltpu.VMEM(value.shape, bf16),
            pltpu.VMEM((tokens, width), bf16),
            pltpu.VMEM((tokens, width), f32),
            pltpu.VMEM((tokens, width), f32),
            pltpu.VMEM((3, n_local, rows, width), bf16),
            pltpu.VMEM((2, n_local, part, width), bf16),
            pltpu.VMEM((2, n_local, part, width), bf16),
            pltpu.VMEM((3, n_local, 2, 2 * half_rows, width), bf16),
            pltpu.VMEM((n_local, 2, 2, 2 * half_rows, part), f32),
            pltpu.VMEM((2, 2 * half_rows, part), bf16),
            pltpu.VMEM(halves, f32),
            pltpu.VMEM(halves, bf16),
            pltpu.VMEM(halves, bf16),
            pltpu.VMEM(halves, bf16),
            pltpu.VMEM((2, n_local, half_rows, width), bf16),
            dma((11,)),
            dma((2,)),
            dma((2,)),
            dma((2,)),
            dma((1,)),
            dma((3 * n_local * 3 + 2 * (n_peers // 2 - 2),)),
            dma((1,)),
            dma((2, n_local, 2)),
            dma((1,)),
            dma((2 + 2 * n_chunks,)),
            dma((1,)),
            dma((2, n_chunks)),
        ],
        compiler_params=pltpu.CompilerParams(
            collective_id=0, has_side_effects=True, vmem_limit_bytes=60 * 1024 * 1024
        ),
        name="whole_pass",
    )(
        state,
        base_state,
        expert,
        place,
        gate,
        gain[None, :],
        length,
        keys,
        queries,
        mults,
        value,
        w_in,
        w_out_t,
    )


def plain_pass(sent, w_in, w_out_t, n_peers, n_dp):
    near = 2 if n_dp % 2 == 0 else 1
    shards = [(w_in, w_out_t)]
    if near == 2:
        swap = [(i, i ^ 1) for i in range(n_dp)]
        shards.append((lax.ppermute(w_in, "dp", swap), lax.ppermute(w_out_t, "dp", swap)))
    own_rows = tuple(
        lax.all_to_all(a, "expert", split_axis=0, concat_axis=1, tiled=True) for a in sent
    )

    def partial_sum(rows):
        total = expert_terms(*rows, *shards[0])
        for part in shards[1:]:
            total = total + expert_terms(*rows, *part)
        return total

    far = n_dp // near
    far_rows = []
    for hop in range(1, far):
        ahead = [(i, (i + hop * near) % n_dp) for i in range(n_dp)]
        far_rows.append(tuple(lax.ppermute(a, "dp", ahead) for a in own_rows))
    slot_mult = partial_sum(own_rows)
    for hop in range(1, far):
        back = [((i + hop * near) % n_dp, i) for i in range(n_dp)]
        far_part = partial_sum(far_rows[hop - 1]).astype(jnp.bfloat16)
        slot_mult = slot_mult + lax.ppermute(far_part, "dp", back).astype(jnp.float32)

    return lax.all_to_all(
        slot_mult.astype(jnp.bfloat16), "expert", split_axis=1, concat_axis=0, tiled=True
    )


def body(
    enc_state,
    baseline,
    enc_keys,
    dec_queries,
    out_mult,
    doc_lengths,
    expert_ids,
    slot_ids,
    gate_prob,
    norm_gain,
    w_in,
    w_out_t,
    w_value,
):
    enc_len = enc_state.shape[2]
    feature_width = enc_state.shape[3]
    local_experts = w_in.shape[0]
    n_experts = local_experts * lax.axis_size("expert")
    n_dp = lax.axis_size("dp")
    capacity = max(2, 2 * enc_len // n_experts)

    n_peers = lax.axis_size("expert")
    if n_dp == 4 and local_experts == 2 and capacity % 16 == 0 and n_peers >= 4 and n_peers & (n_peers - 1) == 0 and feature_width % 512 == 0:
        return whole_pass(
            enc_state[0, 0],
            baseline[0, 0],
            enc_keys[0, 0],
            dec_queries[0, 0],
            out_mult[0, 0],
            doc_lengths,
            expert_ids[0],
            slot_ids[0],
            gate_prob[0],
            norm_gain,
            w_in,
            w_out_t,
            w_value,
            n_peers,
            n_dp,
            capacity,
        )[None, None]

    tokens = enc_state[0, 0].astype(jnp.float32)
    row_scale = norm_gain * lax.rsqrt(jnp.mean(tokens * tokens, axis=-1, keepdims=True) + 1e-06)
    inputs = (tokens * row_scale).astype(jnp.bfloat16)
    base_inputs = (baseline[0, 0].astype(jnp.float32) * row_scale).astype(jnp.bfloat16)
    flat_slot = expert_ids[0, 0] * capacity + slot_ids[0, 0]
    onehot = (
        flat_slot[None, :] == jnp.arange(n_experts * capacity, dtype=jnp.int32)[:, None]
    ).astype(jnp.bfloat16)

    def dispatch(values):
        placed = jnp.dot(onehot, values, preferred_element_type=jnp.float32).astype(jnp.bfloat16)
        return placed.reshape(n_experts, capacity, feature_width)

    layer_mult = attend(
        dec_queries[0, 0], enc_keys[0, 0], out_mult[0, 0], doc_lengths[0, 0], w_value
    )
    scaled_mult = (gate_prob[0, 0][:, None] * layer_mult).astype(jnp.bfloat16)
    sent = (dispatch(inputs), dispatch(base_inputs), dispatch(scaled_mult))
    returned = plain_pass(sent, w_in, w_out_t, n_peers, n_dp)
    per_token = lax.dot_general(
        onehot,
        returned.reshape(n_experts * capacity, feature_width),
        (((0,), (0,)), ((), ())),
        preferred_element_type=jnp.float32,
    )
    result = (layer_mult + row_scale * per_token).astype(jnp.bfloat16)
    return result[None, None]


def solution(mesh):
    in_specs = (
        P("dp", "expert", None, None),
        P("dp", "expert", None, None),
        P("dp", "expert", None, None),
        P("dp", "expert", None, None),
        P("dp", "expert", None, None),
        P("dp", "expert"),
        P("dp", "expert", None),
        P("dp", "expert", None),
        P("dp", "expert", None),
        P(),
        P("expert", None, "dp"),
        P("expert", None, "dp"),
        P(),
    )
    out_specs = P("dp", "expert", None, None)
    return jax.shard_map(body, mesh=mesh, in_specs=in_specs, out_specs=out_specs, check_vma=False)
```
